32 devices in a mesh: dp: 8 (over y, x, core), head: 4 (over z).
Axes of the slice: x: 2, y: 2, z: 4, core: 2. Of those that a mesh axis runs over, the one named last changes fastest.
Arguments:
- series: float32 [512, 512], P(('dp', 'head')), may hold values from -15 to 15
- observed: int32 [512, 512], P(('dp', 'head')), may hold values from 0 to 1, as said below
- item_split: int32 [512], P('dp'), may hold values 0 or 1
- recon_cot: float32 [512, 512], P(('dp', 'head')), may hold values from -6 to 6
- gain_attn: bfloat16 [512], replicated, may hold values from 0.099609375 to 1.8984375
- gain_ff: bfloat16 [512], replicated, may hold values from 0.099609375 to 1.8984375
- gain_final: bfloat16 [512], replicated, may hold values from 0.099609375 to 1.8984375
- patch_weight: bfloat16 [8, 512], replicated, may hold values from -2 to 2
- patch_bias: bfloat16 [512], replicated, may hold values from -4 to 4
- query_weight: bfloat16 [512, 512], P(None, 'head'), may hold values from -0.125 to 0.125
- key_weight: bfloat16 [512, 512], P(None, 'head'), may hold values from -0.125 to 0.125
- value_weight: bfloat16 [512, 512], P(None, 'head'), may hold values from -0.25 to 0.25
- out_weight: bfloat16 [512, 512], P('head'), may hold values from -0.75 to 0.75
- bias_table: bfloat16 [32, 8], P(None, 'head'), may hold values from -4 to 4
- gate_weight: bfloat16 [512, 1024], P(None, 'head'), may hold values from -1 to 1
- up_weight: bfloat16 [512, 1024], P(None, 'head'), may hold values from -1 to 1
- down_weight: bfloat16 [1024, 512], P('head'), may hold values from -2 to 2
- head_weight: bfloat16 [512, 8], replicated, may hold values from -1 to 1
- head_bias: bfloat16 [8], replicated, may hold values from -4 to 4
Outputs:
- rebuilt: float32 [512, 512], P(('dp', 'head'))
- series_grad: float32 [512, 512], P(('dp', 'head'))
- gain_attn_grad: float32 [512], replicated
- gain_ff_grad: float32 [512], replicated
- gain_final_grad: float32 [512], replicated
- patch_weight_grad: float32 [8, 512], replicated
- patch_bias_grad: float32 [512], replicated
- query_grad: float32 [512, 512], P(None, 'head')
- key_grad: float32 [512, 512], P(None, 'head')
- value_grad: float32 [512, 512], P(None, 'head')
- out_grad: float32 [512, 512], P('head')
- table_grad: float32 [32, 8], P(None, 'head')
- gate_grad: float32 [512, 1024], P(None, 'head')
- up_grad: float32 [512, 1024], P(None, 'head')
- down_grad: float32 [1024, 512], P('head')
- head_weight_grad: float32 [512, 8], replicated
- head_bias_grad: float32 [8], replicated
The draws below stay inside these ranges and needn't reach their ends.
Inputs may be any that keep to these rules, and one draw needn't show every extreme that they name: 1 marks an observed value; the first step of every block of 32 steps that starts at a multiple of 32 is observed. `item_split`: 1 marks a row that packs two items of half of 64 patches, 0 a row of one item.
All inputs are finite; a program needn't handle non-finite values. No bound on the sum of `item_split` on one device may be relied on, other than what follows from the above.
Results may differ from the reference program's by a relative error of at most 0.025.
Values may be sent and summed in bfloat16 or wider, within the bound.
A program may use at most 128 MiB of HBM per device.

```python
import math
import jax
import jax.numpy as jnp
import numpy as np
from jax import lax

D = 512
HEADS = 8
HEAD_DIM = 64
FF = 1024
BUCKETS = 32
MAX_DIST = 128
PATCH = 8
ROW_PATCHES = 64
ROWS_DEV = 16
ROWS = 512
SERIES_LEN = 512
N_HEAD = 4


def draw_series(key, part):
    noise_key, scale_key, shift_key = jax.random.split(key, 3)
    noise_draw = jnp.clip(jax.random.normal(noise_key, (ROWS, 2, SERIES_LEN // 2), jnp.float32), -4.0, 4.0)
    item_scale = jnp.exp(jax.random.uniform(scale_key, (ROWS, 2, 1), jnp.float32, math.log(0.3), math.log(3.0)))
    level_shift = jax.random.uniform(shift_key, (ROWS, 2, 1), jnp.float32, -1.0, 1.0) * item_scale
    return (noise_draw * item_scale + level_shift).reshape(ROWS, SERIES_LEN)


def draw_observed(key, part):
    random_picks = jax.random.randint(key, (ROWS, SERIES_LEN), 0, 8)
    step_index = jnp.arange(SERIES_LEN, dtype=jnp.int32)[None, :]
    return jnp.where((random_picks != 0) | (step_index % 32 == 0), 1, 0).astype(jnp.int32)


def clipped_normal(key, shape):
    return jnp.clip(jax.random.normal(key, shape, jnp.float32), -4.0, 4.0)


def head_matrix(key):
    return clipped_normal(jax.random.fold_in(key, 11), (D, PATCH)) / math.sqrt(D)


def draw_head_weight(key, part):
    return head_matrix(key).astype(jnp.bfloat16)


def draw_gate_weight(key, part):
    gate_key = jax.random.fold_in(key, 21)
    mixed_draw = clipped_normal(gate_key, (D, FF))
    return jnp.clip(mixed_draw / math.sqrt(D), -1.0, 1.0).astype(jnp.bfloat16)


def draw_up_weight(key, part):
    up_key = jax.random.fold_in(key, 31)
    mixed_draw = clipped_normal(up_key, (D, FF))
    return jnp.clip(mixed_draw / math.sqrt(D), -1.0, 1.0).astype(jnp.bfloat16)


def draw_down_weight(key, part):
    down_key = jax.random.fold_in(key, 41)
    mixed_draw = clipped_normal(down_key, (FF, D)) / math.sqrt(FF // 4)
    return jnp.clip(mixed_draw, -2.0, 2.0).astype(jnp.bfloat16)


def place_ends(result, rng, least, top_value):
    shape = result.shape
    spot = [jax.random.randint(jax.random.fold_in(rng, axis), (), 0, shape[axis]) for axis in range(len(shape))]
    result = result.at[tuple(spot)].set(least)
    longest = shape.index(max(shape))
    spot[longest] = (spot[longest] + 1) % shape[longest]
    return result.at[tuple(spot)].set(top_value)


def levels(rng, shape, cuts, low, high):
    gain, own = 1.0, jax.random.fold_in(rng, 6)
    for dim, parts in cuts:
        steps = jnp.exp(jax.random.uniform(jax.random.fold_in(own, dim), (parts,), jnp.float32, low / len(cuts), high / len(cuts)))
        gain = gain * jnp.repeat(steps, shape[dim] // parts).reshape([-1 if axis == dim else 1 for axis in range(len(shape))])
    return gain


def bell_draw(rng, extent, width, reach, cuts=(), kind=jnp.bfloat16):
    result = width * jax.random.normal(rng, extent, jnp.float32)
    if cuts:
        result = result * levels(rng, extent, cuts, -0.22, 0.18)
    return jnp.clip(result, -reach, reach).astype(kind)


def setup_inputs(seed: int = 0) -> dict:
    seeds = jax.random.split(jax.random.key(seed), 20)
    return {
        "series": draw_series(jax.random.fold_in(seeds[19], 71), 0),
        "observed": draw_observed(jax.random.fold_in(seeds[19], 71), 0),
        "item_split": place_ends((jax.random.randint(seeds[2], (ROWS,), 0, 3) < 1).astype(jnp.int32), jax.random.fold_in(seeds[2], 1), 0, 1),
        "recon_cot": bell_draw(seeds[3], (ROWS, SERIES_LEN), 1.0, 6.0, ((0, 32),), jnp.float32),
        "gain_attn": jnp.clip(1.0 + 0.18 * jax.random.normal(seeds[4], (D,), jnp.float32), 0.099609375, 1.8984375).astype(jnp.bfloat16),
        "gain_ff": jnp.clip(1.0 + 0.18 * jax.random.normal(seeds[5], (D,), jnp.float32), 0.099609375, 1.8984375).astype(jnp.bfloat16),
        "gain_final": jnp.clip(1.0 + 0.18 * jax.random.normal(seeds[6], (D,), jnp.float32), 0.099609375, 1.8984375).astype(jnp.bfloat16),
        "patch_weight": bell_draw(seeds[7], (PATCH, D), PATCH ** -0.5, 2.0),
        "patch_bias": bell_draw(seeds[8], (D,), 0.3, 4.0),
        "query_weight": bell_draw(seeds[9], (D, D), (4 * D) ** -0.5, 0.125, ((1, 4),)),
        "key_weight": bell_draw(seeds[10], (D, D), (4 * D) ** -0.5, 0.125, ((1, 4),)),
        "value_weight": bell_draw(seeds[11], (D, D), D ** -0.5, 0.25, ((1, 4),)),
        "out_weight": bell_draw(seeds[12], (D, D), (D // 8) ** -0.5, 0.75, ((0, 4),)),
        "bias_table": bell_draw(seeds[13], (BUCKETS, HEADS), 1.0, 4.0, ((1, 4),)),
        "gate_weight": draw_gate_weight(jax.random.fold_in(seeds[19], 71), 0),
        "up_weight": draw_up_weight(jax.random.fold_in(seeds[19], 71), 0),
        "down_weight": draw_down_weight(jax.random.fold_in(seeds[19], 71), 0),
        "head_weight": draw_head_weight(jax.random.fold_in(seeds[19], 71), 0),
        "head_bias": bell_draw(seeds[18], (PATCH,), 0.3, 4.0),
    }


@jax.custom_vjp
def low(v):
    return lax.optimization_barrier(v.astype(jnp.bfloat16)).astype(jnp.float32)

@jax.custom_vjp
def low_back(v):
    return v

def low_keep(v):
    return (low(v), None)

def low_pass(kept, grad):
    return (grad,)

def back_keep(v):
    return (v, None)

def back_low(kept, grad):
    return (low(grad),)
low.defvjp(low_keep, low_pass)
low_back.defvjp(back_keep, back_low)

def bucket_onehot(length, buckets, far_reach):
    half_count = buckets // 2
    exact_count = half_count // 2
    onehot_table = np.zeros((length, length, buckets), np.float32)
    for row_pos in range(length):
        for col_pos in range(length):
            offset = col_pos - row_pos
            distance = abs(offset)
            bucket_id = half_count if offset > 0 else 0
            if distance < exact_count:
                bucket_id += distance
            else:
                bucket_id += min(half_count - 1, exact_count + int(math.log(distance / exact_count) / math.log(far_reach / exact_count) * (half_count - exact_count)))
            onehot_table[row_pos, col_pos, bucket_id] = 1.0
    return onehot_table

def full_dot(left, right):
    return jnp.dot(left, right, precision=lax.Precision.HIGHEST)

def rms_scale(values, gain_vec):
    return values * lax.rsqrt(lax.optimization_barrier(jnp.mean(values * values, axis=-1, keepdims=True)) + 1e-06) * gain_vec

def item_combine(sums, split_col):
    return split_col * sums + (1.0 - split_col) * lax.optimization_barrier(jnp.sum(sums, axis=-1, keepdims=True))

def layer_forward(series, observed, item_split, params, onehot):
    gain_attn, gain_ff, gain_final, patch_weight, patch_bias, query_weight, key_weight, value_weight, out_weight, bias_table, gate_weight, up_weight, down_weight, head_weight, head_bias = params
    rows_here = series.shape[0]
    length = series.shape[1]
    half_len = length // 2
    halves = series.reshape(rows_here, 2, half_len)
    obs_mask = observed.astype(jnp.float32).reshape(rows_here, 2, half_len)
    split_col = item_split.astype(jnp.float32)[:, None]
    counts = item_combine(lax.optimization_barrier(jnp.sum(obs_mask, axis=-1)), split_col)
    item_mean = item_combine(lax.optimization_barrier(jnp.sum(obs_mask * halves, axis=-1)), split_col) / counts
    centred = halves - item_mean[..., None]
    item_var = item_combine(lax.optimization_barrier(jnp.sum(obs_mask * centred * centred, axis=-1)), split_col) / counts
    item_std = jnp.sqrt(item_var + 1e-05)
    normed = obs_mask * centred / item_std[..., None]
    patches = low(normed.reshape(-1, PATCH))
    embedded = low_back(full_dot(patches, patch_weight) + patch_bias)
    attn_in = low(rms_scale(embedded, gain_attn))
    query_rows = low_back(low(full_dot(attn_in, query_weight)))
    key_rows = low_back(low(full_dot(attn_in, key_weight)))
    value_rows = low_back(low(full_dot(attn_in, value_weight)))
    tokens = embedded.shape[0]
    head_shape = (rows_here, ROW_PATCHES, HEADS, HEAD_DIM)
    offsets = jnp.einsum('ijb,bh->hij', onehot, bias_table, precision=lax.Precision.HIGHEST)
    scores = low_back(jnp.einsum('rihd,rjhd->rhij', query_rows.reshape(head_shape), key_rows.reshape(head_shape), precision=lax.Precision.HIGHEST) + offsets[None])
    positions = (jnp.arange(ROW_PATCHES, dtype=jnp.int32) // (ROW_PATCHES // 2)).astype(jnp.int32)
    item_ids = item_split.astype(jnp.int32)[:, None] * positions[None, :]
    same_item = (item_ids[:, :, None] == item_ids[:, None, :])[:, None]
    masked = jnp.where(same_item, scores, -1e+30)
    row_top = lax.optimization_barrier(jnp.max(masked, axis=-1, keepdims=True))
    raised = jnp.where(same_item, jnp.exp(masked - row_top), 0.0)
    prob_low = low(raised / lax.optimization_barrier(jnp.sum(raised, axis=-1, keepdims=True)))
    context = jnp.einsum('rhij,rjhd->rihd', prob_low, value_rows.reshape(head_shape), precision=lax.Precision.HIGHEST)
    context = low_back(low(context.reshape(tokens, HEADS * HEAD_DIM)))
    attn_out = low_back(full_dot(context, out_weight))
    hidden_mid = embedded + attn_out
    ff_in = low(rms_scale(hidden_mid, gain_ff))
    gate_proj = low_back(full_dot(ff_in, gate_weight))
    up_proj = low_back(full_dot(ff_in, up_weight))
    inner_act = low(jax.nn.gelu(gate_proj, approximate=True) * up_proj)
    ff_out = low_back(full_dot(inner_act, down_weight))
    hidden_end = hidden_mid + ff_out
    final_in = low(rms_scale(hidden_end, gain_final))
    output = low_back(full_dot(final_in, head_weight) + head_bias)
    rebuilt = output.reshape(rows_here, 2, half_len) * item_std[..., None] + item_mean[..., None]
    return rebuilt.reshape(rows_here, length)

def reference(series, observed, item_split, recon_cot, gain_attn, gain_ff, gain_final, patch_weight, patch_bias, query_weight, key_weight, value_weight, out_weight, bias_table, gate_weight, up_weight, down_weight, head_weight, head_bias):
    params = tuple((weight_arr.astype(jnp.float32) for weight_arr in (gain_attn, gain_ff, gain_final, patch_weight, patch_bias, query_weight, key_weight, value_weight, out_weight, bias_table, gate_weight, up_weight, down_weight, head_weight, head_bias)))
    group_rows = ROWS_DEV * N_HEAD
    group_count = series.shape[0] // group_rows
    onehot = jnp.asarray(bucket_onehot(ROW_PATCHES, BUCKETS, MAX_DIST), dtype=jnp.float32)

    def one_group(running, pieces):
        piece_series, piece_observed, piece_split, piece_cot = pieces

        def forward(series_in, weights_in):
            return layer_forward(series_in, piece_observed, piece_split, weights_in, onehot)
        rebuilt_rows, pullback = jax.vjp(forward, piece_series, params)
        grad_series, weight_grads = pullback(piece_cot)
        running = jax.tree.map(jnp.add, running, weight_grads)
        return (running, (rebuilt_rows, grad_series))
    zero_grads = tuple((jnp.zeros(weight_arr.shape, jnp.float32) for weight_arr in params))
    stacked = (series.reshape(group_count, group_rows, -1), observed.reshape(group_count, group_rows, -1), item_split.reshape(group_count, group_rows), recon_cot.reshape(group_count, group_rows, -1))
    totals, (rebuilt, series_grad) = lax.scan(one_group, zero_grads, stacked)
    gain_attn_grad, gain_ff_grad, gain_final_grad, patch_weight_grad, patch_bias_grad, query_grad, key_grad, value_grad, out_grad, table_grad, gate_grad, up_grad, down_grad, head_weight_grad, head_bias_grad = totals
    return (rebuilt.reshape(series.shape), series_grad.reshape(series.shape), gain_attn_grad, gain_ff_grad, gain_final_grad, patch_weight_grad, patch_bias_grad, query_grad, key_grad, value_grad, out_grad, table_grad, gate_grad, up_grad, down_grad, head_weight_grad, head_bias_grad)
```

```python
import math

import jax
import jax.numpy as jnp
import numpy as np
from jax import lax
from jax.sharding import PartitionSpec as P

HEAD_DIM = 64
BUCKETS = 32
MAX_DIST = 128


def bucket_onehot(length, buckets, far_reach):
    half_count = buckets // 2
    exact_count = half_count // 2
    onehot_table = np.zeros((length, length, buckets), np.float32)
    for row_pos in range(length):
        for col_pos in range(length):
            offset = col_pos - row_pos
            distance = abs(offset)
            bucket_id = half_count if offset > 0 else 0
            if distance < exact_count:
                bucket_id += distance
            else:
                bucket_id += min(
                    half_count - 1,
                    exact_count
                    + int(
                        math.log(distance / exact_count)
                        / math.log(far_reach / exact_count)
                        * (half_count - exact_count)
                    ),
                )
            onehot_table[row_pos, col_pos, bucket_id] = 1.0
    return onehot_table


def norm_scale(values):
    return lax.rsqrt(jnp.mean(values * values, axis=-1, keepdims=True) + 1e-06)


def norm_back(grad_out, unit_rows, row_scale, gain_vec):
    d_unit = grad_out * gain_vec
    gain_grad = jnp.sum(grad_out * unit_rows, axis=0)
    spread = jnp.mean(d_unit * unit_rows, axis=-1, keepdims=True)
    return (row_scale * (d_unit - unit_rows * spread), gain_grad)


def gelu_tanh(values):
    return jax.nn.gelu(values, approximate=True)


def item_combine(sums, split_col):
    return split_col * sums + (1.0 - split_col) * jnp.sum(sums, axis=-1, keepdims=True)


def same_items(split_rows, length):
    positions = jnp.arange(length, dtype=jnp.int32) // (length // 2)
    item_ids = split_rows[:, None] * positions[None, :]
    return (item_ids[:, :, None] == item_ids[:, None, :])[:, None]


def score_rows(query_rows, key_rows, offsets):
    return (
        jnp.einsum("rihd,rjhd->rhij", query_rows, key_rows, preferred_element_type=jnp.float32)
        + offsets[None]
    )


def attend_forward(rows_in, qkv_weight, table_here, onehot, same_item):
    tokens = rows_in.shape[0]
    length = onehot.shape[0]
    columns = qkv_weight.shape[1] // 3
    head_shape = (tokens // length, length, columns // HEAD_DIM, HEAD_DIM)
    projected = jnp.dot(rows_in, qkv_weight, preferred_element_type=jnp.float32).astype(
        jnp.bfloat16
    )
    query_rows = projected[:, :columns].reshape(head_shape)
    key_rows = projected[:, columns : 2 * columns].reshape(head_shape)
    value_rows = projected[:, 2 * columns :].reshape(head_shape)
    offsets = jnp.einsum(
        "ijb,bh->hij", onehot, table_here.astype(jnp.float32), precision=lax.Precision.HIGHEST
    )
    scores = score_rows(query_rows, key_rows, offsets)
    masked = jnp.where(same_item, scores, -1e30)
    row_top = jnp.max(masked, axis=-1, keepdims=True)
    raised = jnp.where(same_item, jnp.exp(masked - row_top), 0.0)
    totals = jnp.sum(raised, axis=-1, keepdims=True)
    prob_low = (raised / totals).astype(jnp.bfloat16)
    context = jnp.einsum(
        "rhij,rjhd->rihd", prob_low, value_rows, preferred_element_type=jnp.float32
    )
    context = context.reshape(tokens, columns).astype(jnp.bfloat16)
    return (context, (query_rows, key_rows, value_rows, offsets, row_top + jnp.log(totals)))


def attend_backward(d_context, attn_kept, same_item, onehot_low, rows_in):
    query_rows, key_rows, value_rows, offsets, log_total = attn_kept
    tokens = rows_in.shape[0]
    d_heads = d_context.reshape(query_rows.shape)
    scores = score_rows(query_rows, key_rows, offsets)
    probs = jnp.where(same_item, jnp.exp(jnp.where(same_item, scores, -1e30) - log_total), 0.0)
    d_values = jnp.einsum(
        "rhij,rihd->rjhd", probs.astype(jnp.bfloat16), d_heads, preferred_element_type=jnp.float32
    ).astype(jnp.bfloat16)
    d_probs = jnp.einsum("rihd,rjhd->rhij", d_heads, value_rows, preferred_element_type=jnp.float32)
    d_scores = (probs * (d_probs - jnp.sum(probs * d_probs, axis=-1, keepdims=True))).astype(
        jnp.bfloat16
    )
    table_grad = jnp.einsum(
        "rhij,ijb->bh", d_scores, onehot_low, preferred_element_type=jnp.float32
    )
    d_queries = jnp.einsum(
        "rhij,rjhd->rihd", d_scores, key_rows, preferred_element_type=jnp.float32
    ).astype(jnp.bfloat16)
    d_keys = jnp.einsum(
        "rhij,rihd->rjhd", d_scores, query_rows, preferred_element_type=jnp.float32
    ).astype(jnp.bfloat16)
    d_qkv = jnp.concatenate(
        [d_queries.reshape(tokens, -1), d_keys.reshape(tokens, -1), d_values.reshape(tokens, -1)],
        axis=1,
    )
    qkv_grad = jnp.einsum("td,tc->dc", rows_in, d_qkv, preferred_element_type=jnp.float32)
    return (d_qkv, qkv_grad, table_grad)


def feed_forward(rows_in, gate_up_weight):
    gate_up = jnp.dot(rows_in, gate_up_weight, preferred_element_type=jnp.float32)
    width = gate_up_weight.shape[1] // 2
    gate_proj = gate_up[:, :width]
    up_proj = gate_up[:, width:]
    act_value, act_pull = jax.vjp(gelu_tanh, gate_proj)
    inner_act = (act_value * up_proj).astype(jnp.bfloat16)
    return (inner_act, (up_proj, act_value, act_pull))


def feed_back(d_rows, inner_act, ff_kept, rows_in, down_here):
    up_proj, act_value, act_pull = ff_kept
    down_grad = jnp.einsum("tf,td->fd", inner_act, d_rows, preferred_element_type=jnp.float32)
    d_inner = jnp.einsum("td,fd->tf", d_rows, down_here, preferred_element_type=jnp.float32)
    d_gate = act_pull(d_inner * up_proj)[0].astype(jnp.bfloat16)
    d_up = (d_inner * act_value).astype(jnp.bfloat16)
    d_gate_up = jnp.concatenate([d_gate, d_up], axis=1)
    gate_up_grad = jnp.einsum("td,tf->df", rows_in, d_gate_up, preferred_element_type=jnp.float32)
    return (d_gate_up, gate_up_grad, down_grad)


def local(
    series,
    observed,
    item_split,
    recon_cot,
    gain_attn,
    gain_ff,
    gain_final,
    patch_weight,
    patch_bias,
    query_weight,
    key_weight,
    value_weight,
    out_weight,
    bias_table,
    gate_weight,
    up_weight,
    down_weight,
    head_weight,
    head_bias,
):
    rows_here, length = series.shape
    patch_len = patch_weight.shape[0]
    row_patches = length // patch_len
    half_len = length // 2
    local_split = lax.dynamic_slice_in_dim(
        item_split, lax.axis_index("head") * rows_here, rows_here, 0
    )
    split_col = local_split.astype(jnp.float32)[:, None]
    halves = series.reshape(rows_here, 2, half_len)
    obs_mask = observed.astype(jnp.float32).reshape(rows_here, 2, half_len)
    counts = item_combine(jnp.sum(obs_mask, axis=-1), split_col)
    item_mean = item_combine(jnp.sum(obs_mask * halves, axis=-1), split_col) / counts
    centred = halves - item_mean[..., None]
    item_var = item_combine(jnp.sum(obs_mask * centred * centred, axis=-1), split_col) / counts
    item_std = jnp.sqrt(item_var + 1e-05)
    normed = obs_mask * centred / item_std[..., None]
    patches = normed.reshape(-1, patch_len).astype(jnp.bfloat16)
    embedded = jnp.dot(
        patches, patch_weight, preferred_element_type=jnp.float32
    ) + patch_bias.astype(jnp.float32)
    attn_scale = norm_scale(embedded)
    attn_unit = embedded * attn_scale
    attn_in = (attn_unit * gain_attn.astype(jnp.float32)).astype(jnp.bfloat16)
    onehot = jnp.asarray(bucket_onehot(row_patches, BUCKETS, MAX_DIST))
    columns_here = query_weight.shape[1]
    ff_here = gate_weight.shape[1]
    heads_here = bias_table.shape[1]
    mixed = jnp.concatenate(
        [query_weight, key_weight, value_weight, gate_weight, up_weight], axis=1
    )
    mixed_all = lax.all_gather(mixed, "head", axis=0)
    rest_all = lax.all_gather(jnp.concatenate([out_weight, down_weight], axis=0), "head", axis=0)
    table_here = lax.all_gather(bias_table, "head", axis=1, tiled=True)

    def side(start, width):
        return jnp.moveaxis(mixed_all[:, :, start : start + width], 0, 1).reshape(
            mixed_all.shape[1], -1
        )

    qkv_weight = jnp.concatenate([side(i * columns_here, columns_here) for i in range(3)], axis=1)
    gate_up_weight = jnp.concatenate(
        [side(3 * columns_here + i * ff_here, ff_here) for i in range(2)], axis=1
    )
    out_here = rest_all[:, :columns_here].reshape(-1, rest_all.shape[2])
    down_here = rest_all[:, columns_here:].reshape(-1, rest_all.shape[2])
    same_item = same_items(local_split, row_patches)
    attn_rows = attn_in
    context, attn_kept = attend_forward(attn_rows, qkv_weight, table_here, onehot, same_item)
    attn_out = jnp.dot(context, out_here, preferred_element_type=jnp.float32)
    hidden_mid = embedded + attn_out
    ff_scale = norm_scale(hidden_mid)
    ff_unit = hidden_mid * ff_scale
    ff_in = (ff_unit * gain_ff.astype(jnp.float32)).astype(jnp.bfloat16)
    ff_rows = ff_in
    inner_act, ff_kept = feed_forward(ff_rows, gate_up_weight)
    ff_out = jnp.dot(inner_act, down_here, preferred_element_type=jnp.float32)
    hidden_end = hidden_mid + ff_out
    final_scale = norm_scale(hidden_end)
    final_unit = hidden_end * final_scale
    final_in = (final_unit * gain_final.astype(jnp.float32)).astype(jnp.bfloat16)
    output = jnp.dot(final_in, head_weight, preferred_element_type=jnp.float32) + head_bias.astype(
        jnp.float32
    )
    output_items = output.reshape(rows_here, 2, half_len)
    rebuilt = (output_items * item_std[..., None] + item_mean[..., None]).reshape(rows_here, length)
    cot_items = recon_cot.reshape(rows_here, 2, half_len)
    d_output = (cot_items * item_std[..., None]).reshape(-1, patch_len).astype(jnp.bfloat16)
    head_weight_grad = jnp.einsum(
        "td,tp->dp", final_in, d_output, preferred_element_type=jnp.float32
    )
    head_bias_grad = jnp.sum(d_output.astype(jnp.float32), axis=0)
    d_final = jnp.einsum("tp,dp->td", d_output, head_weight, preferred_element_type=jnp.float32)
    d_hidden_end, gain_final_grad = norm_back(
        d_final, final_unit, final_scale, gain_final.astype(jnp.float32)
    )
    ff_grad_low = d_hidden_end.astype(jnp.bfloat16)
    d_ff_rows = ff_grad_low
    d_gate_up, gate_up_grad, down_grad = feed_back(
        d_ff_rows, inner_act, ff_kept, ff_rows, down_here
    )
    d_ff_in = jnp.einsum(
        "tf,df->td", d_gate_up, gate_up_weight, preferred_element_type=jnp.float32
    )
    d_mid_norm, gain_ff_grad = norm_back(d_ff_in, ff_unit, ff_scale, gain_ff.astype(jnp.float32))
    d_hidden_mid = d_hidden_end + d_mid_norm
    attn_grad_low = d_hidden_mid.astype(jnp.bfloat16)
    d_attn_rows = attn_grad_low
    out_grad = jnp.einsum("tc,td->cd", context, d_attn_rows, preferred_element_type=jnp.float32)
    d_context = jnp.einsum(
        "td,cd->tc", d_attn_rows, out_here, preferred_element_type=jnp.float32
    ).astype(jnp.bfloat16)
    d_qkv, qkv_grad, table_grad = attend_backward(
        d_context, attn_kept, same_item, onehot.astype(jnp.bfloat16), attn_rows
    )
    d_attn_in = jnp.einsum("tc,dc->td", d_qkv, qkv_weight, preferred_element_type=jnp.float32)
    d_embed_norm, gain_attn_grad = norm_back(
        d_attn_in, attn_unit, attn_scale, gain_attn.astype(jnp.float32)
    )
    d_embedded = (d_hidden_mid + d_embed_norm).astype(jnp.bfloat16)
    patch_weight_grad = jnp.einsum(
        "tp,td->pd", patches, d_embedded, preferred_element_type=jnp.float32
    )
    patch_bias_grad = jnp.sum(d_embedded.astype(jnp.float32), axis=0)
    d_normed = jnp.einsum(
        "td,pd->tp", d_embedded, patch_weight, preferred_element_type=jnp.float32
    ).reshape(rows_here, 2, half_len)
    std_col = item_std[..., None]
    std_grad = (
        jnp.sum(cot_items * output_items, axis=-1) - jnp.sum(d_normed * normed, axis=-1) / item_std
    )
    var_weight = item_combine(std_grad / (2.0 * item_std) / counts, split_col)
    d_centred = d_normed * obs_mask / std_col + 2.0 * obs_mask * centred * var_weight[..., None]
    mean_grad = jnp.sum(cot_items, axis=-1) - jnp.sum(d_centred, axis=-1)
    mean_weight = item_combine(mean_grad / counts, split_col)
    series_grad = (d_centred + obs_mask * mean_weight[..., None]).reshape(rows_here, length)
    columns = qkv_grad.shape[1] // 3
    query_grad = qkv_grad[:, :columns]
    key_grad = qkv_grad[:, columns : 2 * columns]
    value_grad = qkv_grad[:, 2 * columns :]
    ff_columns = gate_up_grad.shape[1] // 2
    gate_grad = gate_up_grad[:, :ff_columns]
    up_grad = gate_up_grad[:, ff_columns:]
    def by_head(grad, width):
        return jnp.moveaxis(grad.reshape(grad.shape[0], -1, width), 1, 0)

    mixed_grad = jnp.concatenate(
        [by_head(g, columns_here) for g in (query_grad, key_grad, value_grad)]
        + [by_head(g, ff_here) for g in (gate_grad, up_grad)],
        axis=2,
    )
    rest_grad = jnp.concatenate(
        [
            out_grad.reshape(-1, columns_here, out_grad.shape[1]),
            down_grad.reshape(-1, ff_here, down_grad.shape[1]),
        ],
        axis=1,
    )
    mixed_grad = lax.psum_scatter(
        mixed_grad.astype(jnp.bfloat16), "head", scatter_dimension=0, tiled=True
    )[0].astype(jnp.float32)
    rest_grad = lax.psum_scatter(
        rest_grad.astype(jnp.bfloat16), "head", scatter_dimension=0, tiled=True
    )[0].astype(jnp.float32)
    mixed_grad, rest_grad = lax.psum((mixed_grad, rest_grad), "dp")
    query_grad, key_grad, value_grad = (
        mixed_grad[:, i * columns_here : (i + 1) * columns_here] for i in range(3)
    )
    gate_grad, up_grad = (
        mixed_grad[:, 3 * columns_here + i * ff_here : 3 * columns_here + (i + 1) * ff_here]
        for i in range(2)
    )
    out_grad, down_grad = (rest_grad[:columns_here], rest_grad[columns_here:])
    (
        table_grad,
        gain_attn_grad,
        gain_ff_grad,
        gain_final_grad,
        patch_weight_grad,
        patch_bias_grad,
        head_weight_grad,
        head_bias_grad,
    ) = lax.psum(
        (
            table_grad,
            gain_attn_grad,
            gain_ff_grad,
            gain_final_grad,
            patch_weight_grad,
            patch_bias_grad,
            head_weight_grad,
            head_bias_grad,
        ),
        ("dp", "head"),
    )
    table_grad = lax.dynamic_slice_in_dim(
        table_grad, lax.axis_index("head") * heads_here, heads_here, 1
    )
    return (
        rebuilt,
        series_grad,
        gain_attn_grad,
        gain_ff_grad,
        gain_final_grad,
        patch_weight_grad,
        patch_bias_grad,
        query_grad,
        key_grad,
        value_grad,
        out_grad,
        table_grad,
        gate_grad,
        up_grad,
        down_grad,
        head_weight_grad,
        head_bias_grad,
    )


def solution(mesh):
    placed = (
        P(("dp", "head"), None),
        P(("dp", "head"), None),
        P("dp"),
        P(("dp", "head"), None),
        P(),
        P(),
        P(),
        P(),
        P(),
        P(None, "head"),
        P(None, "head"),
        P(None, "head"),
        P("head", None),
        P(None, "head"),
        P(None, "head"),
        P(None, "head"),
        P("head", None),
        P(),
        P(),
    )
    return jax.shard_map(
        local,
        mesh=mesh,
        in_specs=placed,
        out_specs=(
            P(("dp", "head"), None),
            P(("dp", "head"), None),
            P(),
            P(),
            P(),
            P(),
            P(),
            P(None, "head"),
            P(None, "head"),
            P(None, "head"),
            P("head", None),
            P(None, "head"),
            P(None, "head"),
            P(None, "head"),
            P("head", None),
            P(),
            P(),
        ),
        check_vma=False,
    )
```

```python
import functools
import math

import jax
import jax.numpy as jnp
from jax import lax
from jax.experimental import pallas as pl
from jax.experimental.pallas import tpu as pltpu
from jax.sharding import PartitionSpec as P

F32 = jnp.float32
BF16 = jnp.bfloat16
EPS = 1e-06
TILE = 256
MAX_DIST = 128


def bucket_cuts(buckets, length):
    half_count = buckets // 2
    exact_count = half_count // 2
    ids = []
    for distance in range(length):
        if distance < exact_count:
            ids.append(distance)
        else:
            ids.append(
                min(
                    half_count - 1,
                    exact_count
                    + int(
                        math.log(distance / exact_count)
                        / math.log(MAX_DIST / exact_count)
                        * (half_count - exact_count)
                    ),
                )
            )
    cuts = []
    for distance in range(1, length):
        cuts += [distance] * (ids[distance] - ids[distance - 1])
    return cuts, ids[-1]


def nt(left, right):
    return lax.dot_general(left, right, (((1,), (1,)), ((), ())), preferred_element_type=F32)


def nn(left, right):
    return jnp.dot(left, right, preferred_element_type=F32)


def tn(left, right):
    return lax.dot_general(left, right, (((0,), (0,)), ((), ())), preferred_element_type=F32)


def iota(shape, dim):
    return lax.broadcasted_iota(jnp.int32, shape, dim)


def fold8(values):
    return jnp.sum(values.reshape(values.shape[0] // 8, 8, values.shape[1]), axis=0)


def row_scale(values):
    return lax.rsqrt(jnp.mean(values * values, axis=-1, keepdims=True) + EPS)


def norm_back(grad_out, unit_rows, scale, gain_row):
    d_unit = grad_out * gain_row
    spread = jnp.mean(d_unit * unit_rows, axis=-1, keepdims=True)
    return scale * (d_unit - unit_rows * spread), fold8(grad_out * unit_rows)


class Layer:
    def __init__(self, **refs):
        self.__dict__.update(refs)

    def prepare(self, head_index):
        rows, steps = self.series.shape
        half = steps // 2
        length = self.pm.shape[0]
        patch = steps // length
        split_row = self.split[...].astype(F32)
        pick = iota((rows, split_row.shape[1]), 1) == (
            iota((rows, split_row.shape[1]), 0) + head_index * rows
        )
        split_col = jnp.sum(jnp.where(pick, split_row, 0.0), axis=1, keepdims=True)
        self.splitb[...] = jnp.broadcast_to(split_col, self.splitb.shape)
        obs = self.observed[...].astype(F32)
        series = self.series[...]
        low_half = iota((rows, steps), 1) < half

        def halves(values):
            return [
                jnp.sum(values[:, :half], axis=1, keepdims=True),
                jnp.sum(values[:, half:], axis=1, keepdims=True),
            ]

        def combine(sums):
            both = sums[0] + sums[1]
            return [split_col * one + (1.0 - split_col) * both for one in sums]

        def spread(pair):
            return jnp.where(low_half, pair[0], pair[1])

        self.halves, self.combine, self.spread = halves, combine, spread
        self.counts = combine(halves(obs))
        item_mean = [a / b for a, b in zip(combine(halves(obs * series)), self.counts)]
        centred = series - spread(item_mean)
        item_var = [a / b for a, b in zip(combine(halves(obs * centred * centred)), self.counts)]
        self.std = [jnp.sqrt(v + 1e-05) for v in item_var]
        std_full = spread(self.std)
        self.std_full, self.mean_full = std_full, spread(item_mean)
        normed = obs * centred / std_full
        self.normed[...] = normed
        self.normed_low[...] = normed.astype(BF16).astype(F32)
        self.dout_low[...] = (self.cot[...] * std_full).astype(BF16).astype(F32)
        self.pm[...] = (iota(self.pm.shape, 1) // patch == iota(self.pm.shape, 0)).astype(F32)
        fold = (iota(self.fold.shape, 1) % patch == iota(self.fold.shape, 0)).astype(BF16)
        self.fold[...] = fold
        pw = self.patch_w[...].astype(F32)
        self.ptile[...] = jnp.broadcast_to(
            pw[None], (self.ptile.shape[0] // patch, patch, pw.shape[1])
        ).reshape(self.ptile.shape).astype(BF16)
        self.htile[...] = nn(self.head_w[...], fold[:patch]).astype(BF16)
        hb = jnp.broadcast_to(self.head_b[...], (16, patch))
        self.hbias = nn(hb, fold[:patch])[0:1]

    def spread_rows(self, source, tile):
        rows_tile = TILE // self.pm.shape[0]
        mask = self.pm[...]
        pieces = [
            (source[pl.ds(tile * rows_tile + r, 1), :] * mask).astype(BF16)
            for r in range(rows_tile)
        ]
        return jnp.concatenate(pieces, axis=0)

    def gather_rows(self, target, tile, values, extra=None):
        length = self.pm.shape[0]
        mask = self.pm[...]
        for r in range(TILE // length):
            part = jnp.sum(values[r * length : (r + 1) * length] * mask, axis=0, keepdims=True)
            if extra is not None:
                part = part + extra
            target[pl.ds(tile * (TILE // length) + r, 1), :] = part

    def embed(self, tile):
        at = pl.ds(pl.multiple_of(tile * TILE, TILE), TILE)
        spread = self.spread_rows(self.normed_low, tile)
        self.p8t[:, at] = nt(self.fold[...], spread).astype(BF16)
        embedded = nn(spread, self.ptile[...]) + self.patch_b[...].astype(F32)
        self.embedded[at, :] = embedded
        scale = row_scale(embedded)
        self.s_attn[at, :] = scale
        self.attn_in[at, :] = (embedded * scale * self.gain_attn[...].astype(F32)).astype(BF16)

    def buckets(self):
        length = self.pm.shape[0]
        lanes = 2 * length
        key = iota((length, lanes), 0)
        query = iota((length, lanes), 1) % length
        offset = key - query
        distance = jnp.abs(offset)
        table = self.tab.shape[1]
        cuts, top = bucket_cuts(table, length)
        ids = jnp.where(offset > 0, table // 2, 0)
        for cut in cuts:
            ids = ids + (distance >= cut).astype(jnp.int32)
        used = list(range(top + 1)) + list(range(table // 2, table // 2 + top + 1))
        return ids, used

    def own_table(self):
        table = self.table[...].astype(F32)
        lane = iota((table.shape[0], 128), 1)
        self.tab[0] = jnp.where(lane < 64, table[:, 0:1], table[:, 1:2])

    def offsets(self, slot):
        ids, used = self.buckets()
        total = jnp.zeros(ids.shape, F32)
        for b in used:
            total = jnp.where(ids == b, self.tab[slot, b : b + 1, :], total)
        self.bias[slot] = total

    def head_masks(self):
        lane = iota((1, 128), 1)
        return (lane < 64).astype(BF16), (lane >= 64).astype(BF16)

    def attend(self, slot, tile):
        at = pl.ds(pl.multiple_of(tile * TILE, TILE), TILE)
        wide = pl.ds(pl.multiple_of(slot * 384, 128), 384)
        length = self.pm.shape[0]
        even, odd = self.head_masks()
        projected = nn(self.attn_in[at, :], self.wq[:, wide]).astype(BF16)
        self.qkv[at, wide] = projected
        bias = self.bias[slot]
        block = (
            iota(bias.shape, 0) // (length // 2) != (iota(bias.shape, 1) % length) // (length // 2)
        ).astype(F32) * -1e30
        contexts = []
        for r in range(TILE // length):
            rows = slice(r * length, (r + 1) * length)
            query, key, value = (projected[rows, i * 128 : (i + 1) * 128] for i in range(3))
            both = jnp.concatenate([query * even, query * odd], axis=0)
            split = self.splitb[pl.ds(tile * (TILE // length) + r, 1), :]
            scores = nt(key, both) + (bias + split * block)
            top = jnp.max(scores, axis=0, keepdims=True)
            raised = jnp.exp(scores - top)
            probs = raised * (1.0 / jnp.sum(raised, axis=0, keepdims=True))
            self.probs[slot, pl.ds(pl.multiple_of(tile * TILE + r * length, length), length), :] = (
                probs
            )
            mixed = tn(probs.astype(BF16), value)
            contexts.append(
                jnp.where(iota((1, 128), 1) < 64, mixed[:length], mixed[length:]).astype(BF16)
            )
        self.ctx[at, pl.ds(pl.multiple_of(slot * 128, 128), 128)] = jnp.concatenate(
            contexts, axis=0
        )

    def middle(self, tile):
        at = pl.ds(pl.multiple_of(tile * TILE, TILE), TILE)
        hidden_mid = self.embedded[at, :] + nt(self.ctx[at, :], self.wo[...])
        ff_scale = row_scale(hidden_mid)
        ff_unit = hidden_mid * ff_scale
        gain_ff = self.gain_ff[...].astype(F32)
        ff_in = (ff_unit * gain_ff).astype(BF16)
        self.ff_in[at, :] = ff_in
        slots = self.slots
        ff_out = None
        keep = []
        for s in range(slots):
            w = self.wg.shape[1] // slots
            gu = nn(ff_in, self.wg[:, s * w : (s + 1) * w])
            gate, up = gu[:, : w // 2], gu[:, w // 2 :]
            c = math.sqrt(2.0 / math.pi)
            square = gate * gate
            t = jnp.tanh(gate * (c + (c * 0.044715) * square))
            plus = 0.5 * (1.0 + t)
            act = gate * plus
            slope = plus + (0.5 * gate) * (1.0 - t * t) * (c + (3.0 * c * 0.044715) * square)
            inner = (act * up).astype(BF16)
            cols = slice(s * (w // 2), (s + 1) * (w // 2))
            self.inner[at, cols] = inner
            self.act[:, cols] = act.astype(BF16)
            self.slope[:, cols] = (up * slope).astype(BF16)
        ff_out = nt(self.inner[at, :], self.wd[...])
        hidden_end = hidden_mid + ff_out
        final_scale = row_scale(hidden_end)
        final_unit = hidden_end * final_scale
        gain_final = self.gain_final[...].astype(F32)
        final_in = (final_unit * gain_final).astype(BF16)
        self.final_in[at, :] = final_in
        self.gather_rows(self.output, tile, nn(final_in, self.htile[...]), self.hbias)
        d_spread = self.spread_rows(self.dout_low, tile)
        self.d8t[:, at] = nt(self.fold[...], d_spread).astype(BF16)
        d_final = nt(d_spread, self.htile[...])
        d_end, gain_part = norm_back(d_final, final_unit, final_scale, gain_final)
        self.g_final[...] += gain_part
        d_low = d_end.astype(BF16)
        self.d_end_low[at, :] = d_low
        d_in = None
        for s in range(slots):
            w = self.wg.shape[1] // slots
            cols = slice(s * (w // 2), (s + 1) * (w // 2))
            d_inner = nn(d_low, self.wd[:, cols])
            d_gate = (d_inner * self.slope[:, cols].astype(F32)).astype(BF16)
            d_up = (d_inner * self.act[:, cols].astype(F32)).astype(BF16)
            self.dgu[at, s * w : s * w + w // 2] = d_gate
            self.dgu[at, s * w + w // 2 : (s + 1) * w] = d_up
        d_in = nt(self.dgu[at, :], self.wg[...])
        d_norm, gain_part = norm_back(d_in, ff_unit, ff_scale, gain_ff)
        self.g_ff[...] += gain_part
        d_mid = d_end + d_norm
        self.d_mid[at, :] = d_mid
        d_mid_low = d_mid.astype(BF16)
        self.d_mid_low[at, :] = d_mid_low
        self.d_ctx[at, :] = nn(d_mid_low, self.wo[...]).astype(BF16)

    def attend_back(self, slot, tile):
        length = self.pm.shape[0]
        even, odd = self.head_masks()
        total = jnp.zeros((length, 128), F32)
        for r in range(TILE // length):
            rows = pl.ds(pl.multiple_of(tile * TILE + r * length, length), length)

            def part(i):
                return self.qkv[rows, pl.ds(pl.multiple_of(slot * 384 + i * 128, 128), 128)]

            query, key, value = part(0), part(1), part(2)
            d_ctx = self.d_ctx[rows, pl.ds(pl.multiple_of(slot * 128, 128), 128)]
            query_both = jnp.concatenate([query * even, query * odd], axis=0)
            d_both = jnp.concatenate([d_ctx * even, d_ctx * odd], axis=0)
            probs = self.probs[slot, rows, :]
            d_probs = nt(value, d_both)
            d_value = nn(probs.astype(BF16), d_both)
            dots = jnp.sum(probs * d_probs, axis=0, keepdims=True)
            d_scores = (probs * (d_probs - dots)).astype(BF16)
            total = total + d_scores.astype(F32)
            d_key = nn(d_scores, query_both)
            mixed = tn(d_scores, key)
            d_query = jnp.where(iota((1, 128), 1) < 64, mixed[:length], mixed[length:])
            for i, grad in enumerate((d_query, d_key, d_value)):
                self.dqkv[rows, pl.ds(pl.multiple_of(slot * 384 + i * 128, 128), 128)] = (
                    grad.astype(BF16)
                )
        self.dsum[slot] += total

    def embed_back(self, tile):
        at = pl.ds(pl.multiple_of(tile * TILE, TILE), TILE)
        d_in = nt(self.dqkv[at, :], self.wq[...])
        scale = self.s_attn[at, :]
        d_norm, gain_part = norm_back(
            d_in, self.embedded[at, :] * scale, scale, self.gain_attn[...].astype(F32)
        )
        self.g_attn[...] += gain_part
        d_embedded = (self.d_mid[at, :] + d_norm).astype(BF16)
        self.d_emb[at, :] = d_embedded
        self.g_bias[...] += fold8(d_embedded.astype(F32))
        self.gather_rows(self.d_normed, tile, nt(d_embedded, self.ptile[...]))

    def finish(self):
        obs = self.observed[...].astype(F32)
        cot = self.cot[...]
        output = self.output[...]
        std_full, mean_full = self.std_full, self.mean_full
        self.rebuilt[...] = output * std_full + mean_full
        d_normed = self.d_normed[...]
        std_grad = [
            a - b / c
            for a, b, c in zip(
                self.halves(cot * output), self.halves(d_normed * self.normed[...]), self.std
            )
        ]
        var_weight = self.combine(
            [g / (2.0 * s) / n for g, s, n in zip(std_grad, self.std, self.counts)]
        )
        centred = self.series[...] - mean_full
        d_centred = d_normed * obs / std_full + 2.0 * obs * centred * self.spread(var_weight)
        mean_grad = [a - b for a, b in zip(self.halves(cot), self.halves(d_centred))]
        mean_weight = self.combine([g / n for g, n in zip(mean_grad, self.counts)])
        self.series_grad[...] = d_centred + obs * self.spread(mean_weight)

    def small_grads(self, head_index):
        small = self.small
        heads = self.slots
        zero = jnp.zeros((4, self.embedded.shape[1]), F32)
        small[0:8, :] = jnp.concatenate(
            [jnp.sum(r[...], axis=0, keepdims=True) for r in (self.g_attn, self.g_ff, self.g_final, self.g_bias)]
            + [zero],
            axis=0,
        )
        small[8:16, :] = nn(self.p8t[...], self.d_emb[...])[0:8]
        small[16:24, :] = nn(self.d8t[...], self.final_in[...])[0:8]
        lane = iota((8, 128), 1)
        groups = self.tab.shape[1] // 8
        pieces = [jnp.zeros((8, 128), F32) for _ in range(groups)]
        pieces[0] = jnp.where(
            lane == 2 * heads, jnp.sum(self.d8t[0:8, :].astype(F32), axis=1, keepdims=True), 0.0
        )
        ids, used = self.buckets()
        for s in range(self.slots):
            dsum = self.dsum[s]
            owner = lax.rem(head_index + s, heads)
            for b in range(self.tab.shape[1]):
                if b in used:
                    self.tgr[b : b + 1, :] = jnp.sum(
                        jnp.where(ids == b, dsum, 0.0), axis=0, keepdims=True
                    )
                else:
                    self.tgr[b : b + 1, :] = jnp.zeros((1, 128), F32)
            for g in range(groups):
                rows = self.tgr[8 * g : 8 * g + 8, :]
                for which in range(2):
                    inside = (lane < 64) if which == 0 else (lane >= 64)
                    column = jnp.sum(jnp.where(inside, rows, 0.0), axis=1, keepdims=True)
                    pieces[g] = pieces[g] + jnp.where(lane == 2 * owner + which, column, 0.0)
        small[24:32, :] = jnp.concatenate(pieces, axis=1)

    def small_out(self, head_index):
        small = self.small
        for row, out in enumerate((self.o_attn, self.o_ff, self.o_final, self.o_pb)):
            out[...] = small[row : row + 1, :]
        self.o_pw[...] = small[8:16, :]
        patch = self.o_pw.shape[0]
        block = jnp.concatenate(
            [small[16:24, :], jnp.zeros((120, small.shape[1]), F32)], axis=0
        )
        self.o_hw[...] = block.T[:, :patch]
        lane = iota((8, 128), 1)
        column = jnp.sum(
            jnp.where(lane == 2 * self.slots, small[24:32, 0:128], 0.0), axis=1, keepdims=True
        )
        self.o_hb[...] = jnp.sum(jnp.where(lane == iota((8, 128), 0), column, 0.0), axis=0, keepdims=True)[
            :, :patch
        ]
        for g in range(self.tab.shape[1] // 8):
            piece = small[24:32, g * 128 : (g + 1) * 128]
            columns = [
                jnp.sum(
                    jnp.where(lane == 2 * head_index + which, piece, 0.0), axis=1, keepdims=True
                )
                for which in range(2)
            ]
            self.o_table[8 * g : 8 * g + 8, :] = jnp.where(
                iota((8, 2), 1) == 0, columns[0], columns[1]
            )

    def clear(self):
        for ref in (self.g_attn, self.g_ff, self.g_final, self.g_bias):
            ref[...] = jnp.zeros(ref.shape, F32)
        self.dsum[...] = jnp.zeros(self.dsum.shape, F32)


MESH = pl.DeviceIdType.MESH


class Net:
    def __init__(self, groups, heads, send_sems, recv_sems):
        self.dp, self.head = lax.axis_index("dp"), lax.axis_index("head")
        self.bits = groups.bit_length() - 1
        self.heads = heads
        self.send_sems, self.recv_sems = send_sems, recv_sems
        self.used = 0
        self.sent = []

    def bit(self, which):
        return (self.dp // (1 << which)) % 2

    def across(self, which):
        step = 1 << which
        return (self.dp + (1 - 2 * self.bit(which)) * step, self.head)

    def beside(self, hops):
        return (self.dp, (self.head + hops) % self.heads)

    def beside_bit(self, which):
        step = 1 << which
        mine = (self.head // step) % 2
        return (self.dp, self.head + (1 - 2 * mine) * step)

    def greet_start(self):
        barrier = pltpu.get_barrier_semaphore()
        partners = [self.across(b) for b in range(self.bits)]
        partners += [self.beside(t) for t in range(1, self.heads)]
        for partner in partners:
            pl.semaphore_signal(barrier, inc=1, device_id=partner, device_id_type=MESH)

    def greet_end(self):
        pl.semaphore_wait(pltpu.get_barrier_semaphore(), self.bits + self.heads - 1)

    def claim(self):
        self.used += 1
        return self.used - 1

    def copy(self, index, src, dst, device):
        return pltpu.make_async_remote_copy(
            src_ref=src,
            dst_ref=dst,
            send_sem=self.send_sems.at[index],
            recv_sem=self.recv_sems.at[index],
            device_id=device,
            device_id_type=MESH,
        )

    def send(self, index, src, dst, device):
        copy = self.copy(index, src, dst, device)
        copy.start()
        self.sent.append(copy)

    def arrived(self, index, dst, device):
        self.copy(index, dst, dst, device).wait_recv()

    def drain(self):
        for copy in self.sent:
            copy.wait_send()
        self.sent = []


def rows_at(start, count, unit):
    return pl.ds(pl.multiple_of(start, unit), count)


class Gather:
    ORDERS = ((1, 2, 0), (2, 1, 0))

    def __init__(self, net, ref):
        self.net, self.ref = net, ref
        self.heads = net.heads
        self.width = ref.shape[1] // self.heads
        self.unit = ref.shape[0] // 16
        self.ids = [[net.claim() for _ in range(net.heads - 1 + 3)] for _ in range(2)]

    def block(self, half):
        bits = [self.net.bit(b) for b in self.ORDERS[half]]
        return bits[0] + 2 * bits[1] + 4 * bits[2]

    def span(self, half, level, mine=True):
        size = 1 << level
        first = self.block(half) // size
        if not mine:
            first = first + 1 - 2 * (first % 2)
        return rows_at((half * 8 + first * size) * self.unit, size * self.unit, self.unit)

    def start(self):
        net, width = self.net, self.width
        for half in range(2):
            rows = self.span(half, 0)
            for t in range(1, self.heads):
                slot = self.heads - t
                net.send(
                    self.ids[half][t - 1],
                    self.ref.at[rows, 0:width],
                    self.ref.at[rows, slot * width : (slot + 1) * width],
                    net.beside(t),
                )

    def step(self, level):
        net, width = self.net, self.width
        others = pl.ds(width, (self.heads - 1) * width)
        for half in range(2):
            if level == 0:
                for t in range(1, self.heads):
                    slot = self.heads - t
                    net.arrived(
                        self.ids[half][t - 1],
                        self.ref.at[self.span(half, 0), slot * width : (slot + 1) * width],
                        net.beside(t),
                    )
            else:
                net.arrived(
                    self.ids[half][self.heads - 2 + level],
                    self.ref.at[self.span(half, level - 1, mine=False), others],
                    net.across(self.ORDERS[half][level - 1]),
                )
            if level < 3:
                rows = self.span(half, level)
                net.send(
                    self.ids[half][self.heads - 1 + level],
                    self.ref.at[rows, others],
                    self.ref.at[rows, others],
                    net.across(self.ORDERS[half][level]),
                )


class Reduce:
    ORDERS = ((1, 2), (2, 1))

    def __init__(self, net, refs, columns, width):
        self.net = net
        self.heads = net.heads
        self.width = width
        self.columns = columns
        (
            self.own, self.snd0, self.rcv0, self.snd1, self.rcv1,
            self.snd2, self.rcv2, self.sndz, self.rcvz, self.fin,
        ) = refs
        self.ids = {}

    def id(self, name):
        if name not in self.ids:
            self.ids[name] = self.net.claim()
        return self.ids[name]

    def slots(self, s):
        first = self.columns.start + s * self.width
        return slice(first, first + self.width)

    @property
    def fin_columns(self):
        first = self.columns.start // self.heads
        return slice(first, first + self.width)

    def produce(self, left_t, right, block=512):
        net = self.net
        count = self.own.shape[0]
        core = net.bit(0)
        wide = self.columns.stop - self.columns.start
        for c in range(0, wide, block):
            cols = slice(self.columns.start + c, self.columns.start + c + block)
            self.snd0[:, cols] = nn(
                left_t[rows_at((1 - core) * count, count, count), :], right[:, c : c + block]
            ).astype(BF16)
        net.send(
            self.id("r0"), self.snd0.at[:, self.columns], self.rcv0.at[:, self.columns], net.across(0)
        )
        for c in range(0, wide, block):
            cols = slice(self.columns.start + c, self.columns.start + c + block)
            self.own[:, cols] = nn(
                left_t[rows_at(core * count, count, count), :], right[:, c : c + block]
            )

    def halving(self, level):
        net, cols = self.net, self.columns
        source = (self.rcv0, self.rcv1, self.rcv2)[level]
        count = self.own.shape[0] // 2 >> level
        if level == 0:
            net.arrived(self.id("r0"), self.rcv0.at[:, cols], net.across(0))
        for half in range(2):
            first = half * count
            if level > 0:
                net.arrived(
                    self.id(f"r{level}{half}"),
                    source.at[first : first + count, cols],
                    net.across(self.ORDERS[half][level - 1]),
                )
            at = self.kept(half, level)
            if level < 2:
                bit = net.bit(self.ORDERS[half][level])
                away = (1 - bit) * (count // 2)
                send, target = ((self.snd1, self.rcv1), (self.snd2, self.rcv2))[level]
                place = slice(half * (count // 2), (half + 1) * (count // 2))
                send[place, cols] = (
                    self.own[rows_at(at + away, count // 2, 32), cols]
                    + source[rows_at(first + away, count // 2, 32), cols].astype(F32)
                ).astype(BF16)
                net.send(
                    self.id(f"r{level + 1}{half}"),
                    send.at[place, cols],
                    target.at[place, cols],
                    net.across(self.ORDERS[half][level]),
                )
        for half in range(2):
            at = self.kept(half, level)
            first = half * count
            if level < 2:
                bit = net.bit(self.ORDERS[half][level])
                stay = bit * (count // 2)
                rows = rows_at(at + stay, count // 2, 32)
                self.own[rows, cols] = self.own[rows, cols] + source[
                    rows_at(first + stay, count // 2, 32), cols
                ].astype(F32)
            else:
                rows = rows_at(at, count, 32)
                total = self.own[rows, cols] + source[first : first + count, cols].astype(F32)
                self.own[rows, cols] = total
                if net.bits <= 3:
                    self.sndz[first : first + count, cols] = total.astype(BF16)

    def kept(self, half, level):
        count = self.own.shape[0] // 2
        start = half * count
        for step in range(level):
            count = count // 2
            start = start + self.net.bit(self.ORDERS[half][step]) * count
        return start

    def groups(self):
        net, cols = self.net, self.columns
        count = self.sndz.shape[0] // 2
        for bit in range(3, net.bits):
            inbox = self.extra.at[bit - 3]
            key = f"g{bit}"
            for half in range(2):
                rows = rows_at(self.kept(half, 2), count, 32)
                self.sndz[half * count : (half + 1) * count, cols] = self.own[rows, cols].astype(
                    BF16
                )
            copy = net.copy(
                self.id(key), self.sndz.at[:, cols], inbox.at[:, cols], net.across(bit)
            )
            copy.start()
            copy.wait()
            for half in range(2):
                rows = rows_at(self.kept(half, 2), count, 32)
                place = slice(half * count, (half + 1) * count)
                self.own[rows, cols] = self.sndz[place, cols].astype(F32) + inbox[
                    place, cols
                ].astype(F32)
        if net.bits > 3:
            for half in range(2):
                rows = rows_at(self.kept(half, 2), count, 32)
                self.sndz[half * count : (half + 1) * count, cols] = self.own[rows, cols].astype(
                    BF16
                )

    def owners(self):
        net = self.net
        for s in range(1, self.heads):
            net.send(
                self.id(f"z{s}"),
                self.sndz.at[:, self.slots(s)],
                self.rcvz.at[s - 1, :, self.fin_columns],
                net.beside(s),
            )

    def place(self, half, level, mine=True):
        net = self.net
        quarter = self.fin.shape[0] // 4
        count = quarter // 4
        start = net.bit(0) * 2 * quarter + half * quarter
        order = self.ORDERS[half]
        if level == 0:
            inner = net.bit(order[1]) if mine else 1 - net.bit(order[1])
            start = start + net.bit(order[0]) * 2 * count + inner * count
            return rows_at(start, count, count)
        outer = net.bit(order[0]) if mine else 1 - net.bit(order[0])
        return rows_at(start + outer * 2 * count, 2 * count, count)

    def owned(self):
        net = self.net
        fin = self.fin_columns
        count = self.sndz.shape[0] // 2
        for s in range(1, self.heads):
            net.arrived(self.id(f"z{s}"), self.rcvz.at[s - 1, :, fin], net.beside(s))
        for half in range(2):
            part = slice(half * count, (half + 1) * count)
            total = self.own[rows_at(self.kept(half, 2), count, 32), self.slots(0)]
            for s in range(1, self.heads):
                total = total + self.rcvz[s - 1, part, fin].astype(F32)
            rows = self.place(half, 0)
            self.fin[rows, fin] = total.astype(BF16)
            net.send(
                self.id(f"f0{half}"),
                self.fin.at[rows, fin],
                self.fin.at[rows, fin],
                net.across(self.ORDERS[half][1]),
            )

    def spread(self, level):
        net, fin = self.net, self.fin_columns
        if level < 2:
            for half in range(2):
                net.arrived(
                    self.id(f"f{level}{half}"),
                    self.fin.at[self.place(half, level, mine=False), fin],
                    net.across(self.ORDERS[half][1 - level]),
                )
                if level == 0:
                    rows = self.place(half, 1)
                    net.send(
                        self.id(f"f1{half}"),
                        self.fin.at[rows, fin],
                        self.fin.at[rows, fin],
                        net.across(self.ORDERS[half][0]),
                    )
        half_rows = self.fin.shape[0] // 2
        core = net.bit(0)
        if level == 1:
            rows = rows_at(core * half_rows, half_rows, half_rows)
            net.send(
                self.id("f2"), self.fin.at[rows, fin], self.fin.at[rows, fin], net.across(0)
            )
        if level == 2:
            rows = rows_at((1 - core) * half_rows, half_rows, half_rows)
            net.arrived(self.id("f2"), self.fin.at[rows, fin], net.across(0))

    def steps(self):
        return [
            lambda: self.halving(0),
            lambda: self.halving(1),
            lambda: (self.halving(2), self.groups(), self.owners()),
            self.owned,
            lambda: self.spread(0),
            lambda: self.spread(1),
            lambda: self.spread(2),
        ]


class Total:
    def __init__(self, net, slabs, inbox):
        self.net, self.slabs, self.inbox = net, slabs, inbox
        self.partners = [net.across(b) for b in range(net.bits)]
        self.partners += [net.beside_bit(b) for b in range(net.heads.bit_length() - 1)]
        self.ids = [net.claim() for _ in self.partners]

    def start(self, level):
        self.net.send(
            self.ids[level], self.slabs.at[level], self.inbox.at[level], self.partners[level]
        )

    def step(self, level):
        self.net.arrived(self.ids[level], self.inbox.at[level], self.partners[level])
        self.slabs[level + 1] = self.slabs[level] + self.inbox[level]
        if level + 1 < len(self.partners):
            self.start(level + 1)


def loop(count, body):
    def once(i, carry):
        body(i)
        return carry

    lax.fori_loop(0, count, once, 0)


INPUTS = (
    "series", "observed", "split", "cot", "gain_attn", "gain_ff", "gain_final", "patch_w", "patch_b", "wq_in", "wk_in", "wv_in", "wo_in", "table", "wg_in", "wu_in", "wd_in", "head_w", "head_b",
)
OUTPUTS = (
    "rebuilt", "series_grad", "o_attn", "o_ff", "o_final", "o_pw", "o_pb", "o_q", "o_k", "o_v", "o_o", "o_table", "o_g", "o_u", "o_d", "o_hw", "o_hb",
)
SHARED = (
    "own", "snd0", "rcv0", "snd1", "rcv1", "snd2", "rcv2", "sndz", "rcvz", "fin",
)


def layer_kernel(groups, heads, names, *refs):
    named = dict(zip(names, refs))
    dgu = named["dgu"]
    wq, wo, wg, wd = (named[k] for k in ("wq", "wo", "wg", "wd"))
    named["dqkv"] = dgu.at[:, 0 : wq.shape[1]]
    named["d_emb"] = named["ff_in"]
    named["fin"] = wg.at[:, 0 : named["rcvz"].shape[2]]
    layer = Layer(slots=heads, **named)
    tiles = layer.embedded.shape[0] // TILE
    net = Net(groups, heads, named["send_sems"], named["recv_sems"])
    net.greet_start()
    part = layer.wq_in.shape[1]
    for i, ref in enumerate((layer.wq_in, layer.wk_in, layer.wv_in)):
        wq[:, i * part : (i + 1) * part] = ref[...]
    wo[:, 0 : layer.wo_in.shape[0]] = layer.wo_in[...].T
    part = layer.wg_in.shape[1]
    for i, ref in enumerate((layer.wg_in, layer.wu_in)):
        wg[:, i * part : (i + 1) * part] = ref[...]
    wd[:, 0 : layer.wd_in.shape[0]] = layer.wd_in[...].T
    layer.own_table()
    net.greet_end()
    gather_q, gather_o, gather_g, gather_d = (Gather(net, ref) for ref in (wq, wo, wg, wd))
    table_ids = [net.claim() for _ in range(heads - 1)]
    gather_q.start()
    for t in range(1, heads):
        net.send(table_ids[t - 1], layer.tab.at[0], layer.tab.at[heads - t], net.beside(t))
    gather_o.start()
    gather_g.start()
    gather_d.start()
    layer.clear()
    layer.prepare(net.head)
    loop(tiles, layer.embed)
    layer.offsets(0)
    gather_q.step(0)
    loop(tiles // 2, lambda t: layer.attend(0, t))
    gather_o.step(0)
    gather_q.step(1)
    loop(tiles // 2, lambda t: layer.attend(0, t + tiles // 2))
    gather_g.step(0)
    gather_o.step(1)
    gather_q.step(2)
    for t in range(1, heads):
        net.arrived(table_ids[t - 1], layer.tab.at[heads - t], net.beside(t))
    loop(heads - 1, lambda s: layer.offsets(s + 1))
    gather_d.step(0)
    gather_g.step(1)
    gather_q.step(3)
    loop(tiles, lambda t: layer.attend(1, t))
    gather_o.step(2)
    gather_d.step(1)
    gather_g.step(2)
    loop(tiles, lambda t: layer.attend(2, t))
    gather_o.step(3)
    gather_d.step(2)
    gather_g.step(3)
    loop(tiles, lambda t: layer.attend(3, t))
    gather_d.step(3)
    net.drain()
    loop(tiles, layer.middle)
    shared = [named[k] for k in SHARED]
    bounds = {}
    first = 0
    for key, ref in zip("qogd", (wq, wo, wg, wd)):
        bounds[key] = slice(first, first + ref.shape[1])
        first += ref.shape[1]
    reduce = {
        key: Reduce(net, shared, bounds[key], ref.shape[1] // heads)
        for key, ref in zip("qogd", (wq, wo, wg, wd))
    }
    for one in reduce.values():
        one.extra = named.get("extra")
    left, right = layer.left_t, layer.right_t
    left[...] = layer.ff_in[...].T
    reduce["g"].produce(left, dgu)
    right[...] = layer.d_end_low[...].T
    reduce["d"].produce(right, layer.inner)
    left[...] = layer.d_mid_low[...].T
    reduce["o"].produce(left, layer.ctx)
    right[...] = layer.attn_in[...].T
    pending = []
    steps = {key: reduce[key].steps() for key in "god"}
    for level in range(7):
        pending += [steps[key][level] for key in "gdo"]

    def advance(count):
        for _ in range(min(count, len(pending))):
            pending.pop(0)()

    for s in range(heads):
        advance(2)
        loop(tiles // 2, lambda t: layer.attend_back(s, t))
        advance(3)
        loop(tiles // 2, lambda t: layer.attend_back(s, t + tiles // 2))
    reduce["q"].produce(right, named["dqkv"])
    advance(1)
    loop(tiles, layer.embed_back)
    last = reduce["q"].steps()
    last[0]()
    layer.small = named["slabs"].at[0]
    layer.small_grads(net.head)
    total = Total(net, named["slabs"], named["inbox"])
    total.start(0)
    last[1]()
    layer.finish()
    total.step(0)
    last[2]()
    advance(len(pending))
    levels = len(total.partners)
    total.step(1)
    last[3]()
    total.step(2)
    last[4]()
    total.step(3)
    last[5]()
    fin = named["fin"]
    ff = layer.o_g.shape[1]
    layer.o_o[...] = fin[:, 3 * 128 : 4 * 128].astype(F32).T
    layer.o_g[...] = fin[:, 512 : 512 + ff].astype(F32)
    layer.o_u[...] = fin[:, 512 + ff : 512 + 2 * ff].astype(F32)
    layer.o_d[...] = fin[:, 512 + 2 * ff :].astype(F32).T
    for level in range(4, levels):
        total.step(level)
    layer.small = named["slabs"].at[levels]
    layer.small_out(net.head)
    last[6]()
    for i, out in enumerate((layer.o_q, layer.o_k, layer.o_v)):
        out[...] = fin[:, i * 128 : (i + 1) * 128].astype(F32)
    net.drain()


def layer_call(groups, heads, args):
    series = args[0]
    rows, steps = series.shape
    patch, width = args[7].shape
    length = steps // patch
    tokens = rows * length
    part = args[9].shape[1]
    ff = args[14].shape[1]
    table_rows, table_heads = args[13].shape
    total = heads * (4 * part + 3 * ff)
    bits = groups.bit_length() - 1
    levels = bits + heads.bit_length() - 1
    scratch = dict(
        pm=((length, steps), F32), fold=((16, steps), BF16), ptile=((steps, width), BF16),
        htile=((width, steps), BF16), splitb=((rows, 128), F32), normed=((rows, steps), F32),
        normed_low=((rows, steps), F32), dout_low=((rows, steps), F32), output=((rows, steps), F32),
        d_normed=((rows, steps), F32), p8t=((16, tokens), BF16), d8t=((16, tokens), BF16),
        embedded=((tokens, width), F32), s_attn=((tokens, 1), F32), attn_in=((tokens, width), BF16),
        qkv=((tokens, heads * 3 * part), BF16), tab=((heads, table_rows, 128), F32),
        bias=((heads, length, 128), F32), probs=((heads, tokens, 128), F32),
        ctx=((tokens, heads * part), BF16), ff_in=((tokens, width), BF16),
        inner=((tokens, heads * ff), BF16), act=((TILE, heads * ff), BF16),
        slope=((TILE, heads * ff), BF16), final_in=((tokens, width), BF16),
        d_end_low=((tokens, width), BF16), dgu=((tokens, heads * 2 * ff), BF16),
        d_mid=((tokens, width), F32), d_mid_low=((tokens, width), BF16),
        d_ctx=((tokens, heads * part), BF16), dsum=((heads, length, 128), F32),
        g_attn=((8, width), F32), g_ff=((8, width), F32),
        g_final=((8, width), F32), g_bias=((8, width), F32), tgr=((table_rows, 128), F32),
        left_t=((width, tokens), BF16), right_t=((width, tokens), BF16),
        wq=((width, heads * 3 * part), BF16), wo=((width, heads * part), BF16),
        wg=((width, heads * 2 * ff), BF16), wd=((width, heads * ff), BF16),
        own=((width // 2, total), F32), snd0=((width // 2, total), BF16),
        rcv0=((width // 2, total), BF16), snd1=((width // 4, total), BF16),
        rcv1=((width // 4, total), BF16), snd2=((width // 8, total), BF16),
        rcv2=((width // 8, total), BF16), sndz=((width // 8, total), BF16),
        rcvz=((heads - 1, width // 8, total // heads), BF16),
        slabs=((levels + 1, 32, width), F32), inbox=((levels, 32, width), F32),
    )
    if bits > 3:
        scratch["extra"] = ((bits - 3, width // 8, total), BF16)
    copies = 4 * 2 * (heads - 1 + 3) + heads - 1 + 4 * (10 + heads - 1 + 2 * (bits - 3)) + levels
    outs = [
        (rows, steps), (rows, steps), (1, width), (1, width), (1, width), (patch, width), (1, width),
        (width, part), (width, part), (width, part), (part, width), (table_rows, table_heads),
        (width, ff), (width, ff), (ff, width), (width, patch), (1, patch),
    ]
    names = list(INPUTS + OUTPUTS) + list(scratch) + ["send_sems", "recv_sems"]
    vmem = pl.BlockSpec(memory_space=pltpu.VMEM)
    return pl.pallas_call(
        functools.partial(layer_kernel, groups, heads, names),
        out_shape=[jax.ShapeDtypeStruct(shape, F32) for shape in outs],
        in_specs=[vmem] * len(INPUTS),
        out_specs=[vmem] * len(OUTPUTS),
        scratch_shapes=[pltpu.VMEM(*v) for v in scratch.values()]
        + [pltpu.SemaphoreType.DMA((copies,)), pltpu.SemaphoreType.DMA((copies,))],
        compiler_params=pltpu.CompilerParams(
            collective_id=0, has_side_effects=True, vmem_limit_bytes=61 * 1024 * 1024
        ),
    )(*args)


def solution(mesh):
    groups, heads = mesh.shape["dp"], mesh.shape["head"]

    def local(*args):
        args = list(args)
        for i in (2, 4, 5, 6, 8, 18):
            args[i] = args[i].reshape(1, -1)
        outs = list(layer_call(groups, heads, args))
        for i in (2, 3, 4, 6, 16):
            outs[i] = outs[i].reshape(-1)
        return tuple(outs)

    both = P(("dp", "head"), None)
    by_column, by_row = P(None, "head"), P("head", None)
    return jax.shard_map(
        local,
        mesh=mesh,
        in_specs=(both, both, P("dp"), both) + (P(),) * 5 + (by_column,) * 3
        + (by_row, by_column, by_column, by_column, by_row, P(), P()),
        out_specs=(both, both) + (P(),) * 5 + (by_column,) * 3
        + (by_row, by_column, by_column, by_column, by_row, P(), P()),
        check_vma=False,
    )
```

```python
import functools
import math

import jax
import jax.numpy as jnp
from jax import lax
from jax.experimental import pallas as pl
from jax.experimental.pallas import tpu as pltpu
from jax.sharding import PartitionSpec as P

F32 = jnp.float32
BF16 = jnp.bfloat16
EPS = 1e-06
TILE = 256
MAX_DIST = 128


def bucket_cuts(buckets, length):
    half_count = buckets // 2
    exact_count = half_count // 2
    ids = []
    for distance in range(length):
        if distance < exact_count:
            ids.append(distance)
        else:
            ids.append(
                min(
                    half_count - 1,
                    exact_count
                    + int(
                        math.log(distance / exact_count)
                        / math.log(MAX_DIST / exact_count)
                        * (half_count - exact_count)
                    ),
                )
            )
    cuts = []
    for distance in range(1, length):
        cuts += [distance] * (ids[distance] - ids[distance - 1])
    return cuts, ids[-1]


def nt(left, right):
    return lax.dot_general(left, right, (((1,), (1,)), ((), ())), preferred_element_type=F32)


def nn(left, right):
    return jnp.dot(left, right, preferred_element_type=F32)


def tn(left, right):
    return lax.dot_general(left, right, (((0,), (0,)), ((), ())), preferred_element_type=F32)


def iota(shape, dim):
    return lax.broadcasted_iota(jnp.int32, shape, dim)


def fold8(values):
    return jnp.sum(values.reshape(values.shape[0] // 8, 8, values.shape[1]), axis=0)


def row_scale(values):
    return lax.rsqrt(jnp.mean(values * values, axis=-1, keepdims=True) + EPS)


def norm_back(grad_out, unit_rows, scale, gain_row):
    d_unit = grad_out * gain_row
    spread = jnp.mean(d_unit * unit_rows, axis=-1, keepdims=True)
    return scale * (d_unit - unit_rows * spread), fold8(grad_out * unit_rows)


class Layer:
    def __init__(self, **refs):
        self.__dict__.update(refs)
        self.rows = {}

    def prepare(self, head_index):
        rows, steps = self.series.shape
        half = steps // 2
        length = self.pm.shape[0]
        patch = steps // length
        split_row = self.split[...].astype(F32)
        pick = iota((rows, split_row.shape[1]), 1) == (
            iota((rows, split_row.shape[1]), 0) + head_index * rows
        )
        split_col = jnp.sum(jnp.where(pick, split_row, 0.0), axis=1, keepdims=True)
        self.splitb[...] = jnp.broadcast_to(split_col, self.splitb.shape)
        obs = self.observed[...].astype(F32)
        series = self.series[...]
        low_half = iota((rows, steps), 1) < half

        def halves(values):
            return [
                jnp.sum(values[:, :half], axis=1, keepdims=True),
                jnp.sum(values[:, half:], axis=1, keepdims=True),
            ]

        def combine(sums):
            both = sums[0] + sums[1]
            return [split_col * one + (1.0 - split_col) * both for one in sums]

        def spread(pair):
            return jnp.where(low_half, pair[0], pair[1])

        self.halves, self.combine, self.spread = halves, combine, spread
        self.counts = combine(halves(obs))
        item_mean = [a / b for a, b in zip(combine(halves(obs * series)), self.counts)]
        centred = series - spread(item_mean)
        item_var = [a / b for a, b in zip(combine(halves(obs * centred * centred)), self.counts)]
        self.std = [jnp.sqrt(v + 1e-05) for v in item_var]
        std_full = spread(self.std)
        self.std_full, self.mean_full = std_full, spread(item_mean)
        normed = obs * centred / std_full
        self.normed[...] = normed
        self.normed_low[...] = normed.astype(BF16).astype(F32)
        self.dout_low[...] = (self.cot[...] * std_full).astype(BF16).astype(F32)
        self.pm[...] = (iota(self.pm.shape, 1) // patch == iota(self.pm.shape, 0)).astype(F32)
        fold = (iota(self.fold.shape, 1) % patch == iota(self.fold.shape, 0)).astype(BF16)
        self.fold[...] = fold
        pw = self.patch_w[...].astype(F32)
        for name, source in zip(("g1", "g2", "g3", "pb"), self.vectors):
            self.rows[name] = jnp.concatenate(
                [source[i : i + 1, :].astype(F32) for i in range(source.shape[0])], axis=1
            )
        self.ptile[...] = jnp.broadcast_to(
            pw[None], (self.ptile.shape[0] // patch, patch, pw.shape[1])
        ).reshape(self.ptile.shape).astype(BF16)
        self.htile[...] = tn(self.head_w[...], fold[:patch]).astype(BF16)
        hb = jnp.broadcast_to(self.head_b[...], (16, patch))
        self.hbias = nn(hb, fold[:patch])[0:1]

    def spread_rows(self, source, tile):
        rows_tile = TILE // self.pm.shape[0]
        mask = self.pm[...]
        pieces = [
            (source[pl.ds(tile * rows_tile + r, 1), :] * mask).astype(BF16)
            for r in range(rows_tile)
        ]
        return jnp.concatenate(pieces, axis=0)

    def gather_rows(self, target, tile, values, extra=None):
        length = self.pm.shape[0]
        mask = self.pm[...]
        for r in range(TILE // length):
            part = jnp.sum(values[r * length : (r + 1) * length] * mask, axis=0, keepdims=True)
            if extra is not None:
                part = part + extra
            target[pl.ds(tile * (TILE // length) + r, 1), :] = part

    def embed(self, tile):
        at = pl.ds(pl.multiple_of(tile * TILE, TILE), TILE)
        spread = self.spread_rows(self.normed_low, tile)
        self.p8t[:, at] = nt(self.fold[...], spread).astype(BF16)
        embedded = nn(spread, self.ptile[...]) + self.rows["pb"]
        self.embedded[at, :] = embedded
        scale = row_scale(embedded)
        self.s_attn[at, :] = scale
        self.attn_in[at, :] = (embedded * scale * self.rows["g1"]).astype(BF16)

    def buckets(self):
        length = self.pm.shape[0]
        lanes = 2 * length
        key = iota((length, lanes), 0)
        query = iota((length, lanes), 1) % length
        offset = key - query
        distance = jnp.abs(offset)
        table = self.tab.shape[1]
        cuts, top = bucket_cuts(table, length)
        ids = jnp.where(offset > 0, table // 2, 0)
        for cut in cuts:
            ids = ids + (distance >= cut).astype(jnp.int32)
        used = list(range(top + 1)) + list(range(table // 2, table // 2 + top + 1))
        return ids, used

    def own_table(self):
        table = self.table[...].astype(BF16)
        pick = (iota((2, 128), 1) // 64 == iota((2, 128), 0)).astype(BF16)
        self.tab[0] = tn(table, pick)

    def offsets(self, slot):
        ids, used = self.buckets()
        total = jnp.zeros(ids.shape, F32)
        for b in used:
            total = jnp.where(ids == b, self.tab[slot, b : b + 1, :], total)
        self.bias[slot] = total

    def head_masks(self):
        lane = iota((1, 128), 1)
        return (lane < 64).astype(BF16), (lane >= 64).astype(BF16)

    def attend(self, tile):
        at = pl.ds(pl.multiple_of(tile * TILE, TILE), TILE)
        length = self.pm.shape[0]
        rows_tile = TILE // length
        even, odd = self.head_masks()
        half = length // 2
        shape = (length, 2 * length)
        block = (iota(shape, 0) // half != (iota(shape, 1) % length) // half).astype(F32) * -1e30
        splits = [self.splitb[pl.ds(tile * rows_tile + r, 1), :] * block for r in range(rows_tile)]
        width = self.ctx.shape[1]
        projected = []
        for i in range(3):
            part = nn(self.attn_in[at, :], self.wq[:, i * width : (i + 1) * width]).astype(BF16)
            self.qkv[at, i * width : (i + 1) * width] = part
            projected.append(part)
        items = [(s, r) for s in range(self.slots) for r in range(rows_tile)]

        def piece(s, r, i):
            return projected[i][r * length : (r + 1) * length, s * 128 : (s + 1) * 128]

        scores = []
        for s, r in items:
            query = piece(s, r, 0)
            both = jnp.concatenate([query * even, query * odd], axis=0)
            scores.append(nt(piece(s, r, 1), both))
        turned = []
        for (s, r), score in zip(items, scores):
            score = score + (self.bias[s] + splits[r])
            top = jnp.max(score, axis=0, keepdims=True)
            raised = jnp.exp(score - top)
            probs = raised * (1.0 / jnp.sum(raised, axis=0, keepdims=True))
            self.probs[
                s, pl.ds(pl.multiple_of(tile * TILE + r * length, length), length), :
            ] = probs.astype(self.probs.dtype)
            turned.append(probs.astype(BF16))
        turned = [probs.T for probs in turned]
        mixed = [nn(probs, piece(s, r, 2)) for probs, (s, r) in zip(turned, items)]
        low_lanes = iota((1, 128), 1) < 64
        for s in range(self.slots):
            self.ctx[at, s * 128 : (s + 1) * 128] = jnp.concatenate(
                [
                    jnp.where(low_lanes, m[:length], m[length:]).astype(BF16)
                    for m in mixed[s * rows_tile : (s + 1) * rows_tile]
                ],
                axis=0,
            )

    def middle_gate(self, tile):
        at = pl.ds(pl.multiple_of(tile * TILE, TILE), TILE)
        hidden_mid = self.embedded[at, :] + nt(self.ctx[at, :], self.wo[...])
        self.hidden_mid[at, :] = hidden_mid
        ff_in = (hidden_mid * row_scale(hidden_mid) * self.rows["g2"]).astype(BF16)
        self.ff_in[at, :] = ff_in
        total = self.inner.shape[1]
        block = 256
        c = math.sqrt(2.0 / math.pi)
        for first in range(0, total, block):
            cols = slice(first, first + block)
            gate = nn(ff_in, self.wg[:, first : first + block])
            up = nn(ff_in, self.wg[:, total + first : total + first + block])
            square = gate * gate
            t = jnp.tanh(gate * (c + (c * 0.044715) * square))
            plus = 0.5 * (1.0 + t)
            act = gate * plus
            slope = plus + (0.5 * gate) * (1.0 - t * t) * (c + (3.0 * c * 0.044715) * square)
            self.inner[at, cols] = (act * up).astype(BF16)
            self.act[at, cols] = act.astype(BF16)
            self.slope[at, cols] = (up * slope).astype(BF16)

    def middle_down(self, tile):
        at = pl.ds(pl.multiple_of(tile * TILE, TILE), TILE)
        hidden_end = self.hidden_mid[at, :] + nt(self.inner[at, :], self.wd[...])
        final_scale = row_scale(hidden_end)
        final_unit = hidden_end * final_scale
        gain_final = self.rows["g3"]
        final_in = (final_unit * gain_final).astype(BF16)
        self.final_in[at, :] = final_in
        self.gather_rows(self.output, tile, nn(final_in, self.htile[...]), self.hbias)
        d_spread = self.spread_rows(self.dout_low, tile)
        self.d8t[:, at] = nt(self.fold[...], d_spread).astype(BF16)
        d_final = nt(d_spread, self.htile[...])
        d_end, gain_part = norm_back(d_final, final_unit, final_scale, gain_final)
        self.g_final[...] += gain_part
        self.d_end_low[at, :] = d_end.astype(BF16)
        self.d_mid[at, :] = d_end

    def middle_back(self, tile):
        at = pl.ds(pl.multiple_of(tile * TILE, TILE), TILE)
        d_low = self.d_end_low[at, :]
        total = self.inner.shape[1]
        block = 256
        for first in range(0, total, block):
            cols = slice(first, first + block)
            d_inner = nn(d_low, self.wd[:, cols])
            d_gate = (d_inner * self.slope[at, cols].astype(F32)).astype(BF16)
            d_up = (d_inner * self.act[at, cols].astype(F32)).astype(BF16)
            self.dgu[at, cols] = d_gate
            self.dgu[at, total + first : total + first + block] = d_up
        d_in = nt(self.dgu[at, :], self.wg[...])
        hidden_mid = self.hidden_mid[at, :]
        ff_scale = row_scale(hidden_mid)
        d_norm, gain_part = norm_back(d_in, hidden_mid * ff_scale, ff_scale, self.rows["g2"])
        self.g_ff[...] += gain_part
        d_mid = self.d_mid[at, :] + d_norm
        self.d_mid[at, :] = d_mid
        d_mid_low = d_mid.astype(BF16)
        self.d_mid_low[at, :] = d_mid_low
        self.d_ctx[at, :] = nn(d_mid_low, self.wo[...]).astype(BF16)

    def attend_back(self, tile):
        width = self.ctx.shape[1]
        length = self.pm.shape[0]
        rows_tile = TILE // length
        even, odd = self.head_masks()
        items = [(s, r) for s in range(self.slots) for r in range(rows_tile)]
        rows = [
            pl.ds(pl.multiple_of(tile * TILE + r * length, length), length)
            for r in range(rows_tile)
        ]

        def piece(s, r, i):
            return self.qkv[rows[r], i * width + s * 128 : i * width + (s + 1) * 128]

        d_both = []
        for s, r in items:
            d_ctx = self.d_ctx[rows[r], s * 128 : (s + 1) * 128]
            d_both.append(jnp.concatenate([d_ctx * even, d_ctx * odd], axis=0))
        d_probs = [nt(piece(s, r, 2), both) for (s, r), both in zip(items, d_both)]
        probs = [self.probs[s, rows[r], :] for s, r in items]
        d_value = [nn(p.astype(BF16), both) for p, both in zip(probs, d_both)]
        d_scores = []
        for p, dp in zip(probs, d_probs):
            p = p.astype(F32)
            dots = jnp.sum(p * dp, axis=0, keepdims=True)
            d_scores.append((p * (dp - dots)).astype(BF16))
        turned = [d.T for d in d_scores]
        d_key = []
        for (s, r), d in zip(items, d_scores):
            query = piece(s, r, 0)
            d_key.append(nn(d, jnp.concatenate([query * even, query * odd], axis=0)))
        mixed = [nn(d, piece(s, r, 1)) for (s, r), d in zip(items, turned)]
        low_lanes = iota((1, 128), 1) < 64
        for n, (s, r) in enumerate(items):
            d_query = jnp.where(low_lanes, mixed[n][:length], mixed[n][length:])
            for i, grad in enumerate((d_query, d_key[n], d_value[n])):
                cols = slice(i * width + s * 128, i * width + (s + 1) * 128)
                self.dqkv[rows[r], cols] = grad.astype(BF16)
        for s in range(self.slots):
            total = self.dsum[s]
            for d in d_scores[s * rows_tile : (s + 1) * rows_tile]:
                total = total + d.astype(F32)
            self.dsum[s] = total

    def embed_back(self, tile):
        at = pl.ds(pl.multiple_of(tile * TILE, TILE), TILE)
        d_in = nt(self.dqkv[at, :], self.wq[...])
        scale = self.s_attn[at, :]
        d_norm, gain_part = norm_back(
            d_in, self.embedded[at, :] * scale, scale, self.rows["g1"]
        )
        self.g_attn[...] += gain_part
        d_embedded = (self.d_mid[at, :] + d_norm).astype(BF16)
        self.d_emb[at, :] = d_embedded
        self.g_bias[...] += fold8(d_embedded.astype(F32))
        self.gather_rows(self.d_normed, tile, nt(d_embedded, self.ptile[...]))

    def finish(self):
        obs = self.observed[...].astype(F32)
        cot = self.cot[...]
        output = self.output[...]
        std_full, mean_full = self.std_full, self.mean_full
        self.rebuilt[...] = output * std_full + mean_full
        d_normed = self.d_normed[...]
        std_grad = [
            a - b / c
            for a, b, c in zip(
                self.halves(cot * output), self.halves(d_normed * self.normed[...]), self.std
            )
        ]
        var_weight = self.combine(
            [g / (2.0 * s) / n for g, s, n in zip(std_grad, self.std, self.counts)]
        )
        centred = self.series[...] - mean_full
        d_centred = d_normed * obs / std_full + 2.0 * obs * centred * self.spread(var_weight)
        mean_grad = [a - b for a, b in zip(self.halves(cot), self.halves(d_centred))]
        mean_weight = self.combine([g / n for g, n in zip(mean_grad, self.counts)])
        self.series_grad[...] = d_centred + obs * self.spread(mean_weight)

    def head_grad(self):
        self.small[16:24, :] = nn(self.d8t[...], self.final_in[...])[0:8]

    def small_grads(self, head_index):
        small = self.small
        heads = self.slots
        zero = jnp.zeros((4, self.embedded.shape[1]), F32)
        small[0:8, :] = jnp.concatenate(
            [jnp.sum(r[...], axis=0, keepdims=True) for r in (self.g_attn, self.g_ff, self.g_final, self.g_bias)]
            + [zero],
            axis=0,
        )
        small[8:16, :] = nn(self.p8t[...], self.d_emb[...])[0:8]
        lane = iota((8, 128), 1)
        groups = self.tab.shape[1] // 8
        pieces = [jnp.zeros((8, 128), F32) for _ in range(groups)]
        pieces[0] = jnp.where(
            lane == 2 * heads, jnp.sum(self.d8t[0:8, :].astype(F32), axis=1, keepdims=True), 0.0
        )
        ids, used = self.buckets()
        for s in range(self.slots):
            dsum = self.dsum[s]
            owner = lax.rem(head_index + s, heads)
            for b in range(self.tab.shape[1]):
                if b in used:
                    self.tgr[b : b + 1, :] = jnp.sum(
                        jnp.where(ids == b, dsum, 0.0), axis=0, keepdims=True
                    )
                else:
                    self.tgr[b : b + 1, :] = jnp.zeros((1, 128), F32)
            for g in range(groups):
                rows = self.tgr[8 * g : 8 * g + 8, :]
                for which in range(2):
                    inside = (lane < 64) if which == 0 else (lane >= 64)
                    column = jnp.sum(jnp.where(inside, rows, 0.0), axis=1, keepdims=True)
                    pieces[g] = pieces[g] + jnp.where(lane == 2 * owner + which, column, 0.0)
        small[24:32, :] = jnp.concatenate(pieces, axis=1)

    def clear(self):
        for ref in (self.g_attn, self.g_ff, self.g_final, self.g_bias):
            ref[...] = jnp.zeros(ref.shape, F32)
        self.dsum[...] = jnp.zeros(self.dsum.shape, F32)


MESH = pl.DeviceIdType.MESH


class Net:
    def __init__(self, groups, heads, send_sems, recv_sems):
        self.dp, self.head = lax.axis_index("dp"), lax.axis_index("head")
        self.bits = groups.bit_length() - 1
        self.heads = heads
        self.send_sems, self.recv_sems = send_sems, recv_sems
        self.used = 0
        self.sent = []

    def bit(self, which):
        return (self.dp // (1 << which)) % 2

    def across(self, which):
        step = 1 << which
        return (self.dp + (1 - 2 * self.bit(which)) * step, self.head)

    def beside(self, hops):
        return (self.dp, (self.head + hops) % self.heads)

    def beside_bit(self, which):
        step = 1 << which
        mine = (self.head // step) % 2
        return (self.dp, self.head + (1 - 2 * mine) * step)

    def greet_start(self):
        barrier = pltpu.get_barrier_semaphore()
        partners = [self.across(b) for b in range(self.bits)]
        partners += [self.beside(t) for t in range(1, self.heads)]
        for partner in partners:
            pl.semaphore_signal(barrier, inc=1, device_id=partner, device_id_type=MESH)

    def greet_end(self):
        pl.semaphore_wait(pltpu.get_barrier_semaphore(), self.bits + self.heads - 1)

    def claim(self):
        self.used += 1
        return self.used - 1

    def copy(self, index, src, dst, device):
        return pltpu.make_async_remote_copy(
            src_ref=src,
            dst_ref=dst,
            send_sem=self.send_sems.at[index],
            recv_sem=self.recv_sems.at[index],
            device_id=device,
            device_id_type=MESH,
        )

    def send(self, index, src, dst, device):
        copy = self.copy(index, src, dst, device)
        copy.start()
        self.sent.append(copy)

    def arrived(self, index, dst, device):
        self.copy(index, dst, dst, device).wait_recv()

    def drain(self):
        for copy in self.sent:
            copy.wait_send()
        self.sent = []


def rows_at(start, count, unit):
    return pl.ds(pl.multiple_of(start, unit), count)


class Gather:
    ORDERS = ((1, 2, 0), (2, 1, 0))

    def __init__(self, net, ref, parts):
        self.net, self.ref, self.parts = net, ref, parts
        self.heads = net.heads
        self.unit = ref.shape[0] // 16
        self.ids = {}

    def id(self, *key):
        if key not in self.ids:
            self.ids[key] = self.net.claim()
        return self.ids[key]

    def block(self, half):
        bits = [self.net.bit(b) for b in self.ORDERS[half]]
        return bits[0] + 2 * bits[1] + 4 * bits[2]

    def span(self, half, level, mine=True):
        size = 1 << level
        first = self.block(half) // size
        if not mine:
            first = first + 1 - 2 * (first % 2)
        return rows_at((half * 8 + first * size) * self.unit, size * self.unit, self.unit)

    def start(self):
        net = self.net
        for half in range(2):
            rows = self.span(half, 0)
            for t in range(1, self.heads):
                slot = self.heads - t
                for first, width in self.parts:
                    net.send(
                        self.id(half, "z", t, first),
                        self.ref.at[rows, first : first + width],
                        self.ref.at[rows, first + slot * width : first + (slot + 1) * width],
                        net.beside(t),
                    )

    def others(self, first, width):
        return slice(first + width, first + self.heads * width)

    def step(self, level):
        net = self.net
        for half in range(2):
            for first, width in self.parts:
                if level == 0:
                    for t in range(1, self.heads):
                        slot = self.heads - t
                        net.arrived(
                            self.id(half, "z", t, first),
                            self.ref.at[
                                self.span(half, 0), first + slot * width : first + (slot + 1) * width
                            ],
                            net.beside(t),
                        )
                else:
                    net.arrived(
                        self.id(half, "s", level - 1, first),
                        self.ref.at[self.span(half, level - 1, mine=False), self.others(first, width)],
                        net.across(self.ORDERS[half][level - 1]),
                    )
            if level < 3:
                rows = self.span(half, level)
                for first, width in self.parts:
                    place = self.ref.at[rows, self.others(first, width)]
                    net.send(
                        self.id(half, "s", level, first),
                        place,
                        place,
                        net.across(self.ORDERS[half][level]),
                    )


class Reduce:
    ORDERS = ((1, 2), (2, 1))

    def __init__(self, net, refs, parts):
        self.net = net
        self.heads = net.heads
        self.parts = parts
        last, width = parts[-1]
        self.columns = slice(parts[0][0], last + self.heads * width)
        (
            self.own, self.snd0, self.rcv0, self.snd1, self.rcv1,
            self.snd2, self.rcv2, self.sndz, self.rcvz, self.fin,
        ) = refs
        self.ids = {}

    def id(self, name):
        if name not in self.ids:
            self.ids[name] = self.net.claim()
        return self.ids[name]

    def slots(self, part, s):
        first, width = part
        return slice(first + s * width, first + (s + 1) * width)

    def fin_part(self, part):
        first, width = part
        return slice(first // self.heads, first // self.heads + width)

    @property
    def fin_columns(self):
        return slice(self.columns.start // self.heads, self.columns.stop // self.heads)

    def produce(self, left_t, right, block=512):
        net = self.net
        count = self.own.shape[0]
        core = net.bit(0)
        wide = self.columns.stop - self.columns.start
        for c in range(0, wide, block):
            cols = slice(self.columns.start + c, self.columns.start + c + block)
            self.snd0[:, cols] = nn(
                left_t[rows_at((1 - core) * count, count, count), :], right[:, c : c + block]
            ).astype(BF16)
        net.send(
            self.id("r0"), self.snd0.at[:, self.columns], self.rcv0.at[:, self.columns], net.across(0)
        )
        for c in range(0, wide, block):
            cols = slice(self.columns.start + c, self.columns.start + c + block)
            self.own[:, cols] = nn(
                left_t[rows_at(core * count, count, count), :], right[:, c : c + block]
            ).astype(self.own.dtype)

    def halving(self, level):
        net, cols = self.net, self.columns
        source = (self.rcv0, self.rcv1, self.rcv2)[level]
        count = self.own.shape[0] // 2 >> level
        if level == 0:
            net.arrived(self.id("r0"), self.rcv0.at[:, cols], net.across(0))
        for half in range(2):
            first = half * count
            if level > 0:
                net.arrived(
                    self.id(f"r{level}{half}"),
                    source.at[first : first + count, cols],
                    net.across(self.ORDERS[half][level - 1]),
                )
            at = self.kept(half, level)
            if level < 2:
                bit = net.bit(self.ORDERS[half][level])
                away = (1 - bit) * (count // 2)
                send, target = ((self.snd1, self.rcv1), (self.snd2, self.rcv2))[level]
                place = slice(half * (count // 2), (half + 1) * (count // 2))
                send[place, cols] = (
                    self.own[rows_at(at + away, count // 2, 32), cols].astype(F32)
                    + source[rows_at(first + away, count // 2, 32), cols].astype(F32)
                ).astype(BF16)
                net.send(
                    self.id(f"r{level + 1}{half}"),
                    send.at[place, cols],
                    target.at[place, cols],
                    net.across(self.ORDERS[half][level]),
                )
        for half in range(2):
            at = self.kept(half, level)
            first = half * count
            if level < 2:
                bit = net.bit(self.ORDERS[half][level])
                stay = bit * (count // 2)
                rows = rows_at(at + stay, count // 2, 32)
                self.own[rows, cols] = (
                    self.own[rows, cols].astype(F32)
                    + source[rows_at(first + stay, count // 2, 32), cols].astype(F32)
                ).astype(self.own.dtype)
            else:
                rows = rows_at(at, count, 32)
                total = self.own[rows, cols].astype(F32) + source[
                    first : first + count, cols
                ].astype(F32)
                self.own[rows, cols] = total.astype(self.own.dtype)
                if net.bits <= 3:
                    self.sndz[first : first + count, cols] = total.astype(BF16)

    def kept(self, half, level):
        count = self.own.shape[0] // 2
        start = half * count
        for step in range(level):
            count = count // 2
            start = start + self.net.bit(self.ORDERS[half][step]) * count
        return start

    def groups(self):
        net, cols = self.net, self.columns
        count = self.sndz.shape[0] // 2
        for bit in range(3, net.bits):
            inbox = self.extra.at[bit - 3]
            key = f"g{bit}"
            for half in range(2):
                rows = rows_at(self.kept(half, 2), count, 32)
                self.sndz[half * count : (half + 1) * count, cols] = self.own[rows, cols].astype(
                    BF16
                )
            copy = net.copy(
                self.id(key), self.sndz.at[:, cols], inbox.at[:, cols], net.across(bit)
            )
            copy.start()
            copy.wait()
            for half in range(2):
                rows = rows_at(self.kept(half, 2), count, 32)
                place = slice(half * count, (half + 1) * count)
                self.own[rows, cols] = (
                    self.sndz[place, cols].astype(F32) + inbox[place, cols].astype(F32)
                ).astype(self.own.dtype)
        if net.bits > 3:
            for half in range(2):
                rows = rows_at(self.kept(half, 2), count, 32)
                self.sndz[half * count : (half + 1) * count, cols] = self.own[rows, cols].astype(
                    BF16
                )

    def owners(self):
        net = self.net
        for s in range(1, self.heads):
            for part in self.parts:
                net.send(
                    self.id(f"z{s}{part[0]}"),
                    self.sndz.at[:, self.slots(part, s)],
                    self.rcvz.at[s - 1, :, self.fin_part(part)],
                    net.beside(s),
                )

    def place(self, half, level, mine=True):
        net = self.net
        quarter = self.fin.shape[0] // 4
        count = quarter // 4
        start = net.bit(0) * 2 * quarter + half * quarter
        order = self.ORDERS[half]
        if level == 0:
            inner = net.bit(order[1]) if mine else 1 - net.bit(order[1])
            start = start + net.bit(order[0]) * 2 * count + inner * count
            return rows_at(start, count, count)
        outer = net.bit(order[0]) if mine else 1 - net.bit(order[0])
        return rows_at(start + outer * 2 * count, 2 * count, count)

    def owned(self):
        net = self.net
        fin = self.fin_columns
        count = self.sndz.shape[0] // 2
        for s in range(1, self.heads):
            for part in self.parts:
                net.arrived(
                    self.id(f"z{s}{part[0]}"),
                    self.rcvz.at[s - 1, :, self.fin_part(part)],
                    net.beside(s),
                )
        for half in range(2):
            rows = self.place(half, 0)
            for part in self.parts:
                total = self.own[
                    rows_at(self.kept(half, 2), count, 32), self.slots(part, 0)
                ].astype(F32)
                for s in range(1, self.heads):
                    total = total + self.rcvz[
                        s - 1, half * count : (half + 1) * count, self.fin_part(part)
                    ].astype(F32)
                self.fin[rows, self.fin_part(part)] = total.astype(BF16)
            net.send(
                self.id(f"f0{half}"),
                self.fin.at[rows, fin],
                self.fin.at[rows, fin],
                net.across(self.ORDERS[half][1]),
            )

    def spread(self, level):
        net, fin = self.net, self.fin_columns
        if level < 2:
            for half in range(2):
                net.arrived(
                    self.id(f"f{level}{half}"),
                    self.fin.at[self.place(half, level, mine=False), fin],
                    net.across(self.ORDERS[half][1 - level]),
                )
                if level == 0:
                    rows = self.place(half, 1)
                    net.send(
                        self.id(f"f1{half}"),
                        self.fin.at[rows, fin],
                        self.fin.at[rows, fin],
                        net.across(self.ORDERS[half][0]),
                    )
        half_rows = self.fin.shape[0] // 2
        core = net.bit(0)
        if level == 1:
            rows = rows_at(core * half_rows, half_rows, half_rows)
            net.send(
                self.id("f2"), self.fin.at[rows, fin], self.fin.at[rows, fin], net.across(0)
            )
        if level == 2:
            rows = rows_at((1 - core) * half_rows, half_rows, half_rows)
            net.arrived(self.id("f2"), self.fin.at[rows, fin], net.across(0))

    def steps(self):
        return [
            lambda: self.halving(0),
            lambda: self.halving(1),
            lambda: (self.halving(2), self.groups(), self.owners()),
            self.owned,
            lambda: self.spread(0),
            lambda: self.spread(1),
            lambda: self.spread(2),
        ]


class Total:
    def __init__(self, net, slabs, inbox):
        self.net, self.slabs, self.inbox = net, slabs, inbox
        self.partners = [net.across(b) for b in range(net.bits)]
        self.partners += [net.beside_bit(b) for b in range(net.heads.bit_length() - 1)]
        self.ids = [net.claim() for _ in self.partners]

    def start(self, level):
        self.net.send(
            self.ids[level], self.slabs.at[level], self.inbox.at[level], self.partners[level]
        )

    def step(self, level):
        self.net.arrived(self.ids[level], self.inbox.at[level], self.partners[level])
        self.slabs[level + 1] = self.slabs[level] + self.inbox[level]
        if level + 1 < len(self.partners):
            self.start(level + 1)


def loop(count, body):
    def once(i, carry):
        body(i)
        return carry

    lax.fori_loop(0, count, once, 0)


INPUTS = (
    "series", "observed", "split", "cot", "gain_attn", "gain_ff", "gain_final", "patch_w", "patch_b",
    "wq_in", "wk_in", "wv_in", "wo_in", "table", "wg_in", "wu_in", "wd_in", "head_w", "head_b",
)
OUTPUTS = ("rebuilt", "series_grad", "sums", "fin_out")
SHARED = ("own", "snd0", "rcv0", "snd1", "rcv1", "snd2", "rcv2", "sndz", "rcvz", "fin")


def layer_kernel(groups, heads, names, *refs):
    named = dict(zip(names, refs))
    dgu, weights = named["dgu"], named["weights"]
    starts = {}
    first = 0
    for key, width in zip("qkvogud", [named["wq_in"].shape[1]] * 4 + [named["wg_in"].shape[1]] * 3):
        starts[key] = (first, width)
        first += heads * width
    parts = {keys: [starts[key] for key in keys] for keys in ("qkv", "o", "gu", "g", "u", "d")}
    named["wq"] = weights.at[:, 0 : starts["o"][0]]
    named["wo"] = weights.at[:, starts["o"][0] : starts["g"][0]]
    named["wg"] = weights.at[:, starts["g"][0] : starts["d"][0]]
    named["wd"] = weights.at[:, starts["d"][0] : first]
    named["dqkv"] = dgu.at[:, 0 : starts["o"][0]]
    named["d_emb"] = named["ff_in"]
    named["d_mid_low"] = named["final_in"]
    named["small"] = named["slabs"].at[0]
    layer = Layer(slots=heads, **named)
    layer.vectors = (layer.gain_attn, layer.gain_ff, layer.gain_final, layer.patch_b)
    tiles = layer.embedded.shape[0] // TILE
    net = Net(groups, heads, named["send_sems"], named["recv_sems"])

    def own(key, ref, turn=False):
        first, width = starts[key]
        weights[:, first : first + width] = ref[...].T if turn else ref[...]

    net.greet_start()
    own("q", layer.wq_in)
    own("k", layer.wk_in)
    own("v", layer.wv_in)
    layer.own_table()
    net.greet_end()
    gather = {keys: Gather(net, weights, parts[keys]) for keys in ("qkv", "o", "gu", "d")}
    gather["qkv"].start()
    table_ids = [net.claim() for _ in range(heads - 1)]
    for t in range(1, heads):
        net.send(table_ids[t - 1], layer.tab.at[0], layer.tab.at[heads - t], net.beside(t))
    own("o", layer.wo_in, turn=True)
    own("g", layer.wg_in)
    own("u", layer.wu_in)
    own("d", layer.wd_in, turn=True)
    layer.clear()
    layer.prepare(net.head)
    loop(tiles, layer.embed)
    gather["qkv"].step(0)
    gather["o"].start()
    gather["gu"].start()
    for t in range(1, heads):
        net.arrived(table_ids[t - 1], layer.tab.at[heads - t], net.beside(t))
    loop(heads, layer.offsets)
    gather["qkv"].step(1)
    gather["o"].step(0)
    gather["qkv"].step(2)
    gather["gu"].step(0)
    gather["d"].start()
    gather["o"].step(1)
    gather["qkv"].step(3)
    loop(tiles // 2, layer.attend)
    gather["gu"].step(1)
    gather["o"].step(2)
    gather["d"].step(0)
    loop(tiles // 2, lambda t: layer.attend(t + tiles // 2))
    gather["gu"].step(2)
    gather["o"].step(3)
    gather["d"].step(1)
    gather["gu"].step(3)
    loop(tiles // 2, layer.middle_gate)
    gather["d"].step(2)
    loop(tiles // 2, lambda t: layer.middle_gate(t + tiles // 2))
    gather["d"].step(3)
    net.drain()
    loop(tiles, layer.middle_down)
    layer.head_grad()

    shared = [named[k] for k in SHARED]
    reduce = {keys: Reduce(net, shared, parts[keys]) for keys in ("qkv", "o", "gu", "d")}
    for one in reduce.values():
        one.extra = named.get("extra")
    steps = {keys: one.steps() for keys, one in reduce.items()}
    left, right = layer.left_t, layer.right_t
    right[...] = layer.d_end_low[...].T
    reduce["d"].produce(right, layer.inner)
    for t in range(tiles):
        layer.middle_back(t)
        steps["d"][t]()
    left[...] = layer.ff_in[...].T
    reduce["gu"].produce(left, dgu)
    steps["d"][4]()
    right[...] = layer.d_mid_low[...].T
    reduce["o"].produce(right, layer.ctx)
    steps["gu"][0]()
    steps["d"][5]()
    left[...] = layer.attn_in[...].T
    layer.attend_back(0)
    steps["o"][0]()
    layer.attend_back(1)
    steps["gu"][1]()
    steps["d"][6]()
    layer.attend_back(2)
    steps["o"][1]()
    layer.attend_back(3)
    reduce["qkv"].produce(left, named["dqkv"])
    steps["gu"][2]()
    steps["o"][2]()
    steps["qkv"][0]()
    loop(tiles // 2, layer.embed_back)
    steps["gu"][3]()
    steps["qkv"][1]()
    loop(tiles // 2, lambda t: layer.embed_back(t + tiles // 2))
    layer.small_grads(net.head)
    total = Total(net, named["slabs"], named["inbox"])
    levels = len(total.partners)
    total.start(0)
    steps["o"][3]()
    steps["gu"][4]()
    total.step(0)
    steps["qkv"][2]()
    steps["o"][4]()
    layer.finish()
    steps["gu"][5]()
    total.step(1)
    steps["qkv"][3]()
    steps["o"][5]()
    total.step(2)
    steps["gu"][6]()
    steps["qkv"][4]()
    steps["o"][6]()
    total.step(3)
    steps["qkv"][5]()
    for level in range(4, levels):
        total.step(level)
    layer.sums[...] = named["slabs"][levels]
    steps["qkv"][6]()
    layer.fin_out[...] = named["fin"][...]
    net.drain()


def finish_kernel(
    heads, rebuilt, series_grad, sums, fin, o_rebuilt, o_series, o_attn, o_ff, o_final, o_pw, o_pb, o_q, o_k, o_v, o_o, o_table, o_g, o_u, o_d, o_hw, o_hb,
):
    o_rebuilt[...] = rebuilt[...]
    o_series[...] = series_grad[...]
    for row, out in enumerate((o_attn, o_ff, o_final, o_pb)):
        out[...] = sums[row : row + 1, :]
    patch = o_pw.shape[0]
    o_pw[...] = sums[8:16, :]
    o_hw[...] = sums[16:24, :]
    lane = iota((8, 128), 1)
    column = jnp.sum(
        jnp.where(lane == 2 * heads, sums[24:32, 0:128], 0.0), axis=1, keepdims=True
    )
    o_hb[...] = jnp.sum(jnp.where(lane == iota((8, 128), 0), column, 0.0), axis=0, keepdims=True)[
        :, :patch
    ]
    head_index = lax.axis_index("head")
    for which in range(2):
        row = jnp.zeros((1, 128), F32)
        for g in range(o_table.shape[1] // 8):
            piece = sums[24:32, g * 128 : (g + 1) * 128]
            column = jnp.sum(
                jnp.where(lane == 2 * head_index + which, piece, 0.0), axis=1, keepdims=True
            )
            row = row + jnp.sum(
                jnp.where(lane == 8 * g + iota((8, 128), 0), column, 0.0), axis=0, keepdims=True
            )
        o_table[which : which + 1, :] = row[:, : o_table.shape[1]]
    first = 0
    for out, turn in ((o_q, False), (o_k, False), (o_v, False), (o_o, True), (o_g, False), (o_u, False), (o_d, True)):
        width = out.shape[0] if turn else out.shape[1]
        block = fin[:, first : first + width].astype(F32)
        out[...] = block.T if turn else block
        first += width


def layer_call(groups, heads, args):
    series = args[0]
    rows, steps = series.shape
    patch, width = args[7].shape
    length = steps // patch
    tokens = rows * length
    part = args[9].shape[1]
    ff = args[14].shape[1]
    table_heads, table_rows = args[13].shape
    total = heads * (4 * part + 3 * ff)
    bits = groups.bit_length() - 1
    levels = bits + heads.bit_length() - 1
    scratch = dict(
        pm=((length, steps), F32), fold=((16, steps), BF16), ptile=((steps, width), BF16),
        htile=((width, steps), BF16), splitb=((rows, 128), F32), normed=((rows, steps), F32),
        normed_low=((rows, steps), F32), dout_low=((rows, steps), F32), output=((rows, steps), F32),
        d_normed=((rows, steps), F32), p8t=((16, tokens), BF16), d8t=((16, tokens), BF16),
        embedded=((tokens, width), F32), s_attn=((tokens, 1), F32), attn_in=((tokens, width), BF16),
        qkv=((tokens, heads * 3 * part), BF16), tab=((heads, table_rows, 128), F32),
        bias=((heads, length, 128), F32), probs=((heads, tokens, 128), F32),
        ctx=((tokens, heads * part), BF16), hidden_mid=((tokens, width), F32),
        ff_in=((tokens, width), BF16), inner=((tokens, heads * ff), BF16),
        act=((tokens, heads * ff), BF16), slope=((tokens, heads * ff), BF16),
        final_in=((tokens, width), BF16), d_end_low=((tokens, width), BF16),
        dgu=((tokens, heads * 2 * ff), BF16), d_mid=((tokens, width), F32),
        d_ctx=((tokens, heads * part), BF16), dsum=((heads, length, 128), F32),
        g_attn=((8, width), F32), g_ff=((8, width), F32), g_final=((8, width), F32),
        g_bias=((8, width), F32), tgr=((table_rows, 128), F32),
        left_t=((width, tokens), BF16), right_t=((width, tokens), BF16),
        weights=((width, total), BF16), own=((width // 2, total), BF16),
        snd0=((width // 2, total), BF16), rcv0=((width // 2, total), BF16),
        snd1=((width // 4, total), BF16), rcv1=((width // 4, total), BF16),
        snd2=((width // 8, total), BF16), rcv2=((width // 8, total), BF16),
        sndz=((width // 8, total), BF16), rcvz=((heads - 1, width // 8, total // heads), BF16),
        fin=((width, total // heads), BF16),
        slabs=((levels + 1, 32, width), F32), inbox=((levels, 32, width), F32),
    )
    if bits > 3:
        scratch["extra"] = ((bits - 3, width // 8, total), BF16)
    copies = 7 * 2 * (heads - 1 + 3) + heads - 1 + 7 * (10 + heads - 1 + bits - 3) + levels
    outs = [((rows, steps), F32), ((rows, steps), F32), ((32, width), F32), ((width, total // heads), BF16)]
    names = list(INPUTS + OUTPUTS) + list(scratch) + ["send_sems", "recv_sems"]
    vmem = pl.BlockSpec(memory_space=pltpu.VMEM)
    parts = pl.pallas_call(
        functools.partial(layer_kernel, groups, heads, names),
        out_shape=[jax.ShapeDtypeStruct(*out) for out in outs],
        in_specs=[vmem] * len(INPUTS),
        out_specs=[vmem] * len(OUTPUTS),
        scratch_shapes=[pltpu.VMEM(*v) for v in scratch.values()]
        + [pltpu.SemaphoreType.DMA((copies,)), pltpu.SemaphoreType.DMA((copies,))],
        compiler_params=pltpu.CompilerParams(
            collective_id=0, has_side_effects=True, vmem_limit_bytes=63 * 1024 * 1024
        ),
    )(*args)
    shapes = [
        (rows, steps), (rows, steps), (1, width), (1, width), (1, width), (patch, width), (1, width), (width, part), (width, part),
        (width, part), (part, width), (table_heads, table_rows), (width, ff), (width, ff), (ff, width),
        (patch, width), (1, patch),
    ]
    return list(
        pl.pallas_call(
            functools.partial(finish_kernel, heads),
            out_shape=[jax.ShapeDtypeStruct(shape, F32) for shape in shapes],
            in_specs=[vmem] * len(parts),
            out_specs=[vmem] * len(shapes),
        )(*parts)
    )


def solution(mesh):
    groups, heads = mesh.shape["dp"], mesh.shape["head"]

    def local(*args):
        args = list(args)
        for i in (2, 18):
            args[i] = args[i].reshape(1, -1)
        for i in (4, 5, 6, 8):
            args[i] = args[i].reshape(-1, 128)
        for i in (13, 17):
            args[i] = args[i].T
        outs = layer_call(groups, heads, args)
        for i in (2, 3, 4, 6, 16):
            outs[i] = outs[i].reshape(-1)
        outs[11], outs[15] = outs[11].T, outs[15].T
        return tuple(outs)

    both = P(("dp", "head"), None)
    by_column, by_row = P(None, "head"), P("head", None)
    return jax.shard_map(
        local,
        mesh=mesh,
        in_specs=(both, both, P("dp"), both) + (P(),) * 5 + (by_column,) * 3
        + (by_row, by_column, by_column, by_column, by_row, P(), P()),
        out_specs=(both, both) + (P(),) * 5 + (by_column,) * 3
        + (by_row, by_column, by_column, by_column, by_row, P(), P()),
        check_vma=False,
    )
```

```python
import functools
import math

import jax
import jax.numpy as jnp
from jax import lax
from jax.experimental import pallas as pl
from jax.experimental.pallas import tpu as pltpu
from jax.sharding import PartitionSpec as P

F32 = jnp.float32
BF16 = jnp.bfloat16
EPS = 1e-06
TILE = 256
MAX_DIST = 128


def bucket_cuts(buckets, length):
    half_count = buckets // 2
    exact_count = half_count // 2
    ids = []
    for distance in range(length):
        if distance < exact_count:
            ids.append(distance)
        else:
            ids.append(
                min(
                    half_count - 1,
                    exact_count
                    + int(
                        math.log(distance / exact_count)
                        / math.log(MAX_DIST / exact_count)
                        * (half_count - exact_count)
                    ),
                )
            )
    cuts = []
    for distance in range(1, length):
        cuts += [distance] * (ids[distance] - ids[distance - 1])
    return cuts, ids[-1]


def nt(left, right):
    return lax.dot_general(left, right, (((1,), (1,)), ((), ())), preferred_element_type=F32)


def nn(left, right):
    return jnp.dot(left, right, preferred_element_type=F32)


def tn(left, right):
    return lax.dot_general(left, right, (((0,), (0,)), ((), ())), preferred_element_type=F32)


def iota(shape, dim):
    return lax.broadcasted_iota(jnp.int32, shape, dim)


def fold8(values):
    return jnp.sum(values.reshape(values.shape[0] // 8, 8, values.shape[1]), axis=0)


def row_scale(values):
    return lax.rsqrt(jnp.mean(values * values, axis=-1, keepdims=True) + EPS)


def norm_back(grad_out, unit_rows, scale, gain_row):
    d_unit = grad_out * gain_row
    spread = jnp.mean(d_unit * unit_rows, axis=-1, keepdims=True)
    return scale * (d_unit - unit_rows * spread), fold8(grad_out * unit_rows)


class Layer:
    more = None

    def __init__(self, **refs):
        self.__dict__.update(refs)

    def prepare(self, head_index):
        rows, steps = self.series.shape
        half = steps // 2
        length = self.pm.shape[0]
        patch = steps // length
        split_row = self.split[...].astype(F32)
        pick = iota((rows, split_row.shape[1]), 1) == (
            iota((rows, split_row.shape[1]), 0) + head_index * rows
        )
        split_col = jnp.sum(jnp.where(pick, split_row, 0.0), axis=1, keepdims=True)
        self.splitb[...] = jnp.broadcast_to(split_col, self.splitb.shape)
        obs = self.observed[...].astype(F32)
        series = self.series[...]
        low_half = iota((rows, steps), 1) < half

        def halves(values):
            return [
                jnp.sum(values[:, :half], axis=1, keepdims=True),
                jnp.sum(values[:, half:], axis=1, keepdims=True),
            ]

        def combine(sums):
            both = sums[0] + sums[1]
            return [split_col * one + (1.0 - split_col) * both for one in sums]

        def spread(pair):
            return jnp.where(low_half, pair[0], pair[1])

        self.halves, self.combine, self.spread = halves, combine, spread
        self.counts = combine(halves(obs))
        item_mean = [a / b for a, b in zip(combine(halves(obs * series)), self.counts)]
        centred = series - spread(item_mean)
        item_var = [a / b for a, b in zip(combine(halves(obs * centred * centred)), self.counts)]
        self.std = [jnp.sqrt(v + 1e-05) for v in item_var]
        std_full = spread(self.std)
        self.std_full, self.mean_full = std_full, spread(item_mean)
        normed = obs * centred / std_full
        self.normed[...] = normed
        self.normed_low[...] = normed.astype(BF16).astype(F32)
        self.dout_low[...] = (self.cot[...] * std_full).astype(BF16).astype(F32)
        self.pm[...] = (iota(self.pm.shape, 1) // patch == iota(self.pm.shape, 0)).astype(F32)
        fold = (iota(self.fold.shape, 1) % patch == iota(self.fold.shape, 0)).astype(BF16)
        self.fold[...] = fold
        pw = self.patch_w[...].astype(F32)
        self.row_attn, self.row_ff, self.row_final, self.row_bias = (
            jnp.concatenate(
                [source[i : i + 1, :].astype(F32) for i in range(source.shape[0])], axis=1
            )
            for source in (self.gain_attn, self.gain_ff, self.gain_final, self.patch_b)
        )
        self.ptile[...] = jnp.broadcast_to(
            pw[None], (self.ptile.shape[0] // patch, patch, pw.shape[1])
        ).reshape(self.ptile.shape).astype(BF16)
        self.htile[...] = tn(self.head_w[...], fold[:patch]).astype(BF16)
        hb = jnp.broadcast_to(self.head_b[...], (16, patch))
        self.hbias = nn(hb, fold[:patch])[0:1]

    def spread_rows(self, source, tile):
        rows_tile = TILE // self.pm.shape[0]
        mask = self.pm[...]
        pieces = [
            (source[pl.ds(tile * rows_tile + r, 1), :] * mask).astype(BF16)
            for r in range(rows_tile)
        ]
        return jnp.concatenate(pieces, axis=0)

    def gather_rows(self, target, tile, values, extra=None):
        length = self.pm.shape[0]
        mask = self.pm[...]
        for r in range(TILE // length):
            part = jnp.sum(values[r * length : (r + 1) * length] * mask, axis=0, keepdims=True)
            if extra is not None:
                part = part + extra
            target[pl.ds(tile * (TILE // length) + r, 1), :] = part

    def embed(self, tile):
        at = pl.ds(pl.multiple_of(tile * TILE, TILE), TILE)
        spread = self.spread_rows(self.normed_low, tile)
        self.p8t[:, at] = nt(self.fold[...], spread).astype(BF16)
        embedded = nn(spread, self.ptile[...]) + self.row_bias
        self.embedded[at, :] = embedded
        scale = row_scale(embedded)
        self.s_attn[at, :] = scale
        self.attn_in[at, :] = (embedded * scale * self.row_attn).astype(BF16)

    def buckets(self):
        length = self.pm.shape[0]
        lanes = 2 * length
        key = iota((length, lanes), 0)
        query = iota((length, lanes), 1) % length
        offset = key - query
        distance = jnp.abs(offset)
        table = self.tab.shape[1]
        cuts, top = bucket_cuts(table, length)
        ids = jnp.where(offset > 0, table // 2, 0)
        for cut in cuts:
            ids = ids + (distance >= cut).astype(jnp.int32)
        used = list(range(top + 1)) + list(range(table // 2, table // 2 + top + 1))
        return ids, used

    def own_table(self):
        table = self.table[...].astype(BF16)
        pick = (iota((2, 128), 1) // 64 == iota((2, 128), 0)).astype(BF16)
        self.tab[0] = tn(table, pick)

    def offsets(self, slot):
        ids, used = self.buckets()
        total = jnp.zeros(ids.shape, F32)
        for b in used:
            total = jnp.where(ids == b, self.tab[slot, b : b + 1, :], total)
        self.bias[slot] = total

    def head_masks(self):
        lane = iota((1, 128), 1)
        return (lane < 64).astype(BF16), (lane >= 64).astype(BF16)

    def attend(self, tile):
        at = pl.ds(pl.multiple_of(tile * TILE, TILE), TILE)
        length = self.pm.shape[0]
        rows_tile = TILE // length
        even, odd = self.head_masks()
        half = length // 2
        shape = (length, 2 * length)
        block = (iota(shape, 0) // half != (iota(shape, 1) % length) // half).astype(F32) * -1e30
        splits = [self.splitb[pl.ds(tile * rows_tile + r, 1), :] * block for r in range(rows_tile)]
        width = self.ctx.shape[1]
        projected = []
        for i in range(3):
            part = nn(self.attn_in[at, :], self.wq[:, i * width : (i + 1) * width]).astype(BF16)
            self.qkv[at, i * width : (i + 1) * width] = part
            projected.append(part)
        items = [(s, r) for s in range(self.slots) for r in range(rows_tile)]

        def piece(s, r, i):
            return projected[i][r * length : (r + 1) * length, s * 128 : (s + 1) * 128]

        scores = []
        for s, r in items:
            query = piece(s, r, 0)
            both = jnp.concatenate([query * even, query * odd], axis=0)
            scores.append(nt(piece(s, r, 1), both))
        turned = []
        for (s, r), score in zip(items, scores):
            score = score + (self.bias[s] + splits[r])
            top = jnp.max(score, axis=0, keepdims=True)
            raised = jnp.exp(score - top)
            probs = raised * (1.0 / jnp.sum(raised, axis=0, keepdims=True))
            self.probs[
                s, pl.ds(pl.multiple_of(tile * TILE + r * length, length), length), :
            ] = probs.astype(self.probs.dtype)
            turned.append(probs.astype(BF16))
        turned = [probs.T for probs in turned]
        mixed = [nn(probs, piece(s, r, 2)) for probs, (s, r) in zip(turned, items)]
        low_lanes = iota((1, 128), 1) < 64
        for s in range(self.slots):
            self.ctx[at, s * 128 : (s + 1) * 128] = jnp.concatenate(
                [
                    jnp.where(low_lanes, m[:length], m[length:]).astype(BF16)
                    for m in mixed[s * rows_tile : (s + 1) * rows_tile]
                ],
                axis=0,
            )

    def middle_gate(self, tile):
        at = pl.ds(pl.multiple_of(tile * TILE, TILE), TILE)
        hidden_mid = self.embedded[at, :] + nt(self.ctx[at, :], self.wo[...])
        self.hidden_mid[at, :] = hidden_mid
        ff_in = (hidden_mid * row_scale(hidden_mid) * self.row_ff).astype(BF16)
        self.ff_in[at, :] = ff_in
        total = self.inner.shape[1]
        block = 256
        c = math.sqrt(2.0 / math.pi)
        for first in range(0, total, block):
            cols = slice(first, first + block)
            gate = nn(ff_in, self.wg[:, first : first + block])
            up = nn(ff_in, self.wg[:, total + first : total + first + block])
            square = gate * gate
            t = jnp.tanh(gate * (c + (c * 0.044715) * square))
            plus = 0.5 * (1.0 + t)
            act = gate * plus
            slope = plus + (0.5 * gate) * (1.0 - t * t) * (c + (3.0 * c * 0.044715) * square)
            self.inner[at, cols] = (act * up).astype(BF16)
            self.act[at, cols] = act.astype(BF16)
            self.slope[at, cols] = (up * slope).astype(BF16)

    def cotangent(self, tile):
        at = pl.ds(pl.multiple_of(tile * TILE, TILE), TILE)
        d_spread = self.spread_rows(self.dout_low, tile)
        self.d8t[:, at] = nt(self.fold[...], d_spread).astype(BF16)
        self.d_mid[at, :] = nt(d_spread, self.htile[...])

    def outputs(self, tile):
        at = pl.ds(pl.multiple_of(tile * TILE, TILE), TILE)
        self.gather_rows(
            self.output, tile, nn(self.final_in[at, :], self.htile[...]), self.hbias
        )

    def middle_down(self, tile):
        at = pl.ds(pl.multiple_of(tile * TILE, TILE), TILE)
        hidden_end = self.hidden_mid[at, :] + nt(self.inner[at, :], self.wd[...])
        final_scale = row_scale(hidden_end)
        final_unit = hidden_end * final_scale
        gain_final = self.row_final
        final_in = (final_unit * gain_final).astype(BF16)
        self.final_in[at, :] = final_in
        d_end, gain_part = norm_back(self.d_mid[at, :], final_unit, final_scale, gain_final)
        self.g_final[...] += gain_part
        self.d_end_low[at, :] = d_end.astype(BF16)
        self.d_mid[at, :] = d_end

    def inner_back(self, tile):
        at = pl.ds(pl.multiple_of(tile * TILE, TILE), TILE)
        d_low = self.d_end_low[at, :]
        total = self.inner.shape[1]
        block = 256
        for first in range(0, total, block):
            cols = slice(first, first + block)
            d_inner = nn(d_low, self.wd[:, cols])
            d_gate = (d_inner * self.slope[at, cols].astype(F32)).astype(BF16)
            d_up = (d_inner * self.act[at, cols].astype(F32)).astype(BF16)
            self.dgu[at, cols] = d_gate
            self.dgu[at, total + first : total + first + block] = d_up

    def middle_back(self, tile):
        at = pl.ds(pl.multiple_of(tile * TILE, TILE), TILE)
        d_in = nt(self.dgu[at, :], self.wg[...])
        hidden_mid = self.hidden_mid[at, :]
        ff_scale = row_scale(hidden_mid)
        d_norm, gain_part = norm_back(d_in, hidden_mid * ff_scale, ff_scale, self.row_ff)
        self.g_ff[...] += gain_part
        d_mid = self.d_mid[at, :] + d_norm
        self.d_mid[at, :] = d_mid
        d_mid_low = d_mid.astype(BF16)
        self.d_mid_low[at, :] = d_mid_low
        self.d_ctx[at, :] = nn(d_mid_low, self.wo[...]).astype(BF16)

    def attend_back(self, tile):
        width = self.ctx.shape[1]
        length = self.pm.shape[0]
        rows_tile = TILE // length
        even, odd = self.head_masks()
        items = [(s, r) for s in range(self.slots) for r in range(rows_tile)]
        rows = [
            pl.ds(pl.multiple_of(tile * TILE + r * length, length), length)
            for r in range(rows_tile)
        ]

        def piece(s, r, i):
            return self.qkv[rows[r], i * width + s * 128 : i * width + (s + 1) * 128]

        d_both = []
        for s, r in items:
            d_ctx = self.d_ctx[rows[r], s * 128 : (s + 1) * 128]
            d_both.append(jnp.concatenate([d_ctx * even, d_ctx * odd], axis=0))
        d_probs = [nt(piece(s, r, 2), both) for (s, r), both in zip(items, d_both)]
        probs = [self.probs[s, rows[r], :] for s, r in items]
        d_value = [nn(p.astype(BF16), both) for p, both in zip(probs, d_both)]
        d_scores = []
        for p, dp in zip(probs, d_probs):
            p = p.astype(F32)
            dots = jnp.sum(p * dp, axis=0, keepdims=True)
            d_scores.append((p * (dp - dots)).astype(BF16))
        turned = [d.T for d in d_scores]
        d_key = []
        for (s, r), d in zip(items, d_scores):
            query = piece(s, r, 0)
            d_key.append(nn(d, jnp.concatenate([query * even, query * odd], axis=0)))
        mixed = [nn(d, piece(s, r, 1)) for (s, r), d in zip(items, turned)]
        low_lanes = iota((1, 128), 1) < 64
        for n, (s, r) in enumerate(items):
            d_query = jnp.where(low_lanes, mixed[n][:length], mixed[n][length:])
            for i, grad in enumerate((d_query, d_key[n], d_value[n])):
                cols = slice(i * width + s * 128, i * width + (s + 1) * 128)
                self.dqkv[rows[r], cols] = grad.astype(BF16)
        for s in range(self.slots):
            total = self.dsum[s]
            for d in d_scores[s * rows_tile : (s + 1) * rows_tile]:
                total = total + d.astype(F32)
            self.dsum[s] = total

    def embed_back(self, tile):
        at = pl.ds(pl.multiple_of(tile * TILE, TILE), TILE)
        d_in = nt(self.dqkv[at, :], self.wq[...])
        scale = self.s_attn[at, :]
        d_norm, gain_part = norm_back(
            d_in, self.embedded[at, :] * scale, scale, self.row_attn
        )
        self.g_attn[...] += gain_part
        d_embedded = (self.d_mid[at, :] + d_norm).astype(BF16)
        self.d_emb[at, :] = d_embedded
        self.g_bias[...] += fold8(d_embedded.astype(F32))
        self.gather_rows(self.d_normed, tile, nt(d_embedded, self.ptile[...]))

    def finish(self):
        obs = self.observed[...].astype(F32)
        cot = self.cot[...]
        output = self.output[...]
        std_full, mean_full = self.std_full, self.mean_full
        self.rebuilt[...] = output * std_full + mean_full
        d_normed = self.d_normed[...]
        std_grad = [
            a - b / c
            for a, b, c in zip(
                self.halves(cot * output), self.halves(d_normed * self.normed[...]), self.std
            )
        ]
        var_weight = self.combine(
            [g / (2.0 * s) / n for g, s, n in zip(std_grad, self.std, self.counts)]
        )
        centred = self.series[...] - mean_full
        d_centred = d_normed * obs / std_full + 2.0 * obs * centred * self.spread(var_weight)
        mean_grad = [a - b for a, b in zip(self.halves(cot), self.halves(d_centred))]
        mean_weight = self.combine([g / n for g, n in zip(mean_grad, self.counts)])
        self.series_grad[...] = d_centred + obs * self.spread(mean_weight)

    def head_grad(self):
        self.small[16:24, :] = nn(self.d8t[...], self.final_in[...])[0:8]

    def small_grads(self, head_index):
        small = self.small
        heads = self.slots
        self.head_grad()
        zero = jnp.zeros((4, self.embedded.shape[1]), F32)
        small[0:8, :] = jnp.concatenate(
            [jnp.sum(r[...], axis=0, keepdims=True) for r in (self.g_attn, self.g_ff, self.g_final, self.g_bias)]
            + [zero],
            axis=0,
        )
        small[8:16, :] = nn(self.p8t[...], self.d_emb[...])[0:8]
        lane = iota((8, 128), 1)
        groups = self.tab.shape[1] // 8
        pieces = [jnp.zeros((8, 128), F32) for _ in range(groups)]
        pieces[0] = jnp.where(
            lane == 2 * heads, jnp.sum(self.d8t[0:8, :].astype(F32), axis=1, keepdims=True), 0.0
        )
        ids, used = self.buckets()
        for s in range(self.slots):
            dsum = self.dsum[s]
            owner = lax.rem(head_index + s, heads)
            for b in range(self.tab.shape[1]):
                if b in used:
                    self.tgr[b : b + 1, :] = jnp.sum(
                        jnp.where(ids == b, dsum, 0.0), axis=0, keepdims=True
                    )
                else:
                    self.tgr[b : b + 1, :] = jnp.zeros((1, 128), F32)
            for g in range(groups):
                rows = self.tgr[8 * g : 8 * g + 8, :]
                for which in range(2):
                    inside = (lane < 64) if which == 0 else (lane >= 64)
                    column = jnp.sum(jnp.where(inside, rows, 0.0), axis=1, keepdims=True)
                    pieces[g] = pieces[g] + jnp.where(lane == 2 * owner + which, column, 0.0)
        small[24:32, :] = jnp.concatenate(pieces, axis=1)

    def clear(self):
        for ref in (self.g_attn, self.g_ff, self.g_final, self.g_bias):
            ref[...] = jnp.zeros(ref.shape, F32)
        self.dsum[...] = jnp.zeros(self.dsum.shape, F32)


MESH = pl.DeviceIdType.MESH


TABLE, WEIGHTS, HALVES, QUARTERS, EIGHTHS, OWNERS, FIN, SMALL, PLANE, HEADS = range(-11, -1)


class Net:
    def __init__(self, groups, heads, send_sems, recv_sems):
        self.dp, self.head = lax.axis_index("dp"), lax.axis_index("head")
        self.bits = groups.bit_length() - 1
        self.heads = heads
        self.send_sems, self.recv_sems = send_sems, recv_sems
        self.recv_ids, self.send_ids = {}, {}

    def bit(self, which):
        return (self.dp // (1 << which)) % 2

    def across(self, *which):
        place = self.dp
        for one in which:
            place = place + (1 - 2 * self.bit(one)) * (1 << one)
        return (place, self.head)

    def beside(self, hops):
        return (self.dp, (self.head + hops) % self.heads)

    def plane(self):
        return [self.across(1), self.across(2), self.across(1, 2)]

    def partners(self):
        found = [self.across(b) for b in range(self.bits)] + [self.across(1, 2)]
        return found + [self.beside(t) for t in range(1, self.heads)]

    def greet_start(self):
        barrier = pltpu.get_barrier_semaphore()
        for partner in self.partners():
            pl.semaphore_signal(barrier, inc=1, device_id=partner, device_id_type=MESH)

    def greet_end(self):
        pl.semaphore_wait(pltpu.get_barrier_semaphore(), len(self.partners()))

    def copy(self, key, group, src, dst, device):
        recv = self.recv_ids.setdefault(key, len(self.recv_ids))
        send = self.send_ids.setdefault(group, len(self.send_ids))
        return pltpu.make_async_remote_copy(
            src_ref=src,
            dst_ref=dst,
            send_sem=self.send_sems.at[send],
            recv_sem=self.recv_sems.at[recv],
            device_id=device,
            device_id_type=MESH,
        )

    def send(self, key, group, src, dst, device):
        self.copy(key, group, src, dst, device).start()

    def arrived(self, key, group, bulk):
        self.copy(key, group, bulk, bulk, self.across(0)).wait_recv()

    def sent(self, group, bulk):
        self.copy(-1, group, bulk, bulk, self.across(0)).wait_send()


def rows_at(start, count, unit):
    return pl.ds(pl.multiple_of(start, unit), count)


class Gather:
    ORDERS = ((1, 2, 0), (2, 1, 0))

    def __init__(self, net, ref, name, first, width):
        self.net, self.ref, self.name = net, ref, name
        self.first, self.width = first, width
        self.heads = net.heads
        self.unit = ref.shape[0] // 16
        self.others = slice(first + width, first + self.heads * width)

    def block(self, half):
        bits = [self.net.bit(b) for b in self.ORDERS[half]]
        return bits[0] + 2 * bits[1] + 4 * bits[2]

    def span(self, half, level):
        size = 1 << level
        first = self.block(half) // size
        return rows_at((half * 8 + first * size) * self.unit, size * self.unit, self.unit)

    def start(self):
        net, first, width = self.net, self.first, self.width
        for half in range(2):
            rows = self.span(half, 0)
            for t in range(1, self.heads):
                slot = self.heads - t
                net.send(
                    (self.name, 0),
                    WEIGHTS,
                    self.ref.at[rows, first : first + width],
                    self.ref.at[rows, first + slot * width : first + (slot + 1) * width],
                    net.beside(t),
                )

    def step(self, level):
        net = self.net
        count = 2 * self.unit << max(level - 1, 0)
        net.arrived((self.name, level), WEIGHTS, self.ref.at[0:count, self.others])
        if level < 3:
            for half in range(2):
                place = self.ref.at[self.span(half, level), self.others]
                net.send(
                    (self.name, level + 1),
                    WEIGHTS,
                    place,
                    place,
                    net.across(self.ORDERS[half][level]),
                )


class Reduce:
    ORDERS = ((1, 2), (2, 1))

    def __init__(self, net, refs, name, first, width):
        self.__dict__.update(refs)
        self.net, self.name = net, name
        self.heads = net.heads
        self.width = width
        self.columns = slice(first, first + self.heads * width)
        self.fin_columns = slice(first // self.heads, first // self.heads + width)

    def slots(self, s):
        first = self.columns.start + s * self.width
        return slice(first, first + self.width)

    def partner(self, left_t, right):
        net, cols = self.net, self.columns
        count = self.own.shape[0]
        rows = rows_at((1 - net.bit(0)) * count, count, count)
        self.snd0[:, cols] = nn(left_t[rows, :], right[...]).astype(BF16)
        net.send(
            (self.name, 4), HALVES, self.snd0.at[:, cols], self.rcv0.at[:, cols], net.across(0)
        )

    def mine(self, left_t, right):
        count = self.own.shape[0]
        rows = rows_at(self.net.bit(0) * count, count, count)
        self.own[:, self.columns] = nn(left_t[rows, :], right[...]).astype(self.own.dtype)

    def kept(self, half, level):
        count = self.own.shape[0] // 2
        start = half * count
        for step in range(level):
            count = count // 2
            start = start + self.net.bit(self.ORDERS[half][step]) * count
        return start

    def halving(self, level):
        net, cols = self.net, self.columns
        source = (self.rcv0, self.rcv1, self.rcv2)[level]
        count = self.own.shape[0] // 2 >> level
        net.arrived((self.name, 4 + level), HALVES, source.at[:, cols])
        if level < 2:
            group = (QUARTERS, EIGHTHS)[level]
            send, target = ((self.snd1, self.rcv1), (self.snd2, self.rcv2))[level]
            part = count // 2
            for half in range(2):
                away = (1 - net.bit(self.ORDERS[half][level])) * part
                place = slice(half * part, (half + 1) * part)
                send[place, cols] = (
                    self.own[rows_at(self.kept(half, level) + away, part, 32), cols].astype(F32)
                    + source[rows_at(half * count + away, part, 32), cols].astype(F32)
                ).astype(BF16)
                net.send(
                    (self.name, 5 + level),
                    group,
                    send.at[place, cols],
                    target.at[place, cols],
                    net.across(self.ORDERS[half][level]),
                )
            for half in range(2):
                stay = net.bit(self.ORDERS[half][level]) * part
                rows = rows_at(self.kept(half, level) + stay, part, 32)
                self.own[rows, cols] = (
                    self.own[rows, cols].astype(F32)
                    + source[rows_at(half * count + stay, part, 32), cols].astype(F32)
                ).astype(self.own.dtype)
        else:
            for half in range(2):
                part = slice(half * count, (half + 1) * count)
                self.sndz[part, cols] = (
                    self.own[rows_at(self.kept(half, 2), count, 32), cols].astype(F32)
                    + source[part, cols].astype(F32)
                ).astype(BF16)

    def groups(self):
        net, cols = self.net, self.columns
        for bit in range(3, net.bits):
            inbox = self.extra.at[bit - 3]
            copy = net.copy(
                (self.name, 8 + bit),
                (self.name, bit),
                self.sndz.at[:, cols],
                inbox.at[:, cols],
                net.across(bit),
            )
            copy.start()
            copy.wait()
            self.sndz[:, cols] = (
                self.sndz[:, cols].astype(F32) + inbox[:, cols].astype(F32)
            ).astype(BF16)

    def owners(self):
        net = self.net
        for s in range(1, self.heads):
            net.send(
                (self.name, 7),
                OWNERS,
                self.sndz.at[:, self.slots(s)],
                self.rcvz.at[s - 1, :, self.fin_columns],
                net.beside(s),
            )

    def place(self, half, level):
        net = self.net
        quarter = self.fin.shape[0] // 4
        count = quarter // 4
        start = net.bit(0) * 2 * quarter + half * quarter
        order = self.ORDERS[half]
        start = start + net.bit(order[0]) * 2 * count
        if level == 0:
            return rows_at(start + net.bit(order[1]) * count, count, count)
        return rows_at(start, 2 * count, count)

    def owned(self):
        net, fin = self.net, self.fin_columns
        count = self.sndz.shape[0] // 2
        net.arrived((self.name, 7), OWNERS, self.rcvz.at[:, :, fin])
        for half in range(2):
            part = slice(half * count, (half + 1) * count)
            total = self.sndz[part, self.slots(0)].astype(F32)
            for s in range(1, self.heads):
                total = total + self.rcvz[s - 1, part, fin].astype(F32)
            rows = self.place(half, 0)
            self.fin[rows, fin] = total.astype(BF16)
            place = self.fin.at[rows, fin]
            net.send((self.name, 8), FIN, place, place, net.across(self.ORDERS[half][1]))

    def spread(self, level):
        net, fin = self.net, self.fin_columns
        rows = self.fin.shape[0]
        count = (rows // 8, rows // 4, rows // 2)[level]
        net.arrived((self.name, 8 + level), FIN, self.fin.at[0:count, fin])
        if level == 0:
            for half in range(2):
                place = self.fin.at[self.place(half, 1), fin]
                net.send((self.name, 9), FIN, place, place, net.across(self.ORDERS[half][0]))
        if level == 1:
            place = self.fin.at[rows_at(net.bit(0) * (rows // 2), rows // 2, rows // 2), fin]
            net.send((self.name, 10), FIN, place, place, net.across(0))
        if level == 2:
            pltpu.make_async_copy(
                self.fin.at[:, fin], self.fin_out.at[:, fin], self.out_sem
            ).start()

    def steps(self):
        return [
            lambda: self.halving(0),
            lambda: self.halving(1),
            lambda: (self.halving(2), self.groups(), self.owners()),
            self.owned,
            lambda: self.spread(0),
            lambda: self.spread(1),
            lambda: self.spread(2),
        ]


class Total:
    def __init__(self, net, small, core_in, plane, more, across):
        self.net, self.small, self.core_in = net, small, core_in
        self.plane, self.more, self.heads = plane, more, across

    def start(self):
        net = self.net
        net.send(SMALL, SMALL, self.small, self.core_in, net.across(0))

    def cores(self):
        net = self.net
        net.arrived(SMALL, SMALL, self.core_in)
        here = net.bit(1) + 2 * net.bit(2)
        self.plane[here] = (self.small[...] + self.core_in[...]).astype(BF16)
        for partner in net.plane():
            net.send(PLANE, PLANE, self.plane.at[here], self.plane.at[here], partner)

    def chips(self):
        net = self.net
        net.arrived(PLANE, PLANE, self.plane.at[0:3])
        total = self.summed(self.plane, 4)
        for bit in range(3, net.bits):
            mine, theirs = self.more.at[2 * (bit - 3)], self.more.at[2 * (bit - 3) + 1]
            mine[...] = total.astype(BF16)
            copy = net.copy((SMALL, bit), (SMALL, bit), mine, theirs, net.across(bit))
            copy.start()
            copy.wait()
            total = mine[...].astype(F32) + theirs[...].astype(F32)
        self.heads[net.head] = total.astype(BF16)
        for t in range(1, net.heads):
            place = self.heads.at[net.head]
            net.send(HEADS, HEADS, place, place, net.beside(t))

    def done(self):
        net = self.net
        net.arrived(HEADS, HEADS, self.heads.at[1 : net.heads])
        return self.summed(self.heads, net.heads)

    def summed(self, ref, count):
        total = ref[0].astype(F32)
        for i in range(1, count):
            total = total + ref[i].astype(F32)
        return total


def loop(count, body):
    def once(i, carry):
        body(i)
        return carry

    lax.fori_loop(0, count, once, 0)


CHUNKS = 10
Q, K, V, O, G1, G2, U1, U2, D1, D2 = range(CHUNKS)
ORDER = (
    0, 46, 60, 74, 88, 1, 2, 3, 4, 5, 6, 7, 47, 102, 61, 130, 75, 116, 48, 89, 144, 62, 103, 158,
    76, 49, 131, 172, 90, 50, 117, 63, 104, 64, 145, 77, 132, 159, 78, 8, 91, 118, 173, 9, 92, 105,
    146, 10, 106, 133, 11, 160, 134, 119, 174, 120, 147, 148, 12, 161, 13, 162, 175, 14, 176, 15,
    16, 17, 18, 19, 38, 163, 177, 164, 178, 39, 20, 165, 179, 21, 22, 23, 107, 121, 135, 149, 108,
    122, 136, 150, 24, 109, 166, 123, 137, 151, 25, 180, 26, 27, 40, 110, 93, 94, 41, 167, 28, 95,
    124, 29, 30, 138, 31, 51, 65, 79, 52, 152, 66, 80, 32, 168, 181, 111, 53, 67, 81, 33, 96, 34,
    125, 139, 35, 169, 153, 42, 182, 54, 36, 43, 112, 37, 68, 126, 82, 97, 170, 183, 140, 55, 171,
    154, 113, 44, 69, 127, 83, 98, 184, 141, 155, 114, 185, 56, 128, 115, 99, 129, 142, 156, 57,
    143, 157, 45, 100, 70, 101, 58, 84, 59, 71, 85, 72, 73, 86, 87,
)


def inputs(
    series, observed, split, cot, gain_attn, gain_ff, gain_final, patch_w, patch_b, wq_in, wk_in,
    wv_in, wo_in, table, wg_in, wu_in, wd_in, head_w, head_b, rebuilt, series_grad, sums, fin_out,
):
    return locals()


def layer_kernel(groups, heads, names, *refs):
    count = len(refs) - len(names) - 3
    named = inputs(*refs[:count])
    named.update(zip(names, refs[count:]))
    send_sems, recv_sems, out_sem = refs[-3:]
    layer = Layer(slots=heads, **named)
    weights, dgu, fin = layer.weights, layer.dgu, layer.fin
    width = layer.wq_in.shape[1]
    block = heads * width
    layer.wq = weights.at[:, Q * block : O * block]
    layer.wo = weights.at[:, O * block : G1 * block]
    layer.wg = weights.at[:, G1 * block : D1 * block]
    layer.wd = weights.at[:, D1 * block :]
    layer.dqkv = dgu.at[:, 0 : O * block]
    layer.d_emb = layer.ff_in
    tiles = layer.embedded.shape[0] // TILE
    net = Net(groups, heads, send_sems, recv_sems)
    left, right = layer.left_t, layer.right_t

    def own():
        for chunk, ref in ((Q, layer.wq_in), (K, layer.wk_in), (V, layer.wv_in)):
            weights[:, chunk * block : chunk * block + width] = ref[...]
        weights[:, O * block : O * block + width] = layer.wo_in[...].T
        for i in range(layer.wg_in.shape[1] // width):
            cols = slice(i * width, (i + 1) * width)
            for chunk, part in (
                (G1 + i, layer.wg_in[:, cols]),
                (U1 + i, layer.wu_in[:, cols]),
                (D1 + i, layer.wd_in[cols, :].T),
            ):
                weights[:, chunk * block : chunk * block + width] = part
        layer.own_table()

    def greet():
        net.greet_end()
        for t in range(1, heads):
            net.send(TABLE, TABLE, layer.tab.at[0], layer.tab.at[heads - t], net.beside(t))

    def offsets():
        net.arrived(TABLE, TABLE, layer.tab.at[1:heads])
        loop(heads, layer.offsets)

    def turn(target, source):
        target[...] = source[...].T

    def sums():
        layer.sums[...] = total.done()

    total = Total(net, layer.small, layer.core_in, layer.plane, layer.more, layer.heads_in)
    tasks = [
        greet,
        lambda: (layer.clear(), layer.prepare(net.head)),
        lambda: loop(tiles, layer.embed),
        offsets,
    ]
    for body in (
        layer.cotangent,
        layer.attend,
        layer.middle_gate,
        layer.middle_down,
        layer.inner_back,
        layer.middle_back,
        layer.attend_back,
        layer.embed_back,
    ):
        tasks += [functools.partial(body, t) for t in range(tiles)]
    tasks += [
        lambda: loop(tiles, layer.outputs),
        layer.finish,
        lambda: turn(right, layer.d_end_low),
        lambda: turn(left, layer.ff_in),
        lambda: turn(right, layer.d_mid_low),
        lambda: turn(left, layer.attn_in),
        lambda: (layer.small_grads(net.head), total.start()),
        total.cores,
        total.chips,
        sums,
    ]
    sources = [(left, layer.dqkv, i) for i in range(3)] + [(right, layer.ctx, 0)]
    sources += [(left, dgu, i) for i in range(4)] + [(right, layer.inner, i) for i in range(2)]
    named.update(out_sem=out_sem)
    for chunk, (turned, source, i) in enumerate(sources):
        gather = Gather(net, weights, chunk, chunk * block, width)
        reduce = Reduce(net, named, chunk, chunk * block, width)
        source = source.at[:, i * block : (i + 1) * block]
        tasks += [gather.start] + [functools.partial(gather.step, level) for level in range(4)]
        tasks += [
            functools.partial(reduce.partner, turned, source),
            functools.partial(reduce.mine, turned, source),
        ]
        tasks += reduce.steps()

    net.greet_start()
    own()
    for place in ORDER:
        tasks[place]()
    slots = heads - 1
    pltpu.make_async_copy(fin, layer.fin_out, out_sem).wait()
    net.sent(TABLE, layer.tab.at[1:heads])
    net.sent(WEIGHTS, weights.at[:, 0 : slots * fin.shape[1]])
    net.sent(HALVES, layer.snd0)
    net.sent(QUARTERS, layer.snd1)
    net.sent(EIGHTHS, layer.snd2)
    net.sent(OWNERS, layer.sndz.at[:, 0 : slots * fin.shape[1]])
    net.sent(FIN, fin.at[0 : fin.shape[0] * 7 // 8])
    net.sent(SMALL, layer.small)
    net.sent(PLANE, layer.plane.at[0:3])
    net.sent(HEADS, layer.heads_in.at[1:heads])


def finish_kernel(
    heads, rebuilt, series_grad, sums, fin, o_rebuilt, o_series, o_attn, o_ff, o_final, o_pw, o_pb, o_q, o_k, o_v, o_o, o_table, o_g, o_u, o_d, o_hw, o_hb,
):
    o_rebuilt[...] = rebuilt[...]
    o_series[...] = series_grad[...]
    for row, out in enumerate((o_attn, o_ff, o_final, o_pb)):
        out[...] = sums[row : row + 1, :]
    patch = o_pw.shape[0]
    o_pw[...] = sums[8:16, :]
    o_hw[...] = sums[16:24, :]
    lane = iota((8, 128), 1)
    column = jnp.sum(
        jnp.where(lane == 2 * heads, sums[24:32, 0:128], 0.0), axis=1, keepdims=True
    )
    o_hb[...] = jnp.sum(jnp.where(lane == iota((8, 128), 0), column, 0.0), axis=0, keepdims=True)[
        :, :patch
    ]
    head_index = lax.axis_index("head")
    for which in range(2):
        row = jnp.zeros((1, 128), F32)
        for g in range(o_table.shape[1] // 8):
            piece = sums[24:32, g * 128 : (g + 1) * 128]
            column = jnp.sum(
                jnp.where(lane == 2 * head_index + which, piece, 0.0), axis=1, keepdims=True
            )
            row = row + jnp.sum(
                jnp.where(lane == 8 * g + iota((8, 128), 0), column, 0.0), axis=0, keepdims=True
            )
        o_table[which : which + 1, :] = row[:, : o_table.shape[1]]
    first = 0
    for out, turn in ((o_q, False), (o_k, False), (o_v, False), (o_o, True), (o_g, False), (o_u, False), (o_d, True)):
        width = out.shape[0] if turn else out.shape[1]
        block = fin[:, first : first + width].astype(F32)
        out[...] = block.T if turn else block
        first += width


def layer_call(groups, heads, args):
    series = args[0]
    rows, steps = series.shape
    patch, width = args[7].shape
    length = steps // patch
    tokens = rows * length
    part = args[9].shape[1]
    ff = args[14].shape[1]
    table_heads, table_rows = args[13].shape
    total = heads * (4 * part + 3 * ff)
    bits = groups.bit_length() - 1
    scratch = dict(
        pm=((length, steps), F32), fold=((16, steps), BF16), ptile=((steps, width), BF16),
        htile=((width, steps), BF16), splitb=((rows, 128), F32), normed=((rows, steps), F32),
        normed_low=((rows, steps), F32), dout_low=((rows, steps), F32), output=((rows, steps), F32),
        d_normed=((rows, steps), F32), p8t=((16, tokens), BF16), d8t=((16, tokens), BF16),
        embedded=((tokens, width), F32), s_attn=((tokens, 1), F32), attn_in=((tokens, width), BF16),
        qkv=((tokens, heads * 3 * part), BF16), tab=((heads, table_rows, 128), F32),
        bias=((heads, length, 128), F32), probs=((heads, tokens, 128), F32),
        ctx=((tokens, heads * part), BF16), hidden_mid=((tokens, width), F32),
        ff_in=((tokens, width), BF16), inner=((tokens, heads * ff), BF16),
        act=((tokens, heads * ff), BF16), slope=((tokens, heads * ff), BF16),
        final_in=((tokens, width), BF16), d_end_low=((tokens, width), BF16),
        dgu=((tokens, heads * 2 * ff), BF16), d_mid=((tokens, width), F32),
        d_ctx=((tokens, heads * part), BF16), dsum=((heads, length, 128), F32),
        g_attn=((8, width), F32), g_ff=((8, width), F32), g_final=((8, width), F32),
        g_bias=((8, width), F32), tgr=((table_rows, 128), F32),
        left_t=((width, tokens), BF16), right_t=((width, tokens), BF16),
        weights=((width, total), BF16), own=((width // 2, total), BF16),
        snd0=((width // 2, total), BF16), rcv0=((width // 2, total), BF16),
        snd1=((width // 4, total), BF16), rcv1=((width // 4, total), BF16),
        snd2=((width // 8, total), BF16), rcv2=((width // 8, total), BF16),
        sndz=((width // 8, total), BF16), rcvz=((heads - 1, width // 8, total // heads), BF16),
        fin=((width, total // heads), BF16), small=((32, width), F32), core_in=((32, width), F32),
        plane=((4, 32, width), BF16), heads_in=((heads, 32, width), BF16),
        d_mid_low=((tokens, width), BF16),
    )
    extra = bits - 3
    if extra > 0:
        scratch.update(
            extra=((extra, width // 8, total), BF16), more=((2 * extra, 32, width), BF16)
        )
    copies = CHUNKS * (4 + 7 + extra) + 4 + extra + 1
    sends = 10 + (CHUNKS + 1) * extra
    outs = [((rows, steps), F32), ((rows, steps), F32), ((32, width), F32), ((width, total // heads), BF16)]
    vmem = pl.BlockSpec(memory_space=pltpu.VMEM)
    parts = pl.pallas_call(
        functools.partial(layer_kernel, groups, heads, list(scratch)),
        out_shape=[jax.ShapeDtypeStruct(*out) for out in outs],
        in_specs=[vmem] * len(args),
        out_specs=[vmem] * 3 + [pl.BlockSpec(memory_space=pl.ANY)],
        scratch_shapes=[pltpu.VMEM(*v) for v in scratch.values()]
        + [
            pltpu.SemaphoreType.DMA((sends,)),
            pltpu.SemaphoreType.DMA((copies,)),
            pltpu.SemaphoreType.DMA,
        ],
        compiler_params=pltpu.CompilerParams(
            collective_id=0, has_side_effects=True, vmem_limit_bytes=63 * 1024 * 1024
        ),
    )(*args)
    shapes = [
        (rows, steps), (rows, steps), (1, width), (1, width), (1, width), (patch, width), (1, width), (width, part), (width, part),
        (width, part), (part, width), (table_heads, table_rows), (width, ff), (width, ff), (ff, width),
        (patch, width), (1, patch),
    ]
    return list(
        pl.pallas_call(
            functools.partial(finish_kernel, heads),
            out_shape=[jax.ShapeDtypeStruct(shape, F32) for shape in shapes],
            in_specs=[vmem] * len(parts),
            out_specs=[vmem] * len(shapes),
        )(*parts)
    )


def solution(mesh):
    groups, heads = mesh.shape["dp"], mesh.shape["head"]

    def local(*args):
        args = list(args)
        for i in (2, 18):
            args[i] = args[i].reshape(1, -1)
        for i in (4, 5, 6, 8):
            args[i] = args[i].reshape(-1, 128)
        for i in (13, 17):
            args[i] = args[i].T
        outs = layer_call(groups, heads, args)
        for i in (2, 3, 4, 6, 16):
            outs[i] = outs[i].reshape(-1)
        outs[11], outs[15] = outs[11].T, outs[15].T
        return tuple(outs)

    both = P(("dp", "head"), None)
    by_column, by_row = P(None, "head"), P("head", None)
    return jax.shard_map(
        local,
        mesh=mesh,
        in_specs=(both, both, P("dp"), both) + (P(),) * 5 + (by_column,) * 3
        + (by_row, by_column, by_column, by_column, by_row, P(), P()),
        out_specs=(both, both) + (P(),) * 5 + (by_column,) * 3
        + (by_row, by_column, by_column, by_column, by_row, P(), P()),
        check_vma=False,
    )
```

```python
import functools
import math

import jax
import jax.numpy as jnp
from jax import lax
from jax.experimental import pallas as pl
from jax.experimental.pallas import tpu as pltpu
from jax.sharding import PartitionSpec as P

F32 = jnp.float32
BF16 = jnp.bfloat16
EPS = 1e-06
TILE = 256
MAX_DIST = 128


def bucket_cuts(buckets, length):
    half_count = buckets // 2
    exact_count = half_count // 2
    ids = []
    for distance in range(length):
        if distance < exact_count:
            ids.append(distance)
        else:
            ids.append(
                min(
                    half_count - 1,
                    exact_count
                    + int(
                        math.log(distance / exact_count)
                        / math.log(MAX_DIST / exact_count)
                        * (half_count - exact_count)
                    ),
                )
            )
    cuts = []
    for distance in range(1, length):
        cuts += [distance] * (ids[distance] - ids[distance - 1])
    return cuts, ids[-1]


def nt(left, right):
    return lax.dot_general(left, right, (((1,), (1,)), ((), ())), preferred_element_type=F32)


def nn(left, right):
    return jnp.dot(left, right, preferred_element_type=F32)


def tn(left, right):
    return lax.dot_general(left, right, (((0,), (0,)), ((), ())), preferred_element_type=F32)


def iota(shape, dim):
    return lax.broadcasted_iota(jnp.int32, shape, dim)


def fold8(values):
    return jnp.sum(values.reshape(values.shape[0] // 8, 8, values.shape[1]), axis=0)


def row_scale(values):
    return lax.rsqrt(jnp.mean(values * values, axis=-1, keepdims=True) + EPS)


def norm_back(grad_out, unit_rows, scale, gain_row):
    d_unit = grad_out * gain_row
    spread = jnp.mean(d_unit * unit_rows, axis=-1, keepdims=True)
    return scale * (d_unit - unit_rows * spread), fold8(grad_out * unit_rows)


class Layer:
    more = None

    def __init__(self, **refs):
        self.__dict__.update(refs)

    def prepare(self, head_index):
        rows, steps = self.series.shape
        half = steps // 2
        length = self.pm.shape[0]
        patch = steps // length
        split_row = self.split[...].astype(F32)
        pick = iota((rows, split_row.shape[1]), 1) == (
            iota((rows, split_row.shape[1]), 0) + head_index * rows
        )
        split_col = jnp.sum(jnp.where(pick, split_row, 0.0), axis=1, keepdims=True)
        self.splitb[...] = jnp.broadcast_to(split_col, self.splitb.shape)
        obs = self.observed[...].astype(F32)
        series = self.series[...]
        low_half = iota((rows, steps), 1) < half

        def halves(values):
            return [
                jnp.sum(values[:, :half], axis=1, keepdims=True),
                jnp.sum(values[:, half:], axis=1, keepdims=True),
            ]

        def combine(sums):
            both = sums[0] + sums[1]
            return [split_col * one + (1.0 - split_col) * both for one in sums]

        def spread(pair):
            return jnp.where(low_half, pair[0], pair[1])

        self.halves, self.combine, self.spread = halves, combine, spread
        self.counts = combine(halves(obs))
        item_mean = [a / b for a, b in zip(combine(halves(obs * series)), self.counts)]
        centred = series - spread(item_mean)
        item_var = [a / b for a, b in zip(combine(halves(obs * centred * centred)), self.counts)]
        self.std = [jnp.sqrt(v + 1e-05) for v in item_var]
        std_full = spread(self.std)
        self.std_full, self.mean_full = std_full, spread(item_mean)
        normed = obs * centred / std_full
        self.normed[...] = normed
        self.normed_low[...] = normed.astype(BF16).astype(F32)
        self.dout_low[...] = (self.cot[...] * std_full).astype(BF16).astype(F32)
        self.pm[...] = (iota(self.pm.shape, 1) // patch == iota(self.pm.shape, 0)).astype(F32)
        fold = (iota(self.fold.shape, 1) % patch == iota(self.fold.shape, 0)).astype(BF16)
        self.fold[...] = fold
        pw = self.patch_w[...].astype(F32)
        self.row_attn, self.row_ff, self.row_final, self.row_bias = (
            jnp.concatenate(
                [source[i : i + 1, :].astype(F32) for i in range(source.shape[0])], axis=1
            )
            for source in (self.gain_attn, self.gain_ff, self.gain_final, self.patch_b)
        )
        self.ptile[...] = jnp.broadcast_to(
            pw[None], (self.ptile.shape[0] // patch, patch, pw.shape[1])
        ).reshape(self.ptile.shape).astype(BF16)
        self.htile[...] = tn(self.head_w[...], fold[:patch]).astype(BF16)
        hb = jnp.broadcast_to(self.head_b[...], (16, patch))
        self.hbias = nn(hb, fold[:patch])[0:1]

    def spread_rows(self, source, tile):
        rows_tile = TILE // self.pm.shape[0]
        mask = self.pm[...]
        pieces = [
            (source[pl.ds(tile * rows_tile + r, 1), :] * mask).astype(BF16)
            for r in range(rows_tile)
        ]
        return jnp.concatenate(pieces, axis=0)

    def gather_rows(self, target, tile, values, extra=None):
        length = self.pm.shape[0]
        mask = self.pm[...]
        for r in range(TILE // length):
            part = jnp.sum(values[r * length : (r + 1) * length] * mask, axis=0, keepdims=True)
            if extra is not None:
                part = part + extra
            target[pl.ds(tile * (TILE // length) + r, 1), :] = part

    def embed(self, tile):
        at = pl.ds(pl.multiple_of(tile * TILE, TILE), TILE)
        spread = self.spread_rows(self.normed_low, tile)
        self.p8t[:, at] = nt(self.fold[...], spread).astype(BF16)
        embedded = nn(spread, self.ptile[...]) + self.row_bias
        self.embedded[at, :] = embedded
        scale = row_scale(embedded)
        self.s_attn[at, :] = scale
        self.attn_in[at, :] = (embedded * scale * self.row_attn).astype(BF16)

    def buckets(self):
        length = self.pm.shape[0]
        lanes = 2 * length
        key = iota((length, lanes), 0)
        query = iota((length, lanes), 1) % length
        offset = key - query
        distance = jnp.abs(offset)
        table = self.tab.shape[1]
        cuts, top = bucket_cuts(table, length)
        ids = jnp.where(offset > 0, table // 2, 0)
        for cut in cuts:
            ids = ids + (distance >= cut).astype(jnp.int32)
        used = list(range(top + 1)) + list(range(table // 2, table // 2 + top + 1))
        return ids, used

    def own_table(self):
        table = self.table[...].astype(BF16)
        pick = (iota((2, 128), 1) // 64 == iota((2, 128), 0)).astype(BF16)
        self.tab[0] = tn(table, pick)

    def offsets(self, slot):
        ids, used = self.buckets()
        total = jnp.zeros(ids.shape, F32)
        for b in used:
            total = jnp.where(ids == b, self.tab[slot, b : b + 1, :], total)
        self.bias[slot] = total

    def head_masks(self):
        lane = iota((1, 128), 1)
        return (lane < 64).astype(BF16), (lane >= 64).astype(BF16)

    def attend(self, tile):
        at = pl.ds(pl.multiple_of(tile * TILE, TILE), TILE)
        length = self.pm.shape[0]
        rows_tile = TILE // length
        even, odd = self.head_masks()
        half = length // 2
        shape = (length, 2 * length)
        block = (iota(shape, 0) // half != (iota(shape, 1) % length) // half).astype(F32) * -1e30
        splits = [self.splitb[pl.ds(tile * rows_tile + r, 1), :] * block for r in range(rows_tile)]
        width = self.ctx.shape[1]
        projected = []
        for i in range(3):
            part = nn(self.attn_in[at, :], self.wq[:, i * width : (i + 1) * width]).astype(BF16)
            self.qkv[at, i * width : (i + 1) * width] = part
            projected.append(part)
        items = [(s, r) for s in range(self.slots) for r in range(rows_tile)]

        def piece(s, r, i):
            return projected[i][r * length : (r + 1) * length, s * 128 : (s + 1) * 128]

        scores = []
        for s, r in items:
            query = piece(s, r, 0)
            both = jnp.concatenate([query * even, query * odd], axis=0)
            scores.append(nt(piece(s, r, 1), both))
        turned = []
        for (s, r), score in zip(items, scores):
            score = score + (self.bias[s] + splits[r])
            top = jnp.max(score, axis=0, keepdims=True)
            raised = jnp.exp(score - top)
            probs = raised * (1.0 / jnp.sum(raised, axis=0, keepdims=True))
            self.probs[
                s, pl.ds(pl.multiple_of(tile * TILE + r * length, length), length), :
            ] = probs.astype(self.probs.dtype)
            turned.append(probs.astype(BF16))
        turned = [probs.T for probs in turned]
        mixed = [nn(probs, piece(s, r, 2)) for probs, (s, r) in zip(turned, items)]
        low_lanes = iota((1, 128), 1) < 64
        for s in range(self.slots):
            self.ctx[at, s * 128 : (s + 1) * 128] = jnp.concatenate(
                [
                    jnp.where(low_lanes, m[:length], m[length:]).astype(BF16)
                    for m in mixed[s * rows_tile : (s + 1) * rows_tile]
                ],
                axis=0,
            )

    def middle_gate(self, tile):
        at = pl.ds(pl.multiple_of(tile * TILE, TILE), TILE)
        hidden_mid = self.embedded[at, :] + nt(self.ctx[at, :], self.wo[...])
        self.hidden_mid[at, :] = hidden_mid
        ff_in = (hidden_mid * row_scale(hidden_mid) * self.row_ff).astype(BF16)
        self.ff_in[at, :] = ff_in
        self.left_t[:, at] = ff_in.T
        total = self.inner.shape[1]
        block = 256
        c = math.sqrt(2.0 / math.pi)
        for first in range(0, total, block):
            cols = slice(first, first + block)
            gate = nn(ff_in, self.wg[:, first : first + block])
            up = nn(ff_in, self.wg[:, total + first : total + first + block])
            square = gate * gate
            t = jnp.tanh(gate * (c + (c * 0.044715) * square))
            plus = 0.5 * (1.0 + t)
            act = gate * plus
            slope = plus + (0.5 * gate) * (1.0 - t * t) * (c + (3.0 * c * 0.044715) * square)
            self.inner[at, cols] = (act * up).astype(BF16)
            self.act[at, cols] = act.astype(BF16)
            self.slope[at, cols] = (up * slope).astype(BF16)

    def cotangent(self, tile):
        at = pl.ds(pl.multiple_of(tile * TILE, TILE), TILE)
        d_spread = self.spread_rows(self.dout_low, tile)
        self.d8t[:, at] = nt(self.fold[...], d_spread).astype(BF16)
        self.d_mid[at, :] = nt(d_spread, self.htile[...])

    def outputs(self, tile):
        at = pl.ds(pl.multiple_of(tile * TILE, TILE), TILE)
        self.gather_rows(
            self.output, tile, nn(self.final_in[at, :], self.htile[...]), self.hbias
        )

    def middle_down(self, tile):
        at = pl.ds(pl.multiple_of(tile * TILE, TILE), TILE)
        hidden_end = self.hidden_mid[at, :] + nt(self.inner[at, :], self.wd[...])
        final_scale = row_scale(hidden_end)
        final_unit = hidden_end * final_scale
        gain_final = self.row_final
        final_in = (final_unit * gain_final).astype(BF16)
        self.final_in[at, :] = final_in
        d_end, gain_part = norm_back(self.d_mid[at, :], final_unit, final_scale, gain_final)
        self.g_final[...] += gain_part
        d_low = d_end.astype(BF16)
        self.d_end_low[at, :] = d_low
        self.right_t[:, at] = d_low.T
        self.d_mid[at, :] = d_end

    def inner_back(self, tile):
        at = pl.ds(pl.multiple_of(tile * TILE, TILE), TILE)
        d_low = self.d_end_low[at, :]
        total = self.inner.shape[1]
        block = 256
        for first in range(0, total, block):
            cols = slice(first, first + block)
            d_inner = nn(d_low, self.wd[:, cols])
            d_gate = (d_inner * self.slope[at, cols].astype(F32)).astype(BF16)
            d_up = (d_inner * self.act[at, cols].astype(F32)).astype(BF16)
            self.dgu[at, cols] = d_gate
            self.dgu[at, total + first : total + first + block] = d_up

    def middle_back(self, tile):
        at = pl.ds(pl.multiple_of(tile * TILE, TILE), TILE)
        d_in = nt(self.dgu[at, :], self.wg[...])
        hidden_mid = self.hidden_mid[at, :]
        ff_scale = row_scale(hidden_mid)
        d_norm, gain_part = norm_back(d_in, hidden_mid * ff_scale, ff_scale, self.row_ff)
        self.g_ff[...] += gain_part
        d_mid = self.d_mid[at, :] + d_norm
        self.d_mid[at, :] = d_mid
        d_mid_low = d_mid.astype(BF16)
        self.right_t[:, at] = d_mid_low.T
        self.d_ctx[at, :] = nn(d_mid_low, self.wo[...]).astype(BF16)

    def attend_back(self, tile):
        at = pl.ds(pl.multiple_of(tile * TILE, TILE), TILE)
        self.left_t[:, at] = self.attn_in[at, :].T
        width = self.ctx.shape[1]
        length = self.pm.shape[0]
        rows_tile = TILE // length
        even, odd = self.head_masks()
        items = [(s, r) for s in range(self.slots) for r in range(rows_tile)]
        rows = [
            pl.ds(pl.multiple_of(tile * TILE + r * length, length), length)
            for r in range(rows_tile)
        ]

        def piece(s, r, i):
            return self.qkv[rows[r], i * width + s * 128 : i * width + (s + 1) * 128]

        d_both = []
        for s, r in items:
            d_ctx = self.d_ctx[rows[r], s * 128 : (s + 1) * 128]
            d_both.append(jnp.concatenate([d_ctx * even, d_ctx * odd], axis=0))
        d_probs = [nt(piece(s, r, 2), both) for (s, r), both in zip(items, d_both)]
        probs = [self.probs[s, rows[r], :] for s, r in items]
        d_value = [nn(p.astype(BF16), both) for p, both in zip(probs, d_both)]
        d_scores = []
        for p, dp in zip(probs, d_probs):
            p = p.astype(F32)
            dots = jnp.sum(p * dp, axis=0, keepdims=True)
            d_scores.append((p * (dp - dots)).astype(BF16))
        turned = [d.T for d in d_scores]
        d_key = []
        for (s, r), d in zip(items, d_scores):
            query = piece(s, r, 0)
            d_key.append(nn(d, jnp.concatenate([query * even, query * odd], axis=0)))
        mixed = [nn(d, piece(s, r, 1)) for (s, r), d in zip(items, turned)]
        low_lanes = iota((1, 128), 1) < 64
        for n, (s, r) in enumerate(items):
            d_query = jnp.where(low_lanes, mixed[n][:length], mixed[n][length:])
            for i, grad in enumerate((d_query, d_key[n], d_value[n])):
                cols = slice(i * width + s * 128, i * width + (s + 1) * 128)
                self.dqkv[rows[r], cols] = grad.astype(BF16)
        for s in range(self.slots):
            total = self.dsum[s]
            for d in d_scores[s * rows_tile : (s + 1) * rows_tile]:
                total = total + d.astype(F32)
            self.dsum[s] = total

    def embed_back(self, tile):
        at = pl.ds(pl.multiple_of(tile * TILE, TILE), TILE)
        d_in = nt(self.dqkv[at, :], self.wq[...])
        scale = self.s_attn[at, :]
        d_norm, gain_part = norm_back(
            d_in, self.embedded[at, :] * scale, scale, self.row_attn
        )
        self.g_attn[...] += gain_part
        d_embedded = (self.d_mid[at, :] + d_norm).astype(BF16)
        self.d_emb[at, :] = d_embedded
        self.g_bias[...] += fold8(d_embedded.astype(F32))
        self.gather_rows(self.d_normed, tile, nt(d_embedded, self.ptile[...]))

    def finish(self):
        obs = self.observed[...].astype(F32)
        cot = self.cot[...]
        output = self.output[...]
        std_full, mean_full = self.std_full, self.mean_full
        self.rebuilt[...] = output * std_full + mean_full
        d_normed = self.d_normed[...]
        std_grad = [
            a - b / c
            for a, b, c in zip(
                self.halves(cot * output), self.halves(d_normed * self.normed[...]), self.std
            )
        ]
        var_weight = self.combine(
            [g / (2.0 * s) / n for g, s, n in zip(std_grad, self.std, self.counts)]
        )
        centred = self.series[...] - mean_full
        d_centred = d_normed * obs / std_full + 2.0 * obs * centred * self.spread(var_weight)
        mean_grad = [a - b for a, b in zip(self.halves(cot), self.halves(d_centred))]
        mean_weight = self.combine([g / n for g, n in zip(mean_grad, self.counts)])
        self.series_grad[...] = d_centred + obs * self.spread(mean_weight)

    def head_grad(self):
        self.small[16:24, :] = nn(self.d8t[...], self.final_in[...])[0:8]

    def small_grads(self, head_index):
        small = self.small
        heads = self.slots
        self.head_grad()
        zero = jnp.zeros((4, self.embedded.shape[1]), F32)
        small[0:8, :] = jnp.concatenate(
            [jnp.sum(r[...], axis=0, keepdims=True) for r in (self.g_attn, self.g_ff, self.g_final, self.g_bias)]
            + [zero],
            axis=0,
        )
        small[8:16, :] = nn(self.p8t[...], self.d_emb[...])[0:8]
        lane = iota((8, 128), 1)
        groups = self.tab.shape[1] // 8
        pieces = [jnp.zeros((8, 128), F32) for _ in range(groups)]
        pieces[0] = jnp.where(
            lane == 2 * heads, jnp.sum(self.d8t[0:8, :].astype(F32), axis=1, keepdims=True), 0.0
        )
        ids, used = self.buckets()
        for s in range(self.slots):
            dsum = self.dsum[s]
            owner = lax.rem(head_index + s, heads)
            for b in range(self.tab.shape[1]):
                if b in used:
                    self.tgr[b : b + 1, :] = jnp.sum(
                        jnp.where(ids == b, dsum, 0.0), axis=0, keepdims=True
                    )
                else:
                    self.tgr[b : b + 1, :] = jnp.zeros((1, 128), F32)
            for g in range(groups):
                rows = self.tgr[8 * g : 8 * g + 8, :]
                for which in range(2):
                    inside = (lane < 64) if which == 0 else (lane >= 64)
                    column = jnp.sum(jnp.where(inside, rows, 0.0), axis=1, keepdims=True)
                    pieces[g] = pieces[g] + jnp.where(lane == 2 * owner + which, column, 0.0)
        small[24:32, :] = jnp.concatenate(pieces, axis=1)

    def clear(self):
        for ref in (self.g_attn, self.g_ff, self.g_final, self.g_bias):
            ref[...] = jnp.zeros(ref.shape, F32)
        self.dsum[...] = jnp.zeros(self.dsum.shape, F32)


MESH = pl.DeviceIdType.MESH


TABLE, WEIGHTS, HALVES, FIRST, QUARTERS, EIGHTHS, OWNERS, FIN, SMALL, PLANE, HEADS = range(-12, -1)


class Net:
    def __init__(self, groups, heads, send_sems, recv_sems):
        self.dp, self.head = lax.axis_index("dp"), lax.axis_index("head")
        self.bits = groups.bit_length() - 1
        self.heads = heads
        self.send_sems, self.recv_sems = send_sems, recv_sems
        self.recv_ids, self.send_ids = {}, {}

    def bit(self, which):
        return (self.dp // (1 << which)) % 2

    def across(self, *which):
        place = self.dp
        for one in which:
            place = place + (1 - 2 * self.bit(one)) * (1 << one)
        return (place, self.head)

    def beside(self, hops):
        return (self.dp, (self.head + hops) % self.heads)

    def plane(self):
        return [self.across(1), self.across(2), self.across(1, 2)]

    def partners(self):
        found = [self.beside(t) for t in range(1, self.heads)] + [self.across(1, 2)]
        return found + [self.across(b) for b in reversed(range(self.bits))]

    def greet_start(self):
        barrier = pltpu.get_barrier_semaphore()
        for partner in self.partners():
            pl.semaphore_signal(barrier, inc=1, device_id=partner, device_id_type=MESH)

    def greet_end(self):
        pl.semaphore_wait(pltpu.get_barrier_semaphore(), len(self.partners()))

    def copy(self, key, group, src, dst, device):
        recv = self.recv_ids.setdefault(key, len(self.recv_ids))
        send = self.send_ids.setdefault(group, len(self.send_ids))
        return pltpu.make_async_remote_copy(
            src_ref=src,
            dst_ref=dst,
            send_sem=self.send_sems.at[send],
            recv_sem=self.recv_sems.at[recv],
            device_id=device,
            device_id_type=MESH,
        )

    def send(self, key, group, src, dst, device):
        self.copy(key, group, src, dst, device).start()

    def arrived(self, key, group, bulk):
        self.copy(key, group, bulk, bulk, self.across(0)).wait_recv()

    def sent(self, group, bulk):
        self.copy(-1, group, bulk, bulk, self.across(0)).wait_send()


def rows_at(start, count, unit):
    return pl.ds(pl.multiple_of(start, unit), count)


class Gather:
    ORDERS = ((1, 2, 0), (2, 1, 0))

    def __init__(self, net, ref, name, first, width):
        self.net, self.ref, self.name = net, ref, name
        self.first, self.width = first, width
        self.heads = net.heads
        self.unit = ref.shape[0] // 16
        self.others = slice(first + width, first + self.heads * width)

    def block(self, half):
        bits = [self.net.bit(b) for b in self.ORDERS[half]]
        return bits[0] + 2 * bits[1] + 4 * bits[2]

    def span(self, half, level):
        size = 1 << level
        first = self.block(half) // size
        return rows_at((half * 8 + first * size) * self.unit, size * self.unit, self.unit)

    def start(self, ready):
        net, first, width = self.net, self.first, self.width
        ready()
        for half in range(2):
            rows = self.span(half, 0)
            for t in range(1, self.heads):
                slot = self.heads - t
                net.send(
                    (self.name, 0),
                    WEIGHTS,
                    self.ref.at[rows, first : first + width],
                    self.ref.at[rows, first + slot * width : first + (slot + 1) * width],
                    net.beside(t),
                )

    def step(self, level):
        net = self.net
        count = 2 * self.unit << max(level - 1, 0)
        net.arrived((self.name, level), WEIGHTS, self.ref.at[0:count, self.others])
        if level < 3:
            for half in range(2):
                place = self.ref.at[self.span(half, level), self.others]
                net.send(
                    (self.name, level + 1),
                    WEIGHTS,
                    place,
                    place,
                    net.across(self.ORDERS[half][level]),
                )


class Reduce:
    ORDERS = ((1, 2), (2, 1))

    def __init__(self, net, refs, name, first, width):
        self.__dict__.update(refs)
        self.net, self.name = net, name
        self.heads = net.heads
        self.width = width
        self.columns = slice(first, first + self.heads * width)
        self.summed = self.columns
        self.fin_columns = slice(first // self.heads, first // self.heads + width)

    def slots(self, s):
        first = self.columns.start + s * self.width
        return slice(first, first + self.width)

    def partner(self, left_t, right):
        net, cols = self.net, self.columns
        count = self.own.shape[0]
        rows = rows_at((1 - net.bit(0)) * count, count, count)
        self.snd0[:, cols] = nn(left_t[rows, :], right[...]).astype(BF16)
        net.send(
            (self.name, 4), HALVES, self.snd0.at[:, cols], self.rcv0.at[:, cols], net.across(0)
        )

    def mine(self, left_t, right):
        count = self.own.shape[0]
        rows = rows_at(self.net.bit(0) * count, count, count)
        self.own[:, self.columns] = nn(left_t[rows, :], right[...]).astype(self.own.dtype)

    def kept(self, half, level):
        count = self.own.shape[0] // 2
        start = half * count
        for step in range(level):
            count = count // 2
            start = start + self.net.bit(self.ORDERS[half][step]) * count
        return start

    def halving(self, level):
        net, cols = self.net, self.summed
        source = (self.rcv0, self.rcv1, self.rcv2)[level]
        count = self.own.shape[0] // 2 >> level
        net.arrived((self.name, 4 + level), HALVES, source.at[:, cols])
        if level < 2:
            group = (QUARTERS, EIGHTHS)[level]
            send, target = ((self.snd1, self.rcv1), (self.snd2, self.rcv2))[level]
            part = count // 2
            for half in range(2):
                away = (1 - net.bit(self.ORDERS[half][level])) * part
                place = slice(half * part, (half + 1) * part)
                send[place, cols] = (
                    self.own[rows_at(self.kept(half, level) + away, part, 32), cols].astype(F32)
                    + source[rows_at(half * count + away, part, 32), cols].astype(F32)
                ).astype(BF16)
                net.send(
                    (self.name, 5 + level),
                    group,
                    send.at[place, cols],
                    target.at[place, cols],
                    net.across(self.ORDERS[half][level]),
                )
            for half in range(2):
                stay = net.bit(self.ORDERS[half][level]) * part
                rows = rows_at(self.kept(half, level) + stay, part, 32)
                self.own[rows, cols] = (
                    self.own[rows, cols].astype(F32)
                    + source[rows_at(half * count + stay, part, 32), cols].astype(F32)
                ).astype(self.own.dtype)
        else:
            for half in range(2):
                part = slice(half * count, (half + 1) * count)
                self.sndz[part, cols] = (
                    self.own[rows_at(self.kept(half, 2), count, 32), cols].astype(F32)
                    + source[part, cols].astype(F32)
                ).astype(BF16)

    def groups(self):
        net, cols = self.net, self.summed
        for bit in range(3, net.bits):
            inbox = self.extra.at[bit - 3]
            copy = net.copy(
                (self.name, 8 + bit),
                (self.name, bit),
                self.sndz.at[:, cols],
                inbox.at[:, cols],
                net.across(bit),
            )
            copy.start()
            copy.wait()
            self.sndz[:, cols] = (
                self.sndz[:, cols].astype(F32) + inbox[:, cols].astype(F32)
            ).astype(BF16)

    def owners(self):
        net = self.net
        for s in range(1, self.heads):
            net.send(
                (self.name, 7),
                OWNERS,
                self.sndz.at[:, self.slots(s)],
                self.rcvz.at[s - 1, :, self.fin_columns],
                net.beside(s),
            )

    def place(self, half, level):
        net = self.net
        quarter = self.fin.shape[0] // 4
        count = quarter // 4
        start = net.bit(0) * 2 * quarter + half * quarter
        order = self.ORDERS[half]
        start = start + net.bit(order[0]) * 2 * count
        if level == 0:
            return rows_at(start + net.bit(order[1]) * count, count, count)
        return rows_at(start, 2 * count, count)

    def owned(self, apart=True):
        net, fin = self.net, self.fin_columns
        count = self.sndz.shape[0] // 2
        if apart:
            net.arrived((self.name, 7), OWNERS, self.rcvz.at[:, :, fin])
        for half in range(2):
            part = slice(half * count, (half + 1) * count)
            total = self.sndz[part, self.slots(0)].astype(F32)
            for s in range(1, self.heads if apart else 1):
                total = total + self.rcvz[s - 1, part, fin].astype(F32)
            rows = self.place(half, 0)
            self.fin[rows, fin] = total.astype(BF16)
            place = self.fin.at[rows, fin]
            net.send((self.name, 8), FIN, place, place, net.across(self.ORDERS[half][1]))

    def spread(self, level):
        net, fin = self.net, self.fin_columns
        rows = self.fin.shape[0]
        count = (rows // 8, rows // 4, rows // 2)[level]
        net.arrived((self.name, 8 + level), FIN, self.fin.at[0:count, fin])
        if level == 0:
            for half in range(2):
                place = self.fin.at[self.place(half, 1), fin]
                net.send((self.name, 9), FIN, place, place, net.across(self.ORDERS[half][0]))
        if level == 1:
            place = self.fin.at[rows_at(net.bit(0) * (rows // 2), rows // 2, rows // 2), fin]
            net.send((self.name, 10), FIN, place, place, net.across(0))
        if level == 2:
            pltpu.make_async_copy(
                self.fin.at[:, fin], self.fin_out.at[:, fin], self.out_sem
            ).start()

    def steps(self):
        return [
            lambda: self.halving(0),
            lambda: self.halving(1),
            lambda: (self.halving(2), self.groups(), self.owners()),
            self.owned,
            lambda: self.spread(0),
            lambda: self.spread(1),
            lambda: self.spread(2),
        ]


class ReduceFirst(Reduce):
    def __init__(self, net, refs, name, first, width, place):
        super().__init__(net, refs, name, first, width)
        self.summed = self.slots(0)
        self.inbox = slice(place * width, (place + 1) * width)

    def scatter(self):
        net = self.net
        net.arrived((self.name, 4), HALVES, self.rcv0.at[:, self.columns])
        for s in range(1, self.heads):
            cols = self.slots(s)
            self.sndf[s - 1, :, self.inbox] = (
                self.own[:, cols].astype(F32) + self.rcv0[:, cols].astype(F32)
            ).astype(BF16)
            net.send(
                (self.name, 7),
                FIRST,
                self.sndf.at[s - 1, :, self.inbox],
                self.rcvf.at[s - 1, :, self.inbox],
                net.beside(s),
            )

    def gathered(self):
        net, cols = self.net, self.summed
        net.arrived((self.name, 7), FIRST, self.rcvf.at[:, :, self.inbox])
        part = self.own.shape[0] // 4
        for stays in (False, True):
            for half in range(2):
                bit = net.bit(self.ORDERS[half][0])
                rows = rows_at((2 * half + (bit if stays else 1 - bit)) * part, part, 32)
                total = self.own[rows, cols].astype(F32) + self.rcv0[rows, cols].astype(F32)
                for s in range(1, self.heads):
                    total = total + self.rcvf[s - 1, rows, self.inbox].astype(F32)
                if stays:
                    self.own[rows, cols] = total.astype(BF16)
                else:
                    place = slice(half * part, (half + 1) * part)
                    self.snd1[place, cols] = total.astype(BF16)
                    net.send(
                        (self.name, 5),
                        QUARTERS,
                        self.snd1.at[place, cols],
                        self.rcv1.at[place, cols],
                        net.across(self.ORDERS[half][0]),
                    )

    def steps(self):
        return [
            self.scatter,
            self.gathered,
            lambda: self.halving(1),
            lambda: (self.halving(2), self.groups(), self.owned(False)),
            lambda: self.spread(0),
            lambda: self.spread(1),
            lambda: self.spread(2),
        ]


class Total:
    def __init__(self, net, small, core_in, plane, more, across):
        self.net, self.small, self.core_in = net, small, core_in
        self.plane, self.more, self.heads = plane, more, across

    def start(self):
        net = self.net
        net.send(SMALL, SMALL, self.small, self.core_in, net.across(0))

    def cores(self):
        net = self.net
        net.arrived(SMALL, SMALL, self.core_in)
        here = net.bit(1) + 2 * net.bit(2)
        self.plane[here] = (self.small[...] + self.core_in[...]).astype(BF16)
        for partner in net.plane():
            net.send(PLANE, PLANE, self.plane.at[here], self.plane.at[here], partner)

    def chips(self):
        net = self.net
        net.arrived(PLANE, PLANE, self.plane.at[0:3])
        total = self.added(self.plane, 4)
        for bit in range(3, net.bits):
            mine, theirs = self.more.at[2 * (bit - 3)], self.more.at[2 * (bit - 3) + 1]
            mine[...] = total.astype(BF16)
            copy = net.copy((SMALL, bit), (SMALL, bit), mine, theirs, net.across(bit))
            copy.start()
            copy.wait()
            total = mine[...].astype(F32) + theirs[...].astype(F32)
        self.heads[net.head] = total.astype(BF16)
        for t in range(1, net.heads):
            place = self.heads.at[net.head]
            net.send(HEADS, HEADS, place, place, net.beside(t))

    def done(self):
        net = self.net
        net.arrived(HEADS, HEADS, self.heads.at[1 : net.heads])
        return self.added(self.heads, net.heads)

    def added(self, ref, count):
        total = ref[0].astype(F32)
        for i in range(1, count):
            total = total + ref[i].astype(F32)
        return total


def loop(count, body):
    def once(i, carry):
        body(i)
        return carry

    lax.fori_loop(0, count, once, 0)


CHUNKS = 10
Q, K, V, O, G1, G2, U1, U2, D1, D2 = range(CHUNKS)
EARLY = (D1, D2)
ORDER = (
    1, 2, 4, 5, 6, 7, 0, 42, 56, 70, 84, 3, 43, 98, 57, 126, 71, 112, 44, 85, 140, 58, 99, 154, 72,
    45, 127, 168, 86, 46, 113, 59, 100, 60, 141, 73, 128, 155, 74, 8, 87, 169, 114, 9, 101, 88,
    142, 10, 102, 129, 156, 11, 170, 130, 115, 143, 116, 157, 144, 12, 13, 14, 171, 158, 15, 172,
    16, 17, 18, 19, 159, 173, 160, 174, 20, 21, 161, 22, 23, 103, 117, 175, 131, 145, 104, 118,
    132, 105, 146, 119, 24, 133, 25, 147, 26, 27, 106, 89, 90, 28, 120, 29, 91, 134, 30, 31, 47,
    148, 61, 75, 107, 48, 62, 76, 121, 49, 32, 77, 92, 63, 33, 135, 34, 50, 176, 108, 162, 149, 35,
    78, 122, 38, 93, 36, 64, 136, 39, 37, 51, 177, 109, 150, 163, 79, 123, 65, 137, 94, 178, 40,
    110, 151, 52, 164, 124, 138, 95, 111, 80, 125, 139, 179, 66, 152, 53, 165, 153, 81, 96, 180,
    97, 67, 54, 181, 166, 41, 55, 82, 167, 83, 68, 69,
)


def inputs(
    series, observed, split, cot, gain_attn, gain_ff, gain_final, patch_w, patch_b, wq_in, wk_in,
    wv_in, wo_in, table, wg_in, wu_in, wd_in, head_w, head_b, rebuilt, series_grad, sums, fin_out,
):
    return locals()


def layer_kernel(groups, heads, names, *refs):
    count = len(refs) - len(names) - 4
    named = inputs(*refs[:count])
    named.update(zip(names, refs[count:]))
    send_sems, recv_sems, local_sems, out_sem = refs[-4:]
    layer = Layer(slots=heads, **named)
    weights, dgu, fin = layer.weights, layer.dgu, layer.fin
    width = layer.wq_in.shape[1]
    block = heads * width
    layer.wq = weights.at[:, Q * block : O * block]
    layer.wo = weights.at[:, O * block : G1 * block]
    layer.wg = weights.at[:, G1 * block : D1 * block]
    layer.wd = weights.at[:, D1 * block :]
    layer.dqkv = dgu.at[:, 0 : O * block]
    layer.d_emb = layer.ff_in
    tiles = layer.embedded.shape[0] // TILE
    net = Net(groups, heads, send_sems, recv_sems)
    left, right = layer.left_t, layer.right_t

    def place(chunk):
        return weights.at[:, chunk * block : chunk * block + width]

    def fetch(index, source, target):
        return pltpu.make_async_copy(source, target, local_sems.at[index])

    fetches = [
        fetch(0, layer.wq_in, place(Q)),
        fetch(1, layer.wk_in, place(K)),
        fetch(2, layer.wv_in, place(V)),
        fetch(3, layer.wo_in, layer.wo_raw),
    ]
    for i, (source, chunk) in enumerate(
        ((layer.wg_in, G1), (layer.wg_in, G2), (layer.wu_in, U1), (layer.wu_in, U2))
    ):
        cols = slice(i % 2 * width, (i % 2 + 1) * width)
        fetches.append(fetch(4 + i, source.at[:, cols], place(chunk)))
    fetches.append(fetch(8, layer.wd_in, layer.wd_raw))

    def ready(chunk):
        if chunk != D2:
            fetches[chunk].wait()
        if chunk == O:
            place(O)[...] = layer.wo_raw[...].T
        if chunk >= D1:
            first = (chunk - D1) * width
            place(chunk)[...] = layer.wd_raw[first : first + width, :].T

    def greet():
        layer.own_table()
        net.greet_end()
        for t in range(1, heads):
            net.send(TABLE, TABLE, layer.tab.at[0], layer.tab.at[heads - t], net.beside(t))

    def offsets():
        net.arrived(TABLE, TABLE, layer.tab.at[1:heads])
        loop(heads, layer.offsets)

    def sums():
        layer.sums[...] = total.done()

    total = Total(net, layer.small, layer.core_in, layer.plane, layer.more, layer.heads_in)
    tasks = [
        greet,
        lambda: (layer.clear(), layer.prepare(net.head)),
        lambda: loop(tiles, layer.embed),
        offsets,
    ]
    for body in (
        layer.cotangent,
        layer.attend,
        layer.middle_gate,
        layer.middle_down,
        layer.inner_back,
        layer.middle_back,
        layer.attend_back,
        layer.embed_back,
    ):
        tasks += [functools.partial(body, t) for t in range(tiles)]
    tasks += [
        lambda: loop(tiles, layer.outputs),
        layer.finish,
        lambda: (layer.small_grads(net.head), total.start()),
        total.cores,
        total.chips,
        sums,
    ]
    sources = [(left, layer.dqkv, i) for i in range(3)] + [(right, layer.ctx, 0)]
    sources += [(left, dgu, i) for i in range(4)] + [(right, layer.inner, i) for i in range(2)]
    named.update(out_sem=out_sem)
    for chunk, (turned, source, i) in enumerate(sources):
        gather = Gather(net, weights, chunk, chunk * block, width)
        if chunk in EARLY:
            reduce = ReduceFirst(net, named, chunk, chunk * block, width, EARLY.index(chunk))
        else:
            reduce = Reduce(net, named, chunk, chunk * block, width)
        source = source.at[:, i * block : (i + 1) * block]
        tasks += [functools.partial(gather.start, functools.partial(ready, chunk))] + [functools.partial(gather.step, level) for level in range(4)]
        tasks += [
            functools.partial(reduce.partner, turned, source),
            functools.partial(reduce.mine, turned, source),
        ]
        tasks += reduce.steps()

    net.greet_start()
    for one in fetches:
        one.start()
    for step in ORDER:
        tasks[step]()
    slots = heads - 1
    pltpu.make_async_copy(fin, layer.fin_out, out_sem).wait()
    net.sent(TABLE, layer.tab.at[1:heads])
    net.sent(WEIGHTS, weights.at[:, 0 : slots * fin.shape[1]])
    net.sent(HALVES, layer.snd0)
    net.sent(FIRST, layer.sndf)
    late = CHUNKS - len(EARLY)
    count = (late * heads + len(EARLY)) * width
    net.sent(QUARTERS, layer.snd1.at[:, 0:count])
    net.sent(EIGHTHS, layer.snd2.at[:, 0:count])
    net.sent(OWNERS, layer.sndz.at[:, 0 : slots * late * width])
    net.sent(FIN, fin.at[0 : fin.shape[0] * 7 // 8])
    net.sent(SMALL, layer.small)
    net.sent(PLANE, layer.plane.at[0:3])
    net.sent(HEADS, layer.heads_in.at[1:heads])


def finish_kernel(
    heads, rebuilt, series_grad, sums, fin, o_rebuilt, o_series, o_attn, o_ff, o_final, o_pw, o_pb, o_q, o_k, o_v, o_o, o_table, o_g, o_u, o_d, o_hw, o_hb,
):
    o_rebuilt[...] = rebuilt[...]
    o_series[...] = series_grad[...]
    for row, out in enumerate((o_attn, o_ff, o_final, o_pb)):
        out[...] = sums[row : row + 1, :]
    patch = o_pw.shape[0]
    o_pw[...] = sums[8:16, :]
    o_hw[...] = sums[16:24, :]
    lane = iota((8, 128), 1)
    column = jnp.sum(
        jnp.where(lane == 2 * heads, sums[24:32, 0:128], 0.0), axis=1, keepdims=True
    )
    o_hb[...] = jnp.sum(jnp.where(lane == iota((8, 128), 0), column, 0.0), axis=0, keepdims=True)[
        :, :patch
    ]
    head_index = lax.axis_index("head")
    for which in range(2):
        row = jnp.zeros((1, 128), F32)
        for g in range(o_table.shape[1] // 8):
            piece = sums[24:32, g * 128 : (g + 1) * 128]
            column = jnp.sum(
                jnp.where(lane == 2 * head_index + which, piece, 0.0), axis=1, keepdims=True
            )
            row = row + jnp.sum(
                jnp.where(lane == 8 * g + iota((8, 128), 0), column, 0.0), axis=0, keepdims=True
            )
        o_table[which : which + 1, :] = row[:, : o_table.shape[1]]
    first = 0
    for out, turn in ((o_q, False), (o_k, False), (o_v, False), (o_o, True), (o_g, False), (o_u, False), (o_d, True)):
        width = out.shape[0] if turn else out.shape[1]
        block = fin[:, first : first + width].astype(F32)
        out[...] = block.T if turn else block
        first += width


def layer_call(groups, heads, args):
    series = args[0]
    rows, steps = series.shape
    patch, width = args[7].shape
    length = steps // patch
    tokens = rows * length
    part = args[9].shape[1]
    ff = args[14].shape[1]
    table_heads, table_rows = args[13].shape
    total = heads * (4 * part + 3 * ff)
    bits = groups.bit_length() - 1
    scratch = dict(
        pm=((length, steps), F32), fold=((16, steps), BF16), ptile=((steps, width), BF16),
        htile=((width, steps), BF16), splitb=((rows, 128), F32), normed=((rows, steps), F32),
        normed_low=((rows, steps), F32), dout_low=((rows, steps), F32), output=((rows, steps), F32),
        d_normed=((rows, steps), F32), p8t=((16, tokens), BF16), d8t=((16, tokens), BF16),
        embedded=((tokens, width), F32), s_attn=((tokens, 1), F32), attn_in=((tokens, width), BF16),
        qkv=((tokens, heads * 3 * part), BF16), tab=((heads, table_rows, 128), F32),
        bias=((heads, length, 128), F32), probs=((heads, tokens, 128), F32),
        ctx=((tokens, heads * part), BF16), hidden_mid=((tokens, width), F32),
        ff_in=((tokens, width), BF16), inner=((tokens, heads * ff), BF16),
        act=((tokens, heads * ff), BF16), slope=((tokens, heads * ff), BF16),
        final_in=((tokens, width), BF16), d_end_low=((tokens, width), BF16),
        dgu=((tokens, heads * 2 * ff), BF16), d_mid=((tokens, width), F32),
        d_ctx=((tokens, heads * part), BF16), dsum=((heads, length, 128), F32),
        g_attn=((8, width), F32), g_ff=((8, width), F32), g_final=((8, width), F32),
        g_bias=((8, width), F32), tgr=((table_rows, 128), F32),
        left_t=((width, tokens), BF16), right_t=((width, tokens), BF16),
        weights=((width, total), BF16), own=((width // 2, total), BF16),
        snd0=((width // 2, total), BF16), rcv0=((width // 2, total), BF16),
        snd1=((width // 4, total), BF16), rcv1=((width // 4, total), BF16),
        snd2=((width // 8, total), BF16), rcv2=((width // 8, total), BF16),
        sndz=((width // 8, total), BF16), rcvz=((heads - 1, width // 8, total // heads), BF16),
        fin=((width, total // heads), BF16), small=((32, width), F32), core_in=((32, width), F32),
        plane=((4, 32, width), BF16), heads_in=((heads, 32, width), BF16),
        sndf=((heads - 1, width // 2, len(EARLY) * part), BF16),
        wo_raw=((part, width), BF16), wd_raw=((ff, width), BF16),
        rcvf=((heads - 1, width // 2, len(EARLY) * part), BF16),
    )
    extra = bits - 3
    if extra > 0:
        scratch.update(
            extra=((extra, width // 8, total), BF16), more=((2 * extra, 32, width), BF16)
        )
    copies = CHUNKS * (4 + 7 + extra) + 4 + extra + 1
    sends = 11 + (CHUNKS + 1) * extra
    outs = [((rows, steps), F32), ((rows, steps), F32), ((32, width), F32), ((width, total // heads), BF16)]
    vmem = pl.BlockSpec(memory_space=pltpu.VMEM)
    any_space = pl.BlockSpec(memory_space=pl.ANY)
    parts = pl.pallas_call(
        functools.partial(layer_kernel, groups, heads, list(scratch)),
        out_shape=[jax.ShapeDtypeStruct(*out) for out in outs],
        in_specs=[any_space if i in (9, 10, 11, 12, 14, 15, 16) else vmem for i in range(len(args))],
        out_specs=[vmem] * 3 + [any_space],
        scratch_shapes=[pltpu.VMEM(*v) for v in scratch.values()]
        + [
            pltpu.SemaphoreType.DMA((sends,)),
            pltpu.SemaphoreType.DMA((copies,)),
            pltpu.SemaphoreType.DMA((9,)),
            pltpu.SemaphoreType.DMA,
        ],
        compiler_params=pltpu.CompilerParams(
            collective_id=0, has_side_effects=True, vmem_limit_bytes=63 * 1024 * 1024
        ),
    )(*args)
    shapes = [
        (rows, steps), (rows, steps), (1, width), (1, width), (1, width), (patch, width), (1, width), (width, part), (width, part),
        (width, part), (part, width), (table_heads, table_rows), (width, ff), (width, ff), (ff, width),
        (patch, width), (1, patch),
    ]
    return list(
        pl.pallas_call(
            functools.partial(finish_kernel, heads),
            out_shape=[jax.ShapeDtypeStruct(shape, F32) for shape in shapes],
            in_specs=[vmem] * len(parts),
            out_specs=[vmem] * len(shapes),
        )(*parts)
    )


def solution(mesh):
    groups, heads = mesh.shape["dp"], mesh.shape["head"]

    def local(*args):
        args = list(args)
        for i in (2, 18):
            args[i] = args[i].reshape(1, -1)
        for i in (4, 5, 6, 8):
            args[i] = args[i].reshape(-1, 128)
        for i in (13, 17):
            args[i] = args[i].T
        outs = layer_call(groups, heads, args)
        for i in (2, 3, 4, 6, 16):
            outs[i] = outs[i].reshape(-1)
        outs[11], outs[15] = outs[11].T, outs[15].T
        return tuple(outs)

    both = P(("dp", "head"), None)
    by_column, by_row = P(None, "head"), P("head", None)
    return jax.shard_map(
        local,
        mesh=mesh,
        in_specs=(both, both, P("dp"), both) + (P(),) * 5 + (by_column,) * 3
        + (by_row, by_column, by_column, by_column, by_row, P(), P()),
        out_specs=(both, both) + (P(),) * 5 + (by_column,) * 3
        + (by_row, by_column, by_column, by_column, by_row, P(), P()),
        check_vma=False,
    )
```

```python
import functools
import math

import jax
import jax.numpy as jnp
from jax import lax
from jax.experimental import pallas as pl
from jax.experimental.pallas import tpu as pltpu
from jax.sharding import PartitionSpec as P

F32 = jnp.float32
BF16 = jnp.bfloat16
EPS = 1e-06
TILE = 256
MAX_DIST = 128


def bucket_cuts(buckets, length):
    half_count = buckets // 2
    exact_count = half_count // 2
    ids = []
    for distance in range(length):
        if distance < exact_count:
            ids.append(distance)
        else:
            ids.append(
                min(
                    half_count - 1,
                    exact_count
                    + int(
                        math.log(distance / exact_count)
                        / math.log(MAX_DIST / exact_count)
                        * (half_count - exact_count)
                    ),
                )
            )
    cuts = []
    for distance in range(1, length):
        cuts += [distance] * (ids[distance] - ids[distance - 1])
    return cuts, ids[-1]


def nt(left, right):
    return lax.dot_general(left, right, (((1,), (1,)), ((), ())), preferred_element_type=F32)


def nn(left, right):
    return jnp.dot(left, right, preferred_element_type=F32)


def tn(left, right):
    return lax.dot_general(left, right, (((0,), (0,)), ((), ())), preferred_element_type=F32)


def iota(shape, dim):
    return lax.broadcasted_iota(jnp.int32, shape, dim)


def fold8(values):
    return jnp.sum(values.reshape(values.shape[0] // 8, 8, values.shape[1]), axis=0)


def row_scale(values):
    return lax.rsqrt(jnp.mean(values * values, axis=-1, keepdims=True) + EPS)


def norm_back(grad_out, unit_rows, scale, gain_row):
    d_unit = grad_out * gain_row
    spread = jnp.mean(d_unit * unit_rows, axis=-1, keepdims=True)
    return scale * (d_unit - unit_rows * spread), fold8(grad_out * unit_rows)


class Layer:
    more = None

    def __init__(self, **refs):
        self.__dict__.update(refs)

    def prepare(self, head_index):
        rows, steps = self.series.shape
        half = steps // 2
        length = self.pm.shape[0]
        patch = steps // length
        split_row = self.split[...].astype(F32)
        pick = iota((rows, split_row.shape[1]), 1) == (
            iota((rows, split_row.shape[1]), 0) + head_index * rows
        )
        split_col = jnp.sum(jnp.where(pick, split_row, 0.0), axis=1, keepdims=True)
        self.splitb[...] = jnp.broadcast_to(split_col, self.splitb.shape)
        obs = self.observed[...].astype(F32)
        series = self.series[...]
        low_half = iota((rows, steps), 1) < half

        def halves(values):
            return [
                jnp.sum(values[:, :half], axis=1, keepdims=True),
                jnp.sum(values[:, half:], axis=1, keepdims=True),
            ]

        def combine(sums):
            both = sums[0] + sums[1]
            return [split_col * one + (1.0 - split_col) * both for one in sums]

        def spread(pair):
            return jnp.where(low_half, pair[0], pair[1])

        self.halves, self.combine, self.spread = halves, combine, spread
        self.counts = combine(halves(obs))
        item_mean = [a / b for a, b in zip(combine(halves(obs * series)), self.counts)]
        centred = series - spread(item_mean)
        item_var = [a / b for a, b in zip(combine(halves(obs * centred * centred)), self.counts)]
        self.std = [jnp.sqrt(v + 1e-05) for v in item_var]
        std_full = spread(self.std)
        self.std_full, self.mean_full = std_full, spread(item_mean)
        normed = obs * centred / std_full
        self.normed[...] = normed
        self.normed_low[...] = normed.astype(BF16).astype(F32)
        self.dout_low[...] = (self.cot[...] * std_full).astype(BF16).astype(F32)
        self.pm[...] = (iota(self.pm.shape, 1) // patch == iota(self.pm.shape, 0)).astype(F32)
        fold = (iota(self.fold.shape, 1) % patch == iota(self.fold.shape, 0)).astype(BF16)
        self.fold[...] = fold
        pw = self.patch_w[...].astype(F32)
        self.row_attn, self.row_ff, self.row_final, self.row_bias = (
            jnp.concatenate(
                [source[i : i + 1, :].astype(F32) for i in range(source.shape[0])], axis=1
            )
            for source in (self.gain_attn, self.gain_ff, self.gain_final, self.patch_b)
        )
        self.ptile[...] = jnp.broadcast_to(
            pw[None], (self.ptile.shape[0] // patch, patch, pw.shape[1])
        ).reshape(self.ptile.shape).astype(BF16)
        self.htile[...] = tn(self.head_w[...], fold[:patch]).astype(BF16)
        hb = jnp.broadcast_to(self.head_b[...], (16, patch))
        self.hbias = nn(hb, fold[:patch])[0:1]

    def spread_rows(self, source, tile):
        rows_tile = TILE // self.pm.shape[0]
        mask = self.pm[...]
        pieces = [
            (source[pl.ds(tile * rows_tile + r, 1), :] * mask).astype(BF16)
            for r in range(rows_tile)
        ]
        return jnp.concatenate(pieces, axis=0)

    def gather_rows(self, target, tile, values, extra=None):
        length = self.pm.shape[0]
        mask = self.pm[...]
        for r in range(TILE // length):
            part = jnp.sum(values[r * length : (r + 1) * length] * mask, axis=0, keepdims=True)
            if extra is not None:
                part = part + extra
            target[pl.ds(tile * (TILE // length) + r, 1), :] = part

    def embed(self, tile):
        at = pl.ds(pl.multiple_of(tile * TILE, TILE), TILE)
        spread = self.spread_rows(self.normed_low, tile)
        self.p8t[:, at] = nt(self.fold[...], spread).astype(BF16)
        embedded = nn(spread, self.ptile[...]) + self.row_bias
        self.embedded[at, :] = embedded
        scale = row_scale(embedded)
        self.s_attn[at, :] = scale
        self.attn_in[at, :] = (embedded * scale * self.row_attn).astype(BF16)

    def buckets(self):
        length = self.pm.shape[0]
        lanes = 2 * length
        key = iota((length, lanes), 0)
        query = iota((length, lanes), 1) % length
        offset = key - query
        distance = jnp.abs(offset)
        table = self.tab.shape[1]
        cuts, top = bucket_cuts(table, length)
        ids = jnp.where(offset > 0, table // 2, 0)
        for cut in cuts:
            ids = ids + (distance >= cut).astype(jnp.int32)
        used = list(range(top + 1)) + list(range(table // 2, table // 2 + top + 1))
        return ids, used

    def own_table(self):
        table = self.table[...].astype(BF16)
        pick = (iota((2, 128), 1) // 64 == iota((2, 128), 0)).astype(BF16)
        self.tab[0] = tn(table, pick)

    def offsets(self, slot):
        ids, used = self.buckets()
        total = jnp.zeros(ids.shape, F32)
        for b in used:
            total = jnp.where(ids == b, self.tab[slot, b : b + 1, :], total)
        self.bias[slot] = total

    def head_masks(self):
        lane = iota((1, 128), 1)
        return (lane < 64).astype(BF16), (lane >= 64).astype(BF16)

    def project(self, at, i):
        width = self.ctx.shape[1]
        part = nn(self.attn_in[at, :], self.wq[:, i * width : (i + 1) * width]).astype(BF16)
        self.qkv[at, i * width : (i + 1) * width] = part
        return part

    def weigh(self, tile):
        at = pl.ds(pl.multiple_of(tile * TILE, TILE), TILE)
        length = self.pm.shape[0]
        rows_tile = TILE // length
        even, odd = self.head_masks()
        half = length // 2
        shape = (length, 2 * length)
        block = (iota(shape, 0) // half != (iota(shape, 1) % length) // half).astype(F32) * -1e30
        splits = [self.splitb[pl.ds(tile * rows_tile + r, 1), :] * block for r in range(rows_tile)]
        projected = [self.project(at, i) for i in range(2)]
        items = [(s, r) for s in range(self.slots) for r in range(rows_tile)]

        def piece(s, r, i):
            return projected[i][r * length : (r + 1) * length, s * 128 : (s + 1) * 128]

        scores = []
        for s, r in items:
            query = piece(s, r, 0)
            both = jnp.concatenate([query * even, query * odd], axis=0)
            scores.append(nt(piece(s, r, 1), both))
        for (s, r), score in zip(items, scores):
            score = score + (self.bias[s] + splits[r])
            top = jnp.max(score, axis=0, keepdims=True)
            raised = jnp.exp(score - top)
            probs = raised * (1.0 / jnp.sum(raised, axis=0, keepdims=True))
            self.probs[
                s, pl.ds(pl.multiple_of(tile * TILE + r * length, length), length), :
            ] = probs.astype(self.probs.dtype)

    def mix(self, tile):
        at = pl.ds(pl.multiple_of(tile * TILE, TILE), TILE)
        length = self.pm.shape[0]
        rows_tile = TILE // length
        value = self.project(at, 2)
        items = [(s, r) for s in range(self.slots) for r in range(rows_tile)]
        turned = []
        for s, r in items:
            rows = pl.ds(pl.multiple_of(tile * TILE + r * length, length), length)
            turned.append(self.probs[s, rows, :].astype(BF16).T)
        mixed = [
            nn(probs, value[r * length : (r + 1) * length, s * 128 : (s + 1) * 128])
            for probs, (s, r) in zip(turned, items)
        ]
        low_lanes = iota((1, 128), 1) < 64
        for s in range(self.slots):
            self.ctx[at, s * 128 : (s + 1) * 128] = jnp.concatenate(
                [
                    jnp.where(low_lanes, m[:length], m[length:]).astype(BF16)
                    for m in mixed[s * rows_tile : (s + 1) * rows_tile]
                ],
                axis=0,
            )

    def middle_in(self, tile):
        at = pl.ds(pl.multiple_of(tile * TILE, TILE), TILE)
        hidden_mid = self.embedded[at, :] + nt(self.ctx[at, :], self.wo[...])
        self.hidden_mid[at, :] = hidden_mid
        ff_in = (hidden_mid * row_scale(hidden_mid) * self.row_ff).astype(BF16)
        self.ff_in[at, :] = ff_in
        self.left_t[:, at] = ff_in.T

    def middle_gate(self, which, tile):
        at = pl.ds(pl.multiple_of(tile * TILE, TILE), TILE)
        ff_in = self.ff_in[at, :]
        total = self.inner.shape[1]
        block = 256
        c = math.sqrt(2.0 / math.pi)
        for first in range(which * total // 2, (which + 1) * total // 2, block):
            cols = slice(first, first + block)
            gate = nn(ff_in, self.wg[:, first : first + block])
            up = nn(ff_in, self.wg[:, total + first : total + first + block])
            square = gate * gate
            t = jnp.tanh(gate * (c + (c * 0.044715) * square))
            plus = 0.5 * (1.0 + t)
            act = gate * plus
            slope = plus + (0.5 * gate) * (1.0 - t * t) * (c + (3.0 * c * 0.044715) * square)
            self.inner[at, cols] = (act * up).astype(BF16)
            self.act[at, cols] = act.astype(BF16)
            self.slope[at, cols] = (up * slope).astype(BF16)

    def cotangent(self, tile):
        at = pl.ds(pl.multiple_of(tile * TILE, TILE), TILE)
        d_spread = self.spread_rows(self.dout_low, tile)
        self.d8t[:, at] = nt(self.fold[...], d_spread).astype(BF16)
        self.d_mid[at, :] = nt(d_spread, self.htile[...])

    def outputs(self, tile):
        at = pl.ds(pl.multiple_of(tile * TILE, TILE), TILE)
        self.gather_rows(
            self.output, tile, nn(self.final_in[at, :], self.htile[...]), self.hbias
        )

    def middle_down(self, tile):
        at = pl.ds(pl.multiple_of(tile * TILE, TILE), TILE)
        hidden_end = self.hidden_mid[at, :] + nt(self.inner[at, :], self.wd[...])
        final_scale = row_scale(hidden_end)
        final_unit = hidden_end * final_scale
        gain_final = self.row_final
        final_in = (final_unit * gain_final).astype(BF16)
        self.final_in[at, :] = final_in
        d_end, gain_part = norm_back(self.d_mid[at, :], final_unit, final_scale, gain_final)
        self.g_final[...] += gain_part
        d_low = d_end.astype(BF16)
        self.d_end_low[at, :] = d_low
        self.right_t[:, at] = d_low.T
        self.d_mid[at, :] = d_end

    def inner_back(self, tile):
        at = pl.ds(pl.multiple_of(tile * TILE, TILE), TILE)
        d_low = self.d_end_low[at, :]
        total = self.inner.shape[1]
        block = 256
        for first in range(0, total, block):
            cols = slice(first, first + block)
            d_inner = nn(d_low, self.wd[:, cols])
            d_gate = (d_inner * self.slope[at, cols].astype(F32)).astype(BF16)
            d_up = (d_inner * self.act[at, cols].astype(F32)).astype(BF16)
            self.dgu[at, cols] = d_gate
            self.dgu[at, total + first : total + first + block] = d_up

    def middle_back(self, tile):
        at = pl.ds(pl.multiple_of(tile * TILE, TILE), TILE)
        d_in = nt(self.dgu[at, :], self.wg[...])
        hidden_mid = self.hidden_mid[at, :]
        ff_scale = row_scale(hidden_mid)
        d_norm, gain_part = norm_back(d_in, hidden_mid * ff_scale, ff_scale, self.row_ff)
        self.g_ff[...] += gain_part
        d_mid = self.d_mid[at, :] + d_norm
        self.d_mid[at, :] = d_mid
        d_mid_low = d_mid.astype(BF16)
        self.right_t[:, at] = d_mid_low.T
        self.d_ctx[at, :] = nn(d_mid_low, self.wo[...]).astype(BF16)

    def attend_back(self, tile):
        at = pl.ds(pl.multiple_of(tile * TILE, TILE), TILE)
        self.left_t[:, at] = self.attn_in[at, :].T
        width = self.ctx.shape[1]
        length = self.pm.shape[0]
        rows_tile = TILE // length
        even, odd = self.head_masks()
        items = [(s, r) for s in range(self.slots) for r in range(rows_tile)]
        rows = [
            pl.ds(pl.multiple_of(tile * TILE + r * length, length), length)
            for r in range(rows_tile)
        ]

        def piece(s, r, i):
            return self.qkv[rows[r], i * width + s * 128 : i * width + (s + 1) * 128]

        d_both = []
        for s, r in items:
            d_ctx = self.d_ctx[rows[r], s * 128 : (s + 1) * 128]
            d_both.append(jnp.concatenate([d_ctx * even, d_ctx * odd], axis=0))
        d_probs = [nt(piece(s, r, 2), both) for (s, r), both in zip(items, d_both)]
        probs = [self.probs[s, rows[r], :] for s, r in items]
        d_value = [nn(p.astype(BF16), both) for p, both in zip(probs, d_both)]
        d_scores = []
        for p, dp in zip(probs, d_probs):
            p = p.astype(F32)
            dots = jnp.sum(p * dp, axis=0, keepdims=True)
            d_scores.append((p * (dp - dots)).astype(BF16))
        turned = [d.T for d in d_scores]
        d_key = []
        for (s, r), d in zip(items, d_scores):
            query = piece(s, r, 0)
            d_key.append(nn(d, jnp.concatenate([query * even, query * odd], axis=0)))
        mixed = [nn(d, piece(s, r, 1)) for (s, r), d in zip(items, turned)]
        low_lanes = iota((1, 128), 1) < 64
        for n, (s, r) in enumerate(items):
            d_query = jnp.where(low_lanes, mixed[n][:length], mixed[n][length:])
            for i, grad in enumerate((d_query, d_key[n], d_value[n])):
                cols = slice(i * width + s * 128, i * width + (s + 1) * 128)
                self.dqkv[rows[r], cols] = grad.astype(BF16)
        for s in range(self.slots):
            total = self.dsum[s]
            for d in d_scores[s * rows_tile : (s + 1) * rows_tile]:
                total = total + d.astype(F32)
            self.dsum[s] = total

    def embed_back(self, tile):
        at = pl.ds(pl.multiple_of(tile * TILE, TILE), TILE)
        d_in = nt(self.dqkv[at, :], self.wq[...])
        scale = self.s_attn[at, :]
        d_norm, gain_part = norm_back(
            d_in, self.embedded[at, :] * scale, scale, self.row_attn
        )
        self.g_attn[...] += gain_part
        d_embedded = (self.d_mid[at, :] + d_norm).astype(BF16)
        self.d_emb[at, :] = d_embedded
        self.g_bias[...] += fold8(d_embedded.astype(F32))
        self.gather_rows(self.d_normed, tile, nt(d_embedded, self.ptile[...]))

    def finish(self):
        obs = self.observed[...].astype(F32)
        cot = self.cot[...]
        output = self.output[...]
        std_full, mean_full = self.std_full, self.mean_full
        self.rebuilt[...] = output * std_full + mean_full
        d_normed = self.d_normed[...]
        std_grad = [
            a - b / c
            for a, b, c in zip(
                self.halves(cot * output), self.halves(d_normed * self.normed[...]), self.std
            )
        ]
        var_weight = self.combine(
            [g / (2.0 * s) / n for g, s, n in zip(std_grad, self.std, self.counts)]
        )
        centred = self.series[...] - mean_full
        d_centred = d_normed * obs / std_full + 2.0 * obs * centred * self.spread(var_weight)
        mean_grad = [a - b for a, b in zip(self.halves(cot), self.halves(d_centred))]
        mean_weight = self.combine([g / n for g, n in zip(mean_grad, self.counts)])
        self.series_grad[...] = d_centred + obs * self.spread(mean_weight)

    def head_grad(self):
        self.small[16:24, :] = nn(self.d8t[...], self.final_in[...])[0:8]

    def small_grads(self, head_index):
        small = self.small
        heads = self.slots
        self.head_grad()
        zero = jnp.zeros((4, self.embedded.shape[1]), F32)
        small[0:8, :] = jnp.concatenate(
            [jnp.sum(r[...], axis=0, keepdims=True) for r in (self.g_attn, self.g_ff, self.g_final, self.g_bias)]
            + [zero],
            axis=0,
        )
        small[8:16, :] = nn(self.p8t[...], self.d_emb[...])[0:8]
        lane = iota((8, 128), 1)
        groups = self.tab.shape[1] // 8
        pieces = [jnp.zeros((8, 128), F32) for _ in range(groups)]
        pieces[0] = jnp.where(
            lane == 2 * heads, jnp.sum(self.d8t[0:8, :].astype(F32), axis=1, keepdims=True), 0.0
        )
        ids, used = self.buckets()
        for s in range(self.slots):
            dsum = self.dsum[s]
            owner = lax.rem(head_index + s, heads)
            for b in range(self.tab.shape[1]):
                if b in used:
                    self.tgr[b : b + 1, :] = jnp.sum(
                        jnp.where(ids == b, dsum, 0.0), axis=0, keepdims=True
                    )
                else:
                    self.tgr[b : b + 1, :] = jnp.zeros((1, 128), F32)
            for g in range(groups):
                rows = self.tgr[8 * g : 8 * g + 8, :]
                for which in range(2):
                    inside = (lane < 64) if which == 0 else (lane >= 64)
                    column = jnp.sum(jnp.where(inside, rows, 0.0), axis=1, keepdims=True)
                    pieces[g] = pieces[g] + jnp.where(lane == 2 * owner + which, column, 0.0)
        small[24:32, :] = jnp.concatenate(pieces, axis=1)

    def clear(self):
        for ref in (self.g_attn, self.g_ff, self.g_final, self.g_bias):
            ref[...] = jnp.zeros(ref.shape, F32)
        self.dsum[...] = jnp.zeros(self.dsum.shape, F32)


MESH = pl.DeviceIdType.MESH


TABLE, WEIGHTS, HALVES, FIRST, QUARTERS, EIGHTHS, OWNERS, FIN, SMALL, PLANE, HEADS = range(-12, -1)


class Net:
    def __init__(self, groups, heads, send_sems, recv_sems):
        self.dp, self.head = lax.axis_index("dp"), lax.axis_index("head")
        self.bits = groups.bit_length() - 1
        self.heads = heads
        self.send_sems, self.recv_sems = send_sems, recv_sems
        self.recv_ids, self.send_ids = {}, {}

    def bit(self, which):
        return (self.dp // (1 << which)) % 2

    def across(self, *which):
        place = self.dp
        for one in which:
            place = place + (1 - 2 * self.bit(one)) * (1 << one)
        return (place, self.head)

    def beside(self, hops):
        return (self.dp, (self.head + hops) % self.heads)

    def plane(self):
        return [self.across(1), self.across(2), self.across(1, 2)]

    def partners(self):
        found = [self.beside(t) for t in range(1, self.heads)] + [self.across(1, 2)]
        return found + [self.across(b) for b in reversed(range(self.bits))]

    def greet_start(self):
        barrier = pltpu.get_barrier_semaphore()
        for partner in self.partners():
            pl.semaphore_signal(barrier, inc=1, device_id=partner, device_id_type=MESH)

    def greet_end(self):
        pl.semaphore_wait(pltpu.get_barrier_semaphore(), len(self.partners()))

    def copy(self, key, group, src, dst, device):
        recv = self.recv_ids.setdefault(key, len(self.recv_ids))
        send = self.send_ids.setdefault(group, len(self.send_ids))
        return pltpu.make_async_remote_copy(
            src_ref=src,
            dst_ref=dst,
            send_sem=self.send_sems.at[send],
            recv_sem=self.recv_sems.at[recv],
            device_id=device,
            device_id_type=MESH,
        )

    def send(self, key, group, src, dst, device):
        self.copy(key, group, src, dst, device).start()

    def arrived(self, key, group, bulk):
        self.copy(key, group, bulk, bulk, self.across(0)).wait_recv()

    def sent(self, group, bulk):
        self.copy(-1, group, bulk, bulk, self.across(0)).wait_send()


def rows_at(start, count, unit):
    return pl.ds(pl.multiple_of(start, unit), count)


class Gather:
    ORDERS = ((1, 2, 0), (2, 1, 0))

    def __init__(self, net, ref, name, first, width):
        self.net, self.ref, self.name = net, ref, name
        self.first, self.width = first, width
        self.heads = net.heads
        self.unit = ref.shape[0] // 16
        self.others = slice(first + width, first + self.heads * width)

    def block(self, half):
        bits = [self.net.bit(b) for b in self.ORDERS[half]]
        return bits[0] + 2 * bits[1] + 4 * bits[2]

    def span(self, half, level):
        size = 1 << level
        first = self.block(half) // size
        return rows_at((half * 8 + first * size) * self.unit, size * self.unit, self.unit)

    def start(self, ready):
        net, first, width = self.net, self.first, self.width
        ready()
        for half in range(2):
            rows = self.span(half, 0)
            for t in range(1, self.heads):
                slot = self.heads - t
                net.send(
                    (self.name, 0),
                    WEIGHTS,
                    self.ref.at[rows, first : first + width],
                    self.ref.at[rows, first + slot * width : first + (slot + 1) * width],
                    net.beside(t),
                )

    def step(self, level):
        net = self.net
        count = 2 * self.unit << max(level - 1, 0)
        net.arrived((self.name, level), WEIGHTS, self.ref.at[0:count, self.others])
        if level < 3:
            for half in range(2):
                place = self.ref.at[self.span(half, level), self.others]
                net.send(
                    (self.name, level + 1),
                    WEIGHTS,
                    place,
                    place,
                    net.across(self.ORDERS[half][level]),
                )


class Reduce:
    ORDERS = ((1, 2), (2, 1))

    def __init__(self, net, refs, name, first, width):
        self.__dict__.update(refs)
        self.net, self.name = net, name
        self.heads = net.heads
        self.width = width
        self.columns = slice(first, first + self.heads * width)
        self.summed = self.columns
        self.fin_columns = slice(first // self.heads, first // self.heads + width)

    def slots(self, s):
        first = self.columns.start + s * self.width
        return slice(first, first + self.width)

    def partner(self, left_t, right):
        net, cols = self.net, self.columns
        count = self.own.shape[0]
        rows = rows_at((1 - net.bit(0)) * count, count, count)
        self.snd0[:, cols] = nn(left_t[rows, :], right[...]).astype(BF16)
        net.send(
            (self.name, 4), HALVES, self.snd0.at[:, cols], self.rcv0.at[:, cols], net.across(0)
        )

    def mine(self, left_t, right):
        count = self.own.shape[0]
        rows = rows_at(self.net.bit(0) * count, count, count)
        self.own[:, self.columns] = nn(left_t[rows, :], right[...]).astype(self.own.dtype)

    def kept(self, half, level):
        count = self.own.shape[0] // 2
        start = half * count
        for step in range(level):
            count = count // 2
            start = start + self.net.bit(self.ORDERS[half][step]) * count
        return start

    def halving(self, level):
        net, cols = self.net, self.summed
        source = (self.rcv0, self.rcv1, self.rcv2)[level]
        count = self.own.shape[0] // 2 >> level
        net.arrived((self.name, 4 + level), HALVES, source.at[:, cols])
        if level < 2:
            group = (QUARTERS, EIGHTHS)[level]
            send, target = ((self.snd1, self.rcv1), (self.snd2, self.rcv2))[level]
            part = count // 2
            for half in range(2):
                away = (1 - net.bit(self.ORDERS[half][level])) * part
                place = slice(half * part, (half + 1) * part)
                send[place, cols] = (
                    self.own[rows_at(self.kept(half, level) + away, part, 32), cols].astype(F32)
                    + source[rows_at(half * count + away, part, 32), cols].astype(F32)
                ).astype(BF16)
                net.send(
                    (self.name, 5 + level),
                    group,
                    send.at[place, cols],
                    target.at[place, cols],
                    net.across(self.ORDERS[half][level]),
                )
            for half in range(2):
                stay = net.bit(self.ORDERS[half][level]) * part
                rows = rows_at(self.kept(half, level) + stay, part, 32)
                self.own[rows, cols] = (
                    self.own[rows, cols].astype(F32)
                    + source[rows_at(half * count + stay, part, 32), cols].astype(F32)
                ).astype(self.own.dtype)
        else:
            for half in range(2):
                part = slice(half * count, (half + 1) * count)
                self.sndz[part, cols] = (
                    self.own[rows_at(self.kept(half, 2), count, 32), cols].astype(F32)
                    + source[part, cols].astype(F32)
                ).astype(BF16)

    def groups(self):
        net, cols = self.net, self.summed
        for bit in range(3, net.bits):
            inbox = self.extra.at[bit - 3]
            copy = net.copy(
                (self.name, 8 + bit),
                (self.name, bit),
                self.sndz.at[:, cols],
                inbox.at[:, cols],
                net.across(bit),
            )
            copy.start()
            copy.wait()
            self.sndz[:, cols] = (
                self.sndz[:, cols].astype(F32) + inbox[:, cols].astype(F32)
            ).astype(BF16)

    def owners(self):
        net = self.net
        for s in range(1, self.heads):
            net.send(
                (self.name, 7),
                OWNERS,
                self.sndz.at[:, self.slots(s)],
                self.rcvz.at[s - 1, :, self.fin_columns],
                net.beside(s),
            )

    def place(self, half):
        net = self.net
        quarter = self.fin.shape[0] // 4
        count = quarter // 4
        start = net.bit(0) * 2 * quarter + half * quarter
        order = self.ORDERS[half]
        return rows_at(
            start + net.bit(order[0]) * 2 * count + net.bit(order[1]) * count, count, count
        )

    def owned(self, apart=True):
        net, fin = self.net, self.fin_columns
        count = self.sndz.shape[0] // 2
        if apart:
            net.arrived((self.name, 7), OWNERS, self.rcvz.at[:, :, fin])
        for half in range(2):
            part = slice(half * count, (half + 1) * count)
            total = self.sndz[part, self.slots(0)].astype(F32)
            for s in range(1, self.heads if apart else 1):
                total = total + self.rcvz[s - 1, part, fin].astype(F32)
            rows = self.place(half)
            self.fin[rows, fin] = total.astype(BF16)
            place = self.fin.at[rows, fin]
            for partner in net.plane():
                net.send((self.name, 8), FIN, place, place, partner)

    def spread(self, level):
        net, fin = self.net, self.fin_columns
        rows = self.fin.shape[0]
        if level == 0:
            net.arrived((self.name, 8), FIN, self.fin.at[0 : rows * 3 // 8, fin])
            place = self.fin.at[rows_at(net.bit(0) * (rows // 2), rows // 2, rows // 2), fin]
            net.send((self.name, 9), FIN, place, place, net.across(0))
        else:
            net.arrived((self.name, 9), FIN, self.fin.at[0 : rows // 2, fin])
            pltpu.make_async_copy(
                self.fin.at[:, fin], self.fin_out.at[:, fin], self.out_sem
            ).start()

    def steps(self):
        return [
            lambda: self.halving(0),
            lambda: self.halving(1),
            lambda: (self.halving(2), self.groups(), self.owners()),
            self.owned,
            lambda: self.spread(0),
            lambda: self.spread(1),
        ]


class ReduceFirst(Reduce):
    def __init__(self, net, refs, name, first, width, place):
        super().__init__(net, refs, name, first, width)
        self.summed = self.slots(0)
        self.inbox = slice(place * width, (place + 1) * width)

    def scatter(self):
        net = self.net
        net.arrived((self.name, 4), HALVES, self.rcv0.at[:, self.columns])
        for s in range(1, self.heads):
            cols = self.slots(s)
            self.sndf[s - 1, :, self.inbox] = (
                self.own[:, cols].astype(F32) + self.rcv0[:, cols].astype(F32)
            ).astype(BF16)
            net.send(
                (self.name, 7),
                FIRST,
                self.sndf.at[s - 1, :, self.inbox],
                self.rcvf.at[s - 1, :, self.inbox],
                net.beside(s),
            )

    def gathered(self):
        net, cols = self.net, self.summed
        net.arrived((self.name, 7), FIRST, self.rcvf.at[:, :, self.inbox])
        part = self.own.shape[0] // 4
        for stays in (False, True):
            for half in range(2):
                bit = net.bit(self.ORDERS[half][0])
                rows = rows_at((2 * half + (bit if stays else 1 - bit)) * part, part, 32)
                total = self.own[rows, cols].astype(F32) + self.rcv0[rows, cols].astype(F32)
                for s in range(1, self.heads):
                    total = total + self.rcvf[s - 1, rows, self.inbox].astype(F32)
                if stays:
                    self.own[rows, cols] = total.astype(BF16)
                else:
                    place = slice(half * part, (half + 1) * part)
                    self.snd1[place, cols] = total.astype(BF16)
                    net.send(
                        (self.name, 5),
                        QUARTERS,
                        self.snd1.at[place, cols],
                        self.rcv1.at[place, cols],
                        net.across(self.ORDERS[half][0]),
                    )

    def steps(self):
        return [
            self.scatter,
            self.gathered,
            lambda: self.halving(1),
            lambda: (self.halving(2), self.groups(), self.owned(False)),
            lambda: self.spread(0),
            lambda: self.spread(1),
        ]


class Total:
    def __init__(self, net, small, core_in, plane, more, across):
        self.net, self.small, self.core_in = net, small, core_in
        self.plane, self.more, self.heads = plane, more, across

    def start(self):
        net = self.net
        net.send(SMALL, SMALL, self.small, self.core_in, net.across(0))

    def cores(self):
        net = self.net
        net.arrived(SMALL, SMALL, self.core_in)
        here = net.bit(1) + 2 * net.bit(2)
        self.plane[here] = (self.small[...] + self.core_in[...]).astype(BF16)
        for partner in net.plane():
            net.send(PLANE, PLANE, self.plane.at[here], self.plane.at[here], partner)

    def chips(self):
        net = self.net
        net.arrived(PLANE, PLANE, self.plane.at[0:3])
        total = self.added(self.plane, 4)
        for bit in range(3, net.bits):
            mine, theirs = self.more.at[2 * (bit - 3)], self.more.at[2 * (bit - 3) + 1]
            mine[...] = total.astype(BF16)
            copy = net.copy((SMALL, bit), (SMALL, bit), mine, theirs, net.across(bit))
            copy.start()
            copy.wait()
            total = mine[...].astype(F32) + theirs[...].astype(F32)
        self.heads[net.head] = total.astype(BF16)
        for t in range(1, net.heads):
            place = self.heads.at[net.head]
            net.send(HEADS, HEADS, place, place, net.beside(t))

    def done(self):
        net = self.net
        net.arrived(HEADS, HEADS, self.heads.at[1 : net.heads])
        return self.added(self.heads, net.heads)

    def added(self, ref, count):
        total = ref[0].astype(F32)
        for i in range(1, count):
            total = total + ref[i].astype(F32)
        return total


def loop(count, body):
    def once(i, carry):
        body(i)
        return carry

    lax.fori_loop(0, count, once, 0)


CHUNKS = 10
Q, K, V, O, G1, G2, U1, U2, D1, D2 = range(CHUNKS)
EARLY = (D1, D2)
ORDER = (
    1, 2, 4, 5, 6, 7, 0, 54, 67, 3, 80, 93, 106, 132, 119, 145, 158, 171, 55, 68, 81, 56, 94, 69,
    107, 82, 57, 133, 95, 58, 70, 120, 108, 71, 8, 146, 134, 83, 9, 96, 159, 10, 84, 121, 172, 97,
    11, 147, 12, 13, 135, 14, 160, 109, 15, 136, 16, 17, 110, 173, 122, 18, 19, 20, 21, 148, 22,
    161, 123, 23, 149, 24, 162, 174, 25, 26, 27, 175, 28, 29, 30, 31, 163, 176, 164, 177, 32, 165,
    33, 34, 35, 111, 124, 137, 150, 112, 125, 138, 113, 151, 126, 36, 152, 37, 38, 114, 139, 39,
    127, 98, 166, 99, 178, 40, 100, 41, 115, 153, 42, 43, 59, 72, 128, 140, 85, 167, 60, 73, 86,
    101, 61, 44, 74, 154, 87, 45, 141, 102, 46, 62, 168, 179, 47, 75, 116, 50, 88, 48, 63, 51, 155,
    49, 180, 169, 142, 129, 76, 170, 103, 117, 89, 118, 64, 52, 181, 156, 77, 143, 157, 130, 90,
    144, 104, 131, 65, 105, 182, 66, 78, 183, 91, 79, 53, 92,
)


def inputs(
    series, observed, split, cot, gain_attn, gain_ff, gain_final, patch_w, patch_b, wq_in, wk_in,
    wv_in, wo_in, table, wg_in, wu_in, wd_in, head_w, head_b, rebuilt, series_grad, sums, fin_out,
):
    return locals()


def layer_kernel(groups, heads, names, *refs):
    count = len(refs) - len(names) - 4
    named = inputs(*refs[:count])
    named.update(zip(names, refs[count:]))
    send_sems, recv_sems, local_sems, out_sem = refs[-4:]
    layer = Layer(slots=heads, **named)
    weights, dgu, fin = layer.weights, layer.dgu, layer.fin
    width = layer.wq_in.shape[1]
    block = heads * width
    layer.wq = weights.at[:, Q * block : O * block]
    layer.wo = weights.at[:, O * block : G1 * block]
    layer.wg = weights.at[:, G1 * block : D1 * block]
    layer.wd = weights.at[:, D1 * block :]
    layer.dqkv = dgu.at[:, 0 : O * block]
    layer.d_emb = layer.ff_in
    tiles = layer.embedded.shape[0] // TILE
    net = Net(groups, heads, send_sems, recv_sems)
    left, right = layer.left_t, layer.right_t

    def place(chunk):
        return weights.at[:, chunk * block : chunk * block + width]

    def fetch(index, source, target):
        return pltpu.make_async_copy(source, target, local_sems.at[index])

    fetches = [
        fetch(0, layer.wq_in, place(Q)),
        fetch(1, layer.wk_in, place(K)),
        fetch(2, layer.wv_in, place(V)),
        fetch(3, layer.wo_in, layer.wo_raw),
    ]
    for i, (source, chunk) in enumerate(
        ((layer.wg_in, G1), (layer.wg_in, G2), (layer.wu_in, U1), (layer.wu_in, U2))
    ):
        cols = slice(i % 2 * width, (i % 2 + 1) * width)
        fetches.append(fetch(4 + i, source.at[:, cols], place(chunk)))
    fetches.append(fetch(8, layer.wd_in, layer.wd_raw))

    def ready(chunk):
        if chunk != D2:
            fetches[chunk].wait()
        if chunk == O:
            place(O)[...] = layer.wo_raw[...].T
        if chunk >= D1:
            first = (chunk - D1) * width
            place(chunk)[...] = layer.wd_raw[first : first + width, :].T

    def greet():
        layer.own_table()
        net.greet_end()
        for t in range(1, heads):
            net.send(TABLE, TABLE, layer.tab.at[0], layer.tab.at[heads - t], net.beside(t))

    def offsets():
        net.arrived(TABLE, TABLE, layer.tab.at[1:heads])
        loop(heads, layer.offsets)

    def sums():
        layer.sums[...] = total.done()

    total = Total(net, layer.small, layer.core_in, layer.plane, layer.more, layer.heads_in)
    tasks = [
        greet,
        lambda: (layer.clear(), layer.prepare(net.head)),
        lambda: loop(tiles, layer.embed),
        offsets,
    ]
    for body in (
        layer.cotangent,
        layer.weigh,
        layer.mix,
        layer.middle_in,
        functools.partial(layer.middle_gate, 0),
        functools.partial(layer.middle_gate, 1),
        layer.middle_down,
        layer.inner_back,
        layer.middle_back,
        layer.attend_back,
        layer.embed_back,
    ):
        tasks += [functools.partial(body, t) for t in range(tiles)]
    tasks += [
        lambda: loop(tiles, layer.outputs),
        layer.finish,
        lambda: (layer.small_grads(net.head), total.start()),
        total.cores,
        total.chips,
        sums,
    ]
    sources = [(left, layer.dqkv, i) for i in range(3)] + [(right, layer.ctx, 0)]
    sources += [(left, dgu, i) for i in range(4)] + [(right, layer.inner, i) for i in range(2)]
    named.update(out_sem=out_sem)
    for chunk, (turned, source, i) in enumerate(sources):
        gather = Gather(net, weights, chunk, chunk * block, width)
        if chunk in EARLY:
            reduce = ReduceFirst(net, named, chunk, chunk * block, width, EARLY.index(chunk))
        else:
            reduce = Reduce(net, named, chunk, chunk * block, width)
        source = source.at[:, i * block : (i + 1) * block]
        tasks += [functools.partial(gather.start, functools.partial(ready, chunk))] + [functools.partial(gather.step, level) for level in range(4)]
        tasks += [
            functools.partial(reduce.partner, turned, source),
            functools.partial(reduce.mine, turned, source),
        ]
        tasks += reduce.steps()

    net.greet_start()
    for one in fetches:
        one.start()
    for step in ORDER:
        tasks[step]()
    slots = heads - 1
    pltpu.make_async_copy(fin, layer.fin_out, out_sem).wait()
    net.sent(TABLE, layer.tab.at[1:heads])
    net.sent(WEIGHTS, weights.at[:, 0 : slots * fin.shape[1]])
    net.sent(HALVES, layer.snd0)
    net.sent(FIRST, layer.sndf)
    late = CHUNKS - len(EARLY)
    count = (late * heads + len(EARLY)) * width
    net.sent(QUARTERS, layer.snd1.at[:, 0:count])
    net.sent(EIGHTHS, layer.snd2.at[:, 0:count])
    net.sent(OWNERS, layer.sndz.at[:, 0 : slots * late * width])
    net.sent(FIN, fin.at[0 : fin.shape[0] * 7 // 8])
    net.sent(SMALL, layer.small)
    net.sent(PLANE, layer.plane.at[0:3])
    net.sent(HEADS, layer.heads_in.at[1:heads])


def finish_kernel(
    heads, rebuilt, series_grad, sums, fin, o_rebuilt, o_series, o_attn, o_ff, o_final, o_pw, o_pb, o_q, o_k, o_v, o_o, o_table, o_g, o_u, o_d, o_hw, o_hb,
):
    o_rebuilt[...] = rebuilt[...]
    o_series[...] = series_grad[...]
    for row, out in enumerate((o_attn, o_ff, o_final, o_pb)):
        out[...] = sums[row : row + 1, :]
    patch = o_pw.shape[0]
    o_pw[...] = sums[8:16, :]
    o_hw[...] = sums[16:24, :]
    lane = iota((8, 128), 1)
    column = jnp.sum(
        jnp.where(lane == 2 * heads, sums[24:32, 0:128], 0.0), axis=1, keepdims=True
    )
    o_hb[...] = jnp.sum(jnp.where(lane == iota((8, 128), 0), column, 0.0), axis=0, keepdims=True)[
        :, :patch
    ]
    head_index = lax.axis_index("head")
    for which in range(2):
        row = jnp.zeros((1, 128), F32)
        for g in range(o_table.shape[1] // 8):
            piece = sums[24:32, g * 128 : (g + 1) * 128]
            column = jnp.sum(
                jnp.where(lane == 2 * head_index + which, piece, 0.0), axis=1, keepdims=True
            )
            row = row + jnp.sum(
                jnp.where(lane == 8 * g + iota((8, 128), 0), column, 0.0), axis=0, keepdims=True
            )
        o_table[which : which + 1, :] = row[:, : o_table.shape[1]]
    first = 0
    for out, turn in ((o_q, False), (o_k, False), (o_v, False), (o_o, True), (o_g, False), (o_u, False), (o_d, True)):
        width = out.shape[0] if turn else out.shape[1]
        block = fin[:, first : first + width].astype(F32)
        out[...] = block.T if turn else block
        first += width


def layer_call(groups, heads, args):
    series = args[0]
    rows, steps = series.shape
    patch, width = args[7].shape
    length = steps // patch
    tokens = rows * length
    part = args[9].shape[1]
    ff = args[14].shape[1]
    table_heads, table_rows = args[13].shape
    total = heads * (4 * part + 3 * ff)
    bits = groups.bit_length() - 1
    scratch = dict(
        pm=((length, steps), F32), fold=((16, steps), BF16), ptile=((steps, width), BF16),
        htile=((width, steps), BF16), splitb=((rows, 128), F32), normed=((rows, steps), F32),
        normed_low=((rows, steps), F32), dout_low=((rows, steps), F32), output=((rows, steps), F32),
        d_normed=((rows, steps), F32), p8t=((16, tokens), BF16), d8t=((16, tokens), BF16),
        embedded=((tokens, width), F32), s_attn=((tokens, 1), F32), attn_in=((tokens, width), BF16),
        qkv=((tokens, heads * 3 * part), BF16), tab=((heads, table_rows, 128), F32),
        bias=((heads, length, 128), F32), probs=((heads, tokens, 128), F32),
        ctx=((tokens, heads * part), BF16), hidden_mid=((tokens, width), F32),
        ff_in=((tokens, width), BF16), inner=((tokens, heads * ff), BF16),
        act=((tokens, heads * ff), BF16), slope=((tokens, heads * ff), BF16),
        final_in=((tokens, width), BF16), d_end_low=((tokens, width), BF16),
        dgu=((tokens, heads * 2 * ff), BF16), d_mid=((tokens, width), F32),
        d_ctx=((tokens, heads * part), BF16), dsum=((heads, length, 128), F32),
        g_attn=((8, width), F32), g_ff=((8, width), F32), g_final=((8, width), F32),
        g_bias=((8, width), F32), tgr=((table_rows, 128), F32),
        left_t=((width, tokens), BF16), right_t=((width, tokens), BF16),
        weights=((width, total), BF16), own=((width // 2, total), BF16),
        snd0=((width // 2, total), BF16), rcv0=((width // 2, total), BF16),
        snd1=((width // 4, total), BF16), rcv1=((width // 4, total), BF16),
        snd2=((width // 8, total), BF16), rcv2=((width // 8, total), BF16),
        sndz=((width // 8, total), BF16), rcvz=((heads - 1, width // 8, total // heads), BF16),
        fin=((width, total // heads), BF16), small=((32, width), F32), core_in=((32, width), F32),
        plane=((4, 32, width), BF16), heads_in=((heads, 32, width), BF16),
        sndf=((heads - 1, width // 2, len(EARLY) * part), BF16),
        wo_raw=((part, width), BF16), wd_raw=((ff, width), BF16),
        rcvf=((heads - 1, width // 2, len(EARLY) * part), BF16),
    )
    extra = bits - 3
    if extra > 0:
        scratch.update(
            extra=((extra, width // 8, total), BF16), more=((2 * extra, 32, width), BF16)
        )
    copies = CHUNKS * (4 + 6 + extra) + 4 + extra + 1
    sends = 11 + (CHUNKS + 1) * extra
    outs = [((rows, steps), F32), ((rows, steps), F32), ((32, width), F32), ((width, total // heads), BF16)]
    vmem = pl.BlockSpec(memory_space=pltpu.VMEM)
    any_space = pl.BlockSpec(memory_space=pl.ANY)
    parts = pl.pallas_call(
        functools.partial(layer_kernel, groups, heads, list(scratch)),
        out_shape=[jax.ShapeDtypeStruct(*out) for out in outs],
        in_specs=[any_space if i in (9, 10, 11, 12, 14, 15, 16) else vmem for i in range(len(args))],
        out_specs=[vmem] * 3 + [any_space],
        scratch_shapes=[pltpu.VMEM(*v) for v in scratch.values()]
        + [
            pltpu.SemaphoreType.DMA((sends,)),
            pltpu.SemaphoreType.DMA((copies,)),
            pltpu.SemaphoreType.DMA((9,)),
            pltpu.SemaphoreType.DMA,
        ],
        compiler_params=pltpu.CompilerParams(
            collective_id=0, has_side_effects=True, vmem_limit_bytes=63 * 1024 * 1024
        ),
    )(*args)
    shapes = [
        (rows, steps), (rows, steps), (1, width), (1, width), (1, width), (patch, width), (1, width), (width, part), (width, part),
        (width, part), (part, width), (table_heads, table_rows), (width, ff), (width, ff), (ff, width),
        (patch, width), (1, patch),
    ]
    return list(
        pl.pallas_call(
            functools.partial(finish_kernel, heads),
            out_shape=[jax.ShapeDtypeStruct(shape, F32) for shape in shapes],
            in_specs=[vmem] * len(parts),
            out_specs=[vmem] * len(shapes),
        )(*parts)
    )


def solution(mesh):
    groups, heads = mesh.shape["dp"], mesh.shape["head"]

    def local(*args):
        args = list(args)
        for i in (2, 18):
            args[i] = args[i].reshape(1, -1)
        for i in (4, 5, 6, 8):
            args[i] = args[i].reshape(-1, 128)
        for i in (13, 17):
            args[i] = args[i].T
        outs = layer_call(groups, heads, args)
        for i in (2, 3, 4, 6, 16):
            outs[i] = outs[i].reshape(-1)
        outs[11], outs[15] = outs[11].T, outs[15].T
        return tuple(outs)

    both = P(("dp", "head"), None)
    by_column, by_row = P(None, "head"), P("head", None)
    return jax.shard_map(
        local,
        mesh=mesh,
        in_specs=(both, both, P("dp"), both) + (P(),) * 5 + (by_column,) * 3
        + (by_row, by_column, by_column, by_column, by_row, P(), P()),
        out_specs=(both, both) + (P(),) * 5 + (by_column,) * 3
        + (by_row, by_column, by_column, by_column, by_row, P(), P()),
        check_vma=False,
    )
```

```python
import functools
import math

import jax
import jax.numpy as jnp
from jax import lax
from jax.experimental import pallas as pl
from jax.experimental.pallas import tpu as pltpu
from jax.sharding import PartitionSpec as P

F32 = jnp.float32
BF16 = jnp.bfloat16
EPS = 1e-06
TILE = 256
MAX_DIST = 128


def bucket_cuts(buckets, length):
    half_count = buckets // 2
    exact_count = half_count // 2
    ids = []
    for distance in range(length):
        if distance < exact_count:
            ids.append(distance)
        else:
            ids.append(
                min(
                    half_count - 1,
                    exact_count
                    + int(
                        math.log(distance / exact_count)
                        / math.log(MAX_DIST / exact_count)
                        * (half_count - exact_count)
                    ),
                )
            )
    cuts = []
    for distance in range(1, length):
        cuts += [distance] * (ids[distance] - ids[distance - 1])
    return cuts, ids[-1]


def nt(left, right):
    return lax.dot_general(left, right, (((1,), (1,)), ((), ())), preferred_element_type=F32)


def nn(left, right):
    return jnp.dot(left, right, preferred_element_type=F32)


def tn(left, right):
    return lax.dot_general(left, right, (((0,), (0,)), ((), ())), preferred_element_type=F32)


def iota(shape, dim):
    return lax.broadcasted_iota(jnp.int32, shape, dim)


def fold8(values):
    return jnp.sum(values.reshape(values.shape[0] // 8, 8, values.shape[1]), axis=0)


def row_scale(values):
    return lax.rsqrt(jnp.mean(values * values, axis=-1, keepdims=True) + EPS)


def norm_back(grad_out, unit_rows, scale, gain_row):
    d_unit = grad_out * gain_row
    spread = jnp.mean(d_unit * unit_rows, axis=-1, keepdims=True)
    return scale * (d_unit - unit_rows * spread), fold8(grad_out * unit_rows)


class Layer:
    more = None

    def __init__(self, **refs):
        self.__dict__.update(refs)

    def prepare(self, head_index):
        rows, steps = self.series.shape
        half = steps // 2
        length = self.pm.shape[0]
        patch = steps // length
        split_row = self.split[...].astype(F32)
        pick = iota((rows, split_row.shape[1]), 1) == (
            iota((rows, split_row.shape[1]), 0) + head_index * rows
        )
        split_col = jnp.sum(jnp.where(pick, split_row, 0.0), axis=1, keepdims=True)
        self.splitb[...] = jnp.broadcast_to(split_col, self.splitb.shape)
        obs = self.observed[...].astype(F32)
        series = self.series[...]
        low_half = iota((rows, steps), 1) < half

        def halves(values):
            return [
                jnp.sum(values[:, :half], axis=1, keepdims=True),
                jnp.sum(values[:, half:], axis=1, keepdims=True),
            ]

        def combine(sums):
            both = sums[0] + sums[1]
            return [split_col * one + (1.0 - split_col) * both for one in sums]

        def spread(pair):
            return jnp.where(low_half, pair[0], pair[1])

        self.halves, self.combine, self.spread = halves, combine, spread
        self.counts = combine(halves(obs))
        item_mean = [a / b for a, b in zip(combine(halves(obs * series)), self.counts)]
        centred = series - spread(item_mean)
        item_var = [a / b for a, b in zip(combine(halves(obs * centred * centred)), self.counts)]
        self.std = [jnp.sqrt(v + 1e-05) for v in item_var]
        std_full = spread(self.std)
        self.std_full, self.mean_full = std_full, spread(item_mean)
        normed = obs * centred / std_full
        self.normed[...] = normed
        self.normed_low[...] = normed.astype(BF16).astype(F32)
        self.dout_low[...] = (self.cot[...] * std_full).astype(BF16).astype(F32)
        self.pm[...] = (iota(self.pm.shape, 1) // patch == iota(self.pm.shape, 0)).astype(F32)
        fold = (iota(self.fold.shape, 1) % patch == iota(self.fold.shape, 0)).astype(BF16)
        self.fold[...] = fold
        pw = self.patch_w[...].astype(F32)
        self.row_attn, self.row_ff, self.row_final, self.row_bias = (
            jnp.concatenate(
                [source[i : i + 1, :].astype(F32) for i in range(source.shape[0])], axis=1
            )
            for source in (self.gain_attn, self.gain_ff, self.gain_final, self.patch_b)
        )
        self.ptile[...] = jnp.broadcast_to(
            pw[None], (self.ptile.shape[0] // patch, patch, pw.shape[1])
        ).reshape(self.ptile.shape).astype(BF16)
        self.htile[...] = tn(self.head_w[...], fold[:patch]).astype(BF16)
        hb = jnp.broadcast_to(self.head_b[...], (16, patch))
        self.hbias = nn(hb, fold[:patch])[0:1]

    def spread_rows(self, source, tile):
        rows_tile = TILE // self.pm.shape[0]
        mask = self.pm[...]
        pieces = [
            (source[pl.ds(tile * rows_tile + r, 1), :] * mask).astype(BF16)
            for r in range(rows_tile)
        ]
        return jnp.concatenate(pieces, axis=0)

    def gather_rows(self, target, tile, values, extra=None):
        length = self.pm.shape[0]
        mask = self.pm[...]
        for r in range(TILE // length):
            part = jnp.sum(values[r * length : (r + 1) * length] * mask, axis=0, keepdims=True)
            if extra is not None:
                part = part + extra
            target[pl.ds(tile * (TILE // length) + r, 1), :] = part

    def embed(self, tile):
        at = pl.ds(pl.multiple_of(tile * TILE, TILE), TILE)
        spread = self.spread_rows(self.normed_low, tile)
        self.p8t[:, at] = nt(self.fold[...], spread).astype(BF16)
        embedded = nn(spread, self.ptile[...]) + self.row_bias
        self.embedded[at, :] = embedded
        scale = row_scale(embedded)
        self.s_attn[at, :] = scale
        self.attn_in[at, :] = (embedded * scale * self.row_attn).astype(BF16)

    def buckets(self):
        length = self.pm.shape[0]
        lanes = 2 * length
        key = iota((length, lanes), 0)
        query = iota((length, lanes), 1) % length
        offset = key - query
        distance = jnp.abs(offset)
        table = self.tab.shape[1]
        cuts, top = bucket_cuts(table, length)
        ids = jnp.where(offset > 0, table // 2, 0)
        for cut in cuts:
            ids = ids + (distance >= cut).astype(jnp.int32)
        used = list(range(top + 1)) + list(range(table // 2, table // 2 + top + 1))
        return ids, used

    def own_table(self):
        table = self.table[...].astype(BF16)
        pick = (iota((2, 128), 1) // 64 == iota((2, 128), 0)).astype(BF16)
        self.tab[0] = tn(table, pick)

    def offsets(self, slot):
        ids, used = self.buckets()
        total = jnp.zeros(ids.shape, F32)
        for b in used:
            total = jnp.where(ids == b, self.tab[slot, b : b + 1, :], total)
        self.bias[slot] = total

    def head_masks(self):
        lane = iota((1, 128), 1)
        return (lane < 64).astype(BF16), (lane >= 64).astype(BF16)

    def project(self, at, i):
        width = self.ctx.shape[1]
        part = nn(self.attn_in[at, :], self.wq[:, i * width : (i + 1) * width]).astype(BF16)
        self.qkv[at, i * width : (i + 1) * width] = part
        return part

    def weigh(self, tile):
        at = pl.ds(pl.multiple_of(tile * TILE, TILE), TILE)
        length = self.pm.shape[0]
        rows_tile = TILE // length
        even, odd = self.head_masks()
        half = length // 2
        shape = (length, 2 * length)
        block = (iota(shape, 0) // half != (iota(shape, 1) % length) // half).astype(F32) * -1e30
        splits = [self.splitb[pl.ds(tile * rows_tile + r, 1), :] * block for r in range(rows_tile)]
        projected = [self.project(at, i) for i in range(2)]
        items = [(s, r) for s in range(self.slots) for r in range(rows_tile)]

        def piece(s, r, i):
            return projected[i][r * length : (r + 1) * length, s * 128 : (s + 1) * 128]

        scores = []
        for s, r in items:
            query = piece(s, r, 0)
            both = jnp.concatenate([query * even, query * odd], axis=0)
            scores.append(nt(piece(s, r, 1), both))
        for (s, r), score in zip(items, scores):
            score = score + (self.bias[s] + splits[r])
            top = jnp.max(score, axis=0, keepdims=True)
            raised = jnp.exp(score - top)
            probs = raised * (1.0 / jnp.sum(raised, axis=0, keepdims=True))
            self.probs[
                s, pl.ds(pl.multiple_of(tile * TILE + r * length, length), length), :
            ] = probs.astype(self.probs.dtype)

    def mix(self, tile):
        at = pl.ds(pl.multiple_of(tile * TILE, TILE), TILE)
        length = self.pm.shape[0]
        rows_tile = TILE // length
        value = self.project(at, 2)
        items = [(s, r) for s in range(self.slots) for r in range(rows_tile)]
        turned = []
        for s, r in items:
            rows = pl.ds(pl.multiple_of(tile * TILE + r * length, length), length)
            turned.append(self.probs[s, rows, :].astype(BF16).T)
        mixed = [
            nn(probs, value[r * length : (r + 1) * length, s * 128 : (s + 1) * 128])
            for probs, (s, r) in zip(turned, items)
        ]
        low_lanes = iota((1, 128), 1) < 64
        for s in range(self.slots):
            self.ctx[at, s * 128 : (s + 1) * 128] = jnp.concatenate(
                [
                    jnp.where(low_lanes, m[:length], m[length:]).astype(BF16)
                    for m in mixed[s * rows_tile : (s + 1) * rows_tile]
                ],
                axis=0,
            )

    def middle_in(self, tile):
        at = pl.ds(pl.multiple_of(tile * TILE, TILE), TILE)
        hidden_mid = self.embedded[at, :] + nt(self.ctx[at, :], self.wo[...])
        self.hidden_mid[at, :] = hidden_mid
        ff_in = (hidden_mid * row_scale(hidden_mid) * self.row_ff).astype(BF16)
        self.ff_in[at, :] = ff_in
        self.left_t[:, at] = ff_in.T

    def middle_gate(self, which, tile):
        at = pl.ds(pl.multiple_of(tile * TILE, TILE), TILE)
        ff_in = self.ff_in[at, :]
        total = self.inner.shape[1]
        block = 256
        c = math.sqrt(2.0 / math.pi)
        for first in range(which * total // 2, (which + 1) * total // 2, block):
            cols = slice(first, first + block)
            gate = nn(ff_in, self.wg[:, first : first + block])
            up = nn(ff_in, self.wg[:, total + first : total + first + block])
            square = gate * gate
            t = jnp.tanh(gate * (c + (c * 0.044715) * square))
            plus = 0.5 * (1.0 + t)
            act = gate * plus
            slope = plus + (0.5 * gate) * (1.0 - t * t) * (c + (3.0 * c * 0.044715) * square)
            self.inner[at, cols] = (act * up).astype(BF16)
            self.act[at, cols] = act.astype(BF16)
            self.slope[at, cols] = (up * slope).astype(BF16)

    def cotangent(self, tile):
        at = pl.ds(pl.multiple_of(tile * TILE, TILE), TILE)
        d_spread = self.spread_rows(self.dout_low, tile)
        self.d8t[:, at] = nt(self.fold[...], d_spread).astype(BF16)
        self.d_mid[at, :] = nt(d_spread, self.htile[...])

    def outputs(self, tile):
        at = pl.ds(pl.multiple_of(tile * TILE, TILE), TILE)
        self.gather_rows(
            self.output, tile, nn(self.final_in[at, :], self.htile[...]), self.hbias
        )

    def middle_down(self, tile):
        at = pl.ds(pl.multiple_of(tile * TILE, TILE), TILE)
        hidden_end = self.hidden_mid[at, :] + nt(self.inner[at, :], self.wd[...])
        final_scale = row_scale(hidden_end)
        final_unit = hidden_end * final_scale
        gain_final = self.row_final
        final_in = (final_unit * gain_final).astype(BF16)
        self.final_in[at, :] = final_in
        d_end, gain_part = norm_back(self.d_mid[at, :], final_unit, final_scale, gain_final)
        self.g_final[...] += gain_part
        d_low = d_end.astype(BF16)
        self.d_end_low[at, :] = d_low
        self.right_t[:, at] = d_low.T
        self.d_mid[at, :] = d_end

    def inner_back(self, tile):
        at = pl.ds(pl.multiple_of(tile * TILE, TILE), TILE)
        d_low = self.d_end_low[at, :]
        total = self.inner.shape[1]
        block = 256
        for first in range(0, total, block):
            cols = slice(first, first + block)
            d_inner = nn(d_low, self.wd[:, cols])
            d_gate = (d_inner * self.slope[at, cols].astype(F32)).astype(BF16)
            d_up = (d_inner * self.act[at, cols].astype(F32)).astype(BF16)
            self.dgu[at, cols] = d_gate
            self.dgu[at, total + first : total + first + block] = d_up

    def middle_back(self, tile):
        at = pl.ds(pl.multiple_of(tile * TILE, TILE), TILE)
        d_in = nt(self.dgu[at, :], self.wg[...])
        hidden_mid = self.hidden_mid[at, :]
        ff_scale = row_scale(hidden_mid)
        d_norm, gain_part = norm_back(d_in, hidden_mid * ff_scale, ff_scale, self.row_ff)
        self.g_ff[...] += gain_part
        d_mid = self.d_mid[at, :] + d_norm
        self.d_mid[at, :] = d_mid
        d_mid_low = d_mid.astype(BF16)
        self.right_t[:, at] = d_mid_low.T
        self.d_ctx[at, :] = nn(d_mid_low, self.wo[...]).astype(BF16)

    def attend_back(self, tile):
        at = pl.ds(pl.multiple_of(tile * TILE, TILE), TILE)
        self.left_t[:, at] = self.attn_in[at, :].T
        width = self.ctx.shape[1]
        length = self.pm.shape[0]
        rows_tile = TILE // length
        even, odd = self.head_masks()
        items = [(s, r) for s in range(self.slots) for r in range(rows_tile)]
        rows = [
            pl.ds(pl.multiple_of(tile * TILE + r * length, length), length)
            for r in range(rows_tile)
        ]

        def piece(s, r, i):
            return self.qkv[rows[r], i * width + s * 128 : i * width + (s + 1) * 128]

        d_both = []
        for s, r in items:
            d_ctx = self.d_ctx[rows[r], s * 128 : (s + 1) * 128]
            d_both.append(jnp.concatenate([d_ctx * even, d_ctx * odd], axis=0))
        d_probs = [nt(piece(s, r, 2), both) for (s, r), both in zip(items, d_both)]
        probs = [self.probs[s, rows[r], :] for s, r in items]
        d_value = [nn(p.astype(BF16), both) for p, both in zip(probs, d_both)]
        d_scores = []
        for p, dp in zip(probs, d_probs):
            p = p.astype(F32)
            dots = jnp.sum(p * dp, axis=0, keepdims=True)
            d_scores.append((p * (dp - dots)).astype(BF16))
        turned = [d.T for d in d_scores]
        d_key = []
        for (s, r), d in zip(items, d_scores):
            query = piece(s, r, 0)
            d_key.append(nn(d, jnp.concatenate([query * even, query * odd], axis=0)))
        mixed = [nn(d, piece(s, r, 1)) for (s, r), d in zip(items, turned)]
        low_lanes = iota((1, 128), 1) < 64
        for n, (s, r) in enumerate(items):
            d_query = jnp.where(low_lanes, mixed[n][:length], mixed[n][length:])
            for i, grad in enumerate((d_query, d_key[n], d_value[n])):
                cols = slice(i * width + s * 128, i * width + (s + 1) * 128)
                self.dqkv[rows[r], cols] = grad.astype(BF16)
        for s in range(self.slots):
            total = self.dsum[s]
            for d in d_scores[s * rows_tile : (s + 1) * rows_tile]:
                total = total + d.astype(F32)
            self.dsum[s] = total

    def embed_back(self, tile):
        at = pl.ds(pl.multiple_of(tile * TILE, TILE), TILE)
        d_in = nt(self.dqkv[at, :], self.wq[...])
        scale = self.s_attn[at, :]
        d_norm, gain_part = norm_back(
            d_in, self.embedded[at, :] * scale, scale, self.row_attn
        )
        self.g_attn[...] += gain_part
        d_embedded = (self.d_mid[at, :] + d_norm).astype(BF16)
        self.d_emb[at, :] = d_embedded
        self.g_bias[...] += fold8(d_embedded.astype(F32))
        self.gather_rows(self.d_normed, tile, nt(d_embedded, self.ptile[...]))

    def finish(self):
        obs = self.observed[...].astype(F32)
        cot = self.cot[...]
        output = self.output[...]
        std_full, mean_full = self.std_full, self.mean_full
        self.rebuilt[...] = output * std_full + mean_full
        d_normed = self.d_normed[...]
        std_grad = [
            a - b / c
            for a, b, c in zip(
                self.halves(cot * output), self.halves(d_normed * self.normed[...]), self.std
            )
        ]
        var_weight = self.combine(
            [g / (2.0 * s) / n for g, s, n in zip(std_grad, self.std, self.counts)]
        )
        centred = self.series[...] - mean_full
        d_centred = d_normed * obs / std_full + 2.0 * obs * centred * self.spread(var_weight)
        mean_grad = [a - b for a, b in zip(self.halves(cot), self.halves(d_centred))]
        mean_weight = self.combine([g / n for g, n in zip(mean_grad, self.counts)])
        self.series_grad[...] = d_centred + obs * self.spread(mean_weight)

    def head_grad(self):
        self.small[16:24, :] = nn(self.d8t[...], self.final_in[...])[0:8]

    def small_grads(self, head_index):
        small = self.small
        heads = self.slots
        self.head_grad()
        zero = jnp.zeros((4, self.embedded.shape[1]), F32)
        small[0:8, :] = jnp.concatenate(
            [jnp.sum(r[...], axis=0, keepdims=True) for r in (self.g_attn, self.g_ff, self.g_final, self.g_bias)]
            + [zero],
            axis=0,
        )
        small[8:16, :] = nn(self.p8t[...], self.d_emb[...])[0:8]
        lane = iota((8, 128), 1)
        groups = self.tab.shape[1] // 8
        pieces = [jnp.zeros((8, 128), F32) for _ in range(groups)]
        pieces[0] = jnp.where(
            lane == 2 * heads, jnp.sum(self.d8t[0:8, :].astype(F32), axis=1, keepdims=True), 0.0
        )
        ids, used = self.buckets()
        for s in range(self.slots):
            dsum = self.dsum[s]
            owner = lax.rem(head_index + s, heads)
            for b in range(self.tab.shape[1]):
                if b in used:
                    self.tgr[b : b + 1, :] = jnp.sum(
                        jnp.where(ids == b, dsum, 0.0), axis=0, keepdims=True
                    )
                else:
                    self.tgr[b : b + 1, :] = jnp.zeros((1, 128), F32)
            for g in range(groups):
                rows = self.tgr[8 * g : 8 * g + 8, :]
                for which in range(2):
                    inside = (lane < 64) if which == 0 else (lane >= 64)
                    column = jnp.sum(jnp.where(inside, rows, 0.0), axis=1, keepdims=True)
                    pieces[g] = pieces[g] + jnp.where(lane == 2 * owner + which, column, 0.0)
        small[24:32, :] = jnp.concatenate(pieces, axis=1)

    def clear(self):
        for ref in (self.g_attn, self.g_ff, self.g_final, self.g_bias):
            ref[...] = jnp.zeros(ref.shape, F32)
        self.dsum[...] = jnp.zeros(self.dsum.shape, F32)


MESH = pl.DeviceIdType.MESH


TABLE, WEIGHTS, HALVES, FIRST, QUARTERS, EIGHTHS, OWNERS, FIN, SMALL, PLANE, HEADS = range(-12, -1)


class Net:
    def __init__(self, groups, heads, send_sems, recv_sems):
        self.dp, self.head = lax.axis_index("dp"), lax.axis_index("head")
        self.bits = groups.bit_length() - 1
        self.heads = heads
        self.send_sems, self.recv_sems = send_sems, recv_sems
        self.recv_ids, self.send_ids = {}, {}

    def bit(self, which):
        return (self.dp // (1 << which)) % 2

    def across(self, *which):
        place = self.dp
        for one in which:
            place = place + (1 - 2 * self.bit(one)) * (1 << one)
        return (place, self.head)

    def beside(self, hops):
        return (self.dp, (self.head + hops) % self.heads)

    def plane(self):
        return [self.across(1), self.across(2), self.across(1, 2)]

    def partners(self):
        found = [self.beside(t) for t in range(1, self.heads)] + [self.across(1, 2)]
        return found + [self.across(b) for b in reversed(range(self.bits))]

    def greet_start(self):
        barrier = pltpu.get_barrier_semaphore()
        for partner in self.partners():
            pl.semaphore_signal(barrier, inc=1, device_id=partner, device_id_type=MESH)

    def greet_end(self):
        pl.semaphore_wait(pltpu.get_barrier_semaphore(), len(self.partners()))

    def copy(self, key, group, src, dst, device):
        recv = self.recv_ids.setdefault(key, len(self.recv_ids))
        send = self.send_ids.setdefault(group, len(self.send_ids))
        return pltpu.make_async_remote_copy(
            src_ref=src,
            dst_ref=dst,
            send_sem=self.send_sems.at[send],
            recv_sem=self.recv_sems.at[recv],
            device_id=device,
            device_id_type=MESH,
        )

    def send(self, key, group, src, dst, device):
        self.copy(key, group, src, dst, device).start()

    def arrived(self, key, group, bulk):
        self.copy(key, group, bulk, bulk, self.across(0)).wait_recv()

    def sent(self, group, bulk):
        self.copy(-1, group, bulk, bulk, self.across(0)).wait_send()


def rows_at(start, count, unit):
    return pl.ds(pl.multiple_of(start, unit), count)


def far_first(heads):
    return sorted(range(1, heads), key=lambda t: -min(t, heads - t))


class Gather:
    ORDERS = ((1, 2, 0), (2, 1, 0))

    def __init__(self, net, ref, name, first, width):
        self.net, self.ref, self.name = net, ref, name
        self.first, self.width = first, width
        self.heads = net.heads
        self.unit = ref.shape[0] // 16
        self.others = slice(first + width, first + self.heads * width)

    def block(self, half):
        bits = [self.net.bit(b) for b in self.ORDERS[half]]
        return bits[0] + 2 * bits[1] + 4 * bits[2]

    def span(self, half, level):
        size = 1 << level
        first = self.block(half) // size
        return rows_at((half * 8 + first * size) * self.unit, size * self.unit, self.unit)

    def start(self, ready):
        net, first, width = self.net, self.first, self.width
        ready()
        for half in range(2):
            rows = self.span(half, 0)
            for t in far_first(self.heads):
                slot = self.heads - t
                net.send(
                    (self.name, 0),
                    WEIGHTS,
                    self.ref.at[rows, first : first + width],
                    self.ref.at[rows, first + slot * width : first + (slot + 1) * width],
                    net.beside(t),
                )

    def step(self, level):
        net = self.net
        count = 2 * self.unit << max(level - 1, 0)
        net.arrived((self.name, level), WEIGHTS, self.ref.at[0:count, self.others])
        if level < 3:
            for half in range(2):
                place = self.ref.at[self.span(half, level), self.others]
                net.send(
                    (self.name, level + 1),
                    WEIGHTS,
                    place,
                    place,
                    net.across(self.ORDERS[half][level]),
                )


class Reduce:
    ORDERS = ((1, 2), (2, 1))

    def __init__(self, net, refs, name, first, width):
        self.__dict__.update(refs)
        self.net, self.name = net, name
        self.heads = net.heads
        self.width = width
        self.columns = slice(first, first + self.heads * width)
        self.summed = self.columns
        self.fin_columns = slice(first // self.heads, first // self.heads + width)

    def slots(self, s):
        first = self.columns.start + s * self.width
        return slice(first, first + self.width)

    def partner(self, left_t, right):
        net, cols = self.net, self.columns
        count = self.own.shape[0]
        rows = rows_at((1 - net.bit(0)) * count, count, count)
        self.snd0[:, cols] = nn(left_t[rows, :], right[...]).astype(BF16)
        net.send(
            (self.name, 4), HALVES, self.snd0.at[:, cols], self.rcv0.at[:, cols], net.across(0)
        )

    def mine(self, left_t, right):
        count = self.own.shape[0]
        rows = rows_at(self.net.bit(0) * count, count, count)
        self.own[:, self.columns] = nn(left_t[rows, :], right[...]).astype(self.own.dtype)

    def kept(self, half, level):
        count = self.own.shape[0] // 2
        start = half * count
        for step in range(level):
            count = count // 2
            start = start + self.net.bit(self.ORDERS[half][step]) * count
        return start

    def halving(self, level):
        net, cols = self.net, self.summed
        source = (self.rcv0, self.rcv1, self.rcv2)[level]
        count = self.own.shape[0] // 2 >> level
        net.arrived((self.name, 4 + level), HALVES, source.at[:, cols])
        if level < 2:
            group = (QUARTERS, EIGHTHS)[level]
            send, target = ((self.snd1, self.rcv1), (self.snd2, self.rcv2))[level]
            part = count // 2
            for half in range(2):
                away = (1 - net.bit(self.ORDERS[half][level])) * part
                place = slice(half * part, (half + 1) * part)
                send[place, cols] = (
                    self.own[rows_at(self.kept(half, level) + away, part, 32), cols].astype(F32)
                    + source[rows_at(half * count + away, part, 32), cols].astype(F32)
                ).astype(BF16)
                net.send(
                    (self.name, 5 + level),
                    group,
                    send.at[place, cols],
                    target.at[place, cols],
                    net.across(self.ORDERS[half][level]),
                )
            for half in range(2):
                stay = net.bit(self.ORDERS[half][level]) * part
                rows = rows_at(self.kept(half, level) + stay, part, 32)
                self.own[rows, cols] = (
                    self.own[rows, cols].astype(F32)
                    + source[rows_at(half * count + stay, part, 32), cols].astype(F32)
                ).astype(self.own.dtype)
        else:
            for half in range(2):
                part = slice(half * count, (half + 1) * count)
                self.sndz[part, cols] = (
                    self.own[rows_at(self.kept(half, 2), count, 32), cols].astype(F32)
                    + source[part, cols].astype(F32)
                ).astype(BF16)

    def groups(self):
        net, cols = self.net, self.summed
        for bit in range(3, net.bits):
            inbox = self.extra.at[bit - 3]
            copy = net.copy(
                (self.name, 8 + bit),
                (self.name, bit),
                self.sndz.at[:, cols],
                inbox.at[:, cols],
                net.across(bit),
            )
            copy.start()
            copy.wait()
            self.sndz[:, cols] = (
                self.sndz[:, cols].astype(F32) + inbox[:, cols].astype(F32)
            ).astype(BF16)

    def owners(self):
        net = self.net
        for s in far_first(self.heads):
            net.send(
                (self.name, 7),
                OWNERS,
                self.sndz.at[:, self.slots(s)],
                self.rcvz.at[s - 1, :, self.fin_columns],
                net.beside(s),
            )

    def place(self, half):
        net = self.net
        quarter = self.fin.shape[0] // 4
        count = quarter // 4
        start = net.bit(0) * 2 * quarter + half * quarter
        order = self.ORDERS[half]
        return rows_at(
            start + net.bit(order[0]) * 2 * count + net.bit(order[1]) * count, count, count
        )

    def owned(self, apart=True):
        net, fin = self.net, self.fin_columns
        count = self.sndz.shape[0] // 2
        if apart:
            net.arrived((self.name, 7), OWNERS, self.rcvz.at[:, :, fin])
        for half in range(2):
            part = slice(half * count, (half + 1) * count)
            total = self.sndz[part, self.slots(0)].astype(F32)
            for s in range(1, self.heads if apart else 1):
                total = total + self.rcvz[s - 1, part, fin].astype(F32)
            rows = self.place(half)
            self.fin[rows, fin] = total.astype(BF16)
            place = self.fin.at[rows, fin]
            for partner in net.plane():
                net.send((self.name, 8), FIN, place, place, partner)

    def spread(self, level):
        net, fin = self.net, self.fin_columns
        rows = self.fin.shape[0]
        if level == 0:
            net.arrived((self.name, 8), FIN, self.fin.at[0 : rows * 3 // 8, fin])
            place = self.fin.at[rows_at(net.bit(0) * (rows // 2), rows // 2, rows // 2), fin]
            net.send((self.name, 9), FIN, place, place, net.across(0))
        else:
            net.arrived((self.name, 9), FIN, self.fin.at[0 : rows // 2, fin])
            pltpu.make_async_copy(
                self.fin.at[:, fin], self.fin_out.at[:, fin], self.out_sem
            ).start()

    def steps(self):
        return [
            lambda: self.halving(0),
            lambda: self.halving(1),
            lambda: (self.halving(2), self.groups(), self.owners()),
            self.owned,
            lambda: self.spread(0),
            lambda: self.spread(1),
        ]


class ReduceFirst(Reduce):
    def __init__(self, net, refs, name, first, width, place):
        super().__init__(net, refs, name, first, width)
        self.summed = self.slots(0)
        self.inbox = slice(place * width, (place + 1) * width)

    def scatter(self):
        net = self.net
        net.arrived((self.name, 4), HALVES, self.rcv0.at[:, self.columns])
        for s in range(1, self.heads):
            cols = self.slots(s)
            self.sndf[s - 1, :, self.inbox] = (
                self.own[:, cols].astype(F32) + self.rcv0[:, cols].astype(F32)
            ).astype(BF16)
            net.send(
                (self.name, 7),
                FIRST,
                self.sndf.at[s - 1, :, self.inbox],
                self.rcvf.at[s - 1, :, self.inbox],
                net.beside(s),
            )

    def gathered(self):
        net, cols = self.net, self.summed
        net.arrived((self.name, 7), FIRST, self.rcvf.at[:, :, self.inbox])
        part = self.own.shape[0] // 4
        for stays in (False, True):
            for half in range(2):
                bit = net.bit(self.ORDERS[half][0])
                rows = rows_at((2 * half + (bit if stays else 1 - bit)) * part, part, 32)
                total = self.own[rows, cols].astype(F32) + self.rcv0[rows, cols].astype(F32)
                for s in range(1, self.heads):
                    total = total + self.rcvf[s - 1, rows, self.inbox].astype(F32)
                if stays:
                    self.own[rows, cols] = total.astype(BF16)
                else:
                    place = slice(half * part, (half + 1) * part)
                    self.snd1[place, cols] = total.astype(BF16)
                    net.send(
                        (self.name, 5),
                        QUARTERS,
                        self.snd1.at[place, cols],
                        self.rcv1.at[place, cols],
                        net.across(self.ORDERS[half][0]),
                    )

    def steps(self):
        return [
            self.scatter,
            self.gathered,
            lambda: self.halving(1),
            lambda: (self.halving(2), self.groups(), self.owned(False)),
            lambda: self.spread(0),
            lambda: self.spread(1),
        ]


class Total:
    def __init__(self, net, small, core_in, plane, more, across):
        self.net, self.small, self.core_in = net, small, core_in
        self.plane, self.more, self.heads = plane, more, across

    def start(self):
        net = self.net
        net.send(SMALL, SMALL, self.small, self.core_in, net.across(0))

    def cores(self):
        net = self.net
        net.arrived(SMALL, SMALL, self.core_in)
        here = net.bit(1) + 2 * net.bit(2)
        self.plane[here] = (self.small[...] + self.core_in[...]).astype(BF16)
        for partner in net.plane():
            net.send(PLANE, PLANE, self.plane.at[here], self.plane.at[here], partner)

    def chips(self):
        net = self.net
        net.arrived(PLANE, PLANE, self.plane.at[0:3])
        total = self.added(self.plane, 4)
        for bit in range(3, net.bits):
            mine, theirs = self.more.at[2 * (bit - 3)], self.more.at[2 * (bit - 3) + 1]
            mine[...] = total.astype(BF16)
            copy = net.copy((SMALL, bit), (SMALL, bit), mine, theirs, net.across(bit))
            copy.start()
            copy.wait()
            total = mine[...].astype(F32) + theirs[...].astype(F32)
        self.heads[net.head] = total.astype(BF16)
        for t in range(1, net.heads):
            place = self.heads.at[net.head]
            net.send(HEADS, HEADS, place, place, net.beside(t))

    def done(self):
        net = self.net
        net.arrived(HEADS, HEADS, self.heads.at[1 : net.heads])
        return self.added(self.heads, net.heads)

    def added(self, ref, count):
        total = ref[0].astype(F32)
        for i in range(1, count):
            total = total + ref[i].astype(F32)
        return total


def loop(count, body):
    def once(i, carry):
        body(i)
        return carry

    lax.fori_loop(0, count, once, 0)


CHUNKS = 10
Q, K, V, O, G1, G2, U1, U2, D1, D2 = range(CHUNKS)
EARLY = (D1, D2)
ORDER = (
    1, 2, 4, 5, 6, 7, 0, 54, 67, 3, 80, 93, 106, 132, 119, 145, 158, 171, 55, 68, 81, 56, 94, 69,
    107, 82, 57, 133, 95, 58, 70, 120, 108, 71, 8, 146, 134, 83, 9, 96, 159, 10, 84, 121, 172, 97,
    11, 147, 12, 13, 135, 14, 160, 109, 15, 136, 16, 17, 110, 173, 122, 18, 19, 20, 21, 148, 22,
    161, 123, 23, 149, 24, 162, 174, 25, 26, 27, 175, 28, 29, 30, 31, 163, 176, 164, 177, 32, 165,
    33, 34, 35, 111, 124, 137, 150, 112, 125, 138, 113, 151, 126, 36, 152, 37, 38, 114, 139, 39,
    127, 98, 166, 99, 178, 40, 100, 41, 115, 153, 42, 43, 59, 72, 128, 140, 85, 167, 60, 73, 86,
    101, 61, 44, 74, 154, 87, 45, 141, 102, 46, 62, 168, 179, 47, 75, 116, 50, 88, 48, 63, 51, 155,
    49, 180, 169, 142, 129, 76, 170, 103, 117, 89, 118, 64, 52, 181, 156, 77, 143, 157, 130, 90,
    144, 104, 131, 65, 105, 182, 66, 78, 183, 91, 79, 53, 92,
)


def inputs(
    series, observed, split, cot, gain_attn, gain_ff, gain_final, patch_w, patch_b, wq_in, wk_in,
    wv_in, wo_in, table, wg_in, wu_in, wd_in, head_w, head_b, rebuilt, series_grad, sums, fin_out,
):
    return locals()


def layer_kernel(groups, heads, names, *refs):
    count = len(refs) - len(names) - 4
    named = inputs(*refs[:count])
    named.update(zip(names, refs[count:]))
    send_sems, recv_sems, local_sems, out_sem = refs[-4:]
    layer = Layer(slots=heads, **named)
    weights, dgu, fin = layer.weights, layer.dgu, layer.fin
    width = layer.wq_in.shape[1]
    block = heads * width
    layer.wq = weights.at[:, Q * block : O * block]
    layer.wo = weights.at[:, O * block : G1 * block]
    layer.wg = weights.at[:, G1 * block : D1 * block]
    layer.wd = weights.at[:, D1 * block :]
    layer.dqkv = dgu.at[:, 0 : O * block]
    layer.d_emb = layer.ff_in
    tiles = layer.embedded.shape[0] // TILE
    net = Net(groups, heads, send_sems, recv_sems)
    left, right = layer.left_t, layer.right_t

    def place(chunk):
        return weights.at[:, chunk * block : chunk * block + width]

    def fetch(index, source, target):
        return pltpu.make_async_copy(source, target, local_sems.at[index])

    fetches = [
        fetch(0, layer.wq_in, place(Q)),
        fetch(1, layer.wk_in, place(K)),
        fetch(2, layer.wv_in, place(V)),
        fetch(3, layer.wo_in, layer.wo_raw),
    ]
    for i, (source, chunk) in enumerate(
        ((layer.wg_in, G1), (layer.wg_in, G2), (layer.wu_in, U1), (layer.wu_in, U2))
    ):
        cols = slice(i % 2 * width, (i % 2 + 1) * width)
        fetches.append(fetch(4 + i, source.at[:, cols], place(chunk)))
    fetches.append(fetch(8, layer.wd_in, layer.wd_raw))

    def ready(chunk):
        if chunk != D2:
            fetches[chunk].wait()
        if chunk == O:
            place(O)[...] = layer.wo_raw[...].T
        if chunk >= D1:
            first = (chunk - D1) * width
            place(chunk)[...] = layer.wd_raw[first : first + width, :].T

    def greet():
        layer.own_table()
        net.greet_end()
        for t in range(1, heads):
            net.send(TABLE, TABLE, layer.tab.at[0], layer.tab.at[heads - t], net.beside(t))

    def offsets():
        net.arrived(TABLE, TABLE, layer.tab.at[1:heads])
        loop(heads, layer.offsets)

    def sums():
        layer.sums[...] = total.done()

    total = Total(net, layer.small, layer.core_in, layer.plane, layer.more, layer.heads_in)
    tasks = [
        greet,
        lambda: (layer.clear(), layer.prepare(net.head)),
        lambda: loop(tiles, layer.embed),
        offsets,
    ]
    for body in (
        layer.cotangent,
        layer.weigh,
        layer.mix,
        layer.middle_in,
        functools.partial(layer.middle_gate, 0),
        functools.partial(layer.middle_gate, 1),
        layer.middle_down,
        layer.inner_back,
        layer.middle_back,
        layer.attend_back,
        layer.embed_back,
    ):
        tasks += [functools.partial(body, t) for t in range(tiles)]
    tasks += [
        lambda: loop(tiles, layer.outputs),
        layer.finish,
        lambda: (layer.small_grads(net.head), total.start()),
        total.cores,
        total.chips,
        sums,
    ]
    sources = [(left, layer.dqkv, i) for i in range(3)] + [(right, layer.ctx, 0)]
    sources += [(left, dgu, i) for i in range(4)] + [(right, layer.inner, i) for i in range(2)]
    named.update(out_sem=out_sem)
    for chunk, (turned, source, i) in enumerate(sources):
        gather = Gather(net, weights, chunk, chunk * block, width)
        if chunk in EARLY:
            reduce = ReduceFirst(net, named, chunk, chunk * block, width, EARLY.index(chunk))
        else:
            reduce = Reduce(net, named, chunk, chunk * block, width)
        source = source.at[:, i * block : (i + 1) * block]
        tasks += [functools.partial(gather.start, functools.partial(ready, chunk))] + [functools.partial(gather.step, level) for level in range(4)]
        tasks += [
            functools.partial(reduce.partner, turned, source),
            functools.partial(reduce.mine, turned, source),
        ]
        tasks += reduce.steps()

    net.greet_start()
    for one in fetches:
        one.start()
    for step in ORDER:
        tasks[step]()
    slots = heads - 1
    pltpu.make_async_copy(fin, layer.fin_out, out_sem).wait()
    net.sent(TABLE, layer.tab.at[1:heads])
    net.sent(WEIGHTS, weights.at[:, 0 : slots * fin.shape[1]])
    net.sent(HALVES, layer.snd0)
    net.sent(FIRST, layer.sndf)
    late = CHUNKS - len(EARLY)
    count = (late * heads + len(EARLY)) * width
    net.sent(QUARTERS, layer.snd1.at[:, 0:count])
    net.sent(EIGHTHS, layer.snd2.at[:, 0:count])
    net.sent(OWNERS, layer.sndz.at[:, 0 : slots * late * width])
    net.sent(FIN, fin.at[0 : fin.shape[0] * 7 // 8])
    net.sent(SMALL, layer.small)
    net.sent(PLANE, layer.plane.at[0:3])
    net.sent(HEADS, layer.heads_in.at[1:heads])


def finish_kernel(
    heads, rebuilt, series_grad, sums, fin, o_rebuilt, o_series, o_attn, o_ff, o_final, o_pw, o_pb, o_q, o_k, o_v, o_o, o_table, o_g, o_u, o_d, o_hw, o_hb,
):
    o_rebuilt[...] = rebuilt[...]
    o_series[...] = series_grad[...]
    for row, out in enumerate((o_attn, o_ff, o_final, o_pb)):
        out[...] = sums[row : row + 1, :]
    patch = o_pw.shape[0]
    o_pw[...] = sums[8:16, :]
    o_hw[...] = sums[16:24, :]
    lane = iota((8, 128), 1)
    column = jnp.sum(
        jnp.where(lane == 2 * heads, sums[24:32, 0:128], 0.0), axis=1, keepdims=True
    )
    o_hb[...] = jnp.sum(jnp.where(lane == iota((8, 128), 0), column, 0.0), axis=0, keepdims=True)[
        :, :patch
    ]
    head_index = lax.axis_index("head")
    for which in range(2):
        row = jnp.zeros((1, 128), F32)
        for g in range(o_table.shape[1] // 8):
            piece = sums[24:32, g * 128 : (g + 1) * 128]
            column = jnp.sum(
                jnp.where(lane == 2 * head_index + which, piece, 0.0), axis=1, keepdims=True
            )
            row = row + jnp.sum(
                jnp.where(lane == 8 * g + iota((8, 128), 0), column, 0.0), axis=0, keepdims=True
            )
        o_table[which : which + 1, :] = row[:, : o_table.shape[1]]
    first = 0
    for out, turn in ((o_q, False), (o_k, False), (o_v, False), (o_o, True), (o_g, False), (o_u, False), (o_d, True)):
        width = out.shape[0] if turn else out.shape[1]
        block = fin[:, first : first + width].astype(F32)
        out[...] = block.T if turn else block
        first += width


def layer_call(groups, heads, args):
    series = args[0]
    rows, steps = series.shape
    patch, width = args[7].shape
    length = steps // patch
    tokens = rows * length
    part = args[9].shape[1]
    ff = args[14].shape[1]
    table_heads, table_rows = args[13].shape
    total = heads * (4 * part + 3 * ff)
    bits = groups.bit_length() - 1
    scratch = dict(
        pm=((length, steps), F32), fold=((16, steps), BF16), ptile=((steps, width), BF16),
        htile=((width, steps), BF16), splitb=((rows, 128), F32), normed=((rows, steps), F32),
        normed_low=((rows, steps), F32), dout_low=((rows, steps), F32), output=((rows, steps), F32),
        d_normed=((rows, steps), F32), p8t=((16, tokens), BF16), d8t=((16, tokens), BF16),
        embedded=((tokens, width), F32), s_attn=((tokens, 1), F32), attn_in=((tokens, width), BF16),
        qkv=((tokens, heads * 3 * part), BF16), tab=((heads, table_rows, 128), F32),
        bias=((heads, length, 128), F32), probs=((heads, tokens, 128), F32),
        ctx=((tokens, heads * part), BF16), hidden_mid=((tokens, width), F32),
        ff_in=((tokens, width), BF16), inner=((tokens, heads * ff), BF16),
        act=((tokens, heads * ff), BF16), slope=((tokens, heads * ff), BF16),
        final_in=((tokens, width), BF16), d_end_low=((tokens, width), BF16),
        dgu=((tokens, heads * 2 * ff), BF16), d_mid=((tokens, width), F32),
        d_ctx=((tokens, heads * part), BF16), dsum=((heads, length, 128), F32),
        g_attn=((8, width), F32), g_ff=((8, width), F32), g_final=((8, width), F32),
        g_bias=((8, width), F32), tgr=((table_rows, 128), F32),
        left_t=((width, tokens), BF16), right_t=((width, tokens), BF16),
        weights=((width, total), BF16), own=((width // 2, total), BF16),
        snd0=((width // 2, total), BF16), rcv0=((width // 2, total), BF16),
        snd1=((width // 4, total), BF16), rcv1=((width // 4, total), BF16),
        snd2=((width // 8, total), BF16), rcv2=((width // 8, total), BF16),
        sndz=((width // 8, total), BF16), rcvz=((heads - 1, width // 8, total // heads), BF16),
        fin=((width, total // heads), BF16), small=((32, width), F32), core_in=((32, width), F32),
        plane=((4, 32, width), BF16), heads_in=((heads, 32, width), BF16),
        sndf=((heads - 1, width // 2, len(EARLY) * part), BF16),
        wo_raw=((part, width), BF16), wd_raw=((ff, width), BF16),
        rcvf=((heads - 1, width // 2, len(EARLY) * part), BF16),
    )
    extra = bits - 3
    if extra > 0:
        scratch.update(
            extra=((extra, width // 8, total), BF16), more=((2 * extra, 32, width), BF16)
        )
    copies = CHUNKS * (4 + 6 + extra) + 4 + extra + 1
    sends = 11 + (CHUNKS + 1) * extra
    outs = [((rows, steps), F32), ((rows, steps), F32), ((32, width), F32), ((width, total // heads), BF16)]
    vmem = pl.BlockSpec(memory_space=pltpu.VMEM)
    any_space = pl.BlockSpec(memory_space=pl.ANY)
    parts = pl.pallas_call(
        functools.partial(layer_kernel, groups, heads, list(scratch)),
        out_shape=[jax.ShapeDtypeStruct(*out) for out in outs],
        in_specs=[any_space if i in (9, 10, 11, 12, 14, 15, 16) else vmem for i in range(len(args))],
        out_specs=[vmem] * 3 + [any_space],
        scratch_shapes=[pltpu.VMEM(*v) for v in scratch.values()]
        + [
            pltpu.SemaphoreType.DMA((sends,)),
            pltpu.SemaphoreType.DMA((copies,)),
            pltpu.SemaphoreType.DMA((9,)),
            pltpu.SemaphoreType.DMA,
        ],
        compiler_params=pltpu.CompilerParams(
            collective_id=0, has_side_effects=True, vmem_limit_bytes=63 * 1024 * 1024
        ),
    )(*args)
    shapes = [
        (rows, steps), (rows, steps), (1, width), (1, width), (1, width), (patch, width), (1, width), (width, part), (width, part),
        (width, part), (part, width), (table_heads, table_rows), (width, ff), (width, ff), (ff, width),
        (patch, width), (1, patch),
    ]
    return list(
        pl.pallas_call(
            functools.partial(finish_kernel, heads),
            out_shape=[jax.ShapeDtypeStruct(shape, F32) for shape in shapes],
            in_specs=[vmem] * len(parts),
            out_specs=[vmem] * len(shapes),
        )(*parts)
    )


def solution(mesh):
    groups, heads = mesh.shape["dp"], mesh.shape["head"]

    def local(*args):
        args = list(args)
        for i in (2, 18):
            args[i] = args[i].reshape(1, -1)
        for i in (4, 5, 6, 8):
            args[i] = args[i].reshape(-1, 128)
        for i in (13, 17):
            args[i] = args[i].T
        outs = layer_call(groups, heads, args)
        for i in (2, 3, 4, 6, 16):
            outs[i] = outs[i].reshape(-1)
        outs[11], outs[15] = outs[11].T, outs[15].T
        return tuple(outs)

    both = P(("dp", "head"), None)
    by_column, by_row = P(None, "head"), P("head", None)
    return jax.shard_map(
        local,
        mesh=mesh,
        in_specs=(both, both, P("dp"), both) + (P(),) * 5 + (by_column,) * 3
        + (by_row, by_column, by_column, by_column, by_row, P(), P()),
        out_specs=(both, both) + (P(),) * 5 + (by_column,) * 3
        + (by_row, by_column, by_column, by_column, by_row, P(), P()),
        check_vma=False,
    )
```
